32 devices in a mesh: ctx: 8 (over z, y), head: 4 (over x, core).
Axes of the slice: x: 2, y: 2, z: 4, core: 2. Of those that a mesh axis runs over, the one named last changes fastest.
Arguments:
- queries: bfloat16 [3072, 2048], P('ctx', 'head'), may hold values from -10 to 10, as said below
- key_rows: bfloat16 [3072, 2048], P('ctx', 'head'), may hold values from -10 to 10, as said below
- value_rows: bfloat16 [3072, 2048], P('ctx', 'head'), may hold values from -6 to 6
- out_weight: bfloat16 [2048, 2048], P('head'), may hold values from -0.125 to 0.125
- cotangent: bfloat16 [3072, 2048], P('ctx', 'head'), may hold values from -6 to 6
- offsets: int32 [136], replicated, may hold values from 0 to 25920, as said below
Outputs:
- mixed: bfloat16 [3072, 2048], P('ctx', 'head')
- grad_queries: bfloat16 [3072, 2048], P('ctx', 'head')
- grad_keys: bfloat16 [3072, 2048], P('ctx', 'head')
- grad_values: bfloat16 [3072, 2048], P('ctx', 'head')
The draws below stay inside these ranges and needn't reach their ends.
Inputs may be any that keep to these rules, and one draw needn't show every extreme that they name: offsets start at 0 and increase; consecutive entries differ by 1 to 192 except before the last entry, which is (135) * 192 and lies beyond the history, as does the entry before it. `queries`: real values. `key_rows`: real values.
All inputs are finite; a program needn't handle non-finite values.
Results may differ from the reference program's by a relative error of at most 0.018.
Values may be sent and summed in bfloat16 or wider, within the bound.
No kernel may reach another device: no remote copies, remote signals or barrier semaphores. Data moves between devices by JAX's collectives and lax.ppermute only.
A program may use at most 64 MiB of HBM per device.

```python
import math
import jax
import jax.numpy as jnp
from jax import lax

D = 2048
HEADS = 16
HD = 128
T_DEV = 384
REACH = 2
PREV = 3
EP_MAX = 192
TOKENS = 3072
EPISODES = 136


def attention_pair(key):
    columns = HEADS * HD
    key_q = jax.random.fold_in(key, 201)
    key_k = jax.random.fold_in(key, 202)
    query_draw = jnp.clip(jax.random.normal(key_q, (TOKENS, columns), jnp.float32), -4.0, 4.0)
    key_draw = jnp.clip(jax.random.normal(key_k, (TOKENS, columns), jnp.float32), -4.0, 4.0)
    return (query_draw, key_draw)


def draw_queries(key, part):
    return attention_pair(key)[0].astype(jnp.bfloat16)


def draw_key_rows(key, part):
    return attention_pair(key)[1].astype(jnp.bfloat16)


def draw_offsets(key, part):
    key_groups = jax.random.fold_in(key, 101)
    key_trim = jax.random.fold_in(key, 102)
    key_place = jax.random.fold_in(key, 103)
    group_count = EPISODES // 16 + 1
    regime = jax.random.randint(key_groups, (group_count,), 0, 3)
    regime = jnp.repeat(regime, 16)[:EPISODES]
    longest = jnp.right_shift(jnp.full((EPISODES,), EP_MAX, jnp.int32), regime.astype(jnp.int32))
    trimmed = jax.random.randint(key_trim, (EPISODES,), 0, longest // 2 + 1)
    lengths = (longest - trimmed).astype(jnp.int32)
    first_run = jax.random.randint(key_place, (), 3, max(4, TOKENS // (4 * T_DEV)))
    order = jnp.arange(EPISODES)
    lengths = jnp.where((order >= first_run) & (order <= first_run + PREV), EP_MAX, lengths)
    before_fill = jnp.sum(jnp.where(order < first_run - 3, lengths, 0))
    target = before_fill + 3 + jnp.remainder(T_DEV - 4 - before_fill, T_DEV)
    filler = target - before_fill
    lengths = jnp.where(order == first_run - 3, filler // 3, lengths)
    lengths = jnp.where(order == first_run - 2, (filler + 1) // 3, lengths)
    lengths = jnp.where(order == first_run - 1, (filler + 2) // 3, lengths)
    starts = jnp.cumsum(lengths)[:-1]
    listed = jnp.concatenate([jnp.zeros((1,), jnp.int32), starts.astype(jnp.int32)]).astype(jnp.int32)
    last_entry = jnp.full((EPISODES,), (EPISODES - 1) * EP_MAX, jnp.int32)
    return jnp.where(order == EPISODES - 1, last_entry, listed).astype(jnp.int32)


def level_of(key, dims, shards, least, top_value):
    def one(position, blocks):
        steps = jax.random.uniform(jax.random.fold_in(jax.random.fold_in(key, 6), position), (blocks,), jnp.float32, least / len(shards), top_value / len(shards))
        return jnp.repeat(jnp.exp(steps), dims[position] // blocks).reshape((-1,) + (1,) * (len(dims) - position - 1))

    level = one(*shards[0])
    for cut in shards[1:]:
        level = level * one(*cut)
    return level


def centred(rng, extent, scale, reach, cuts=(), kind=jnp.bfloat16):
    array = jax.random.normal(rng, extent, jnp.float32) * scale
    if len(cuts) > 0:
        array = level_of(rng, extent, cuts, -0.22, 0.18) * array
    return jnp.clip(array, min=-reach, max=reach).astype(kind)


def setup_inputs(seed: int = 0) -> dict:
    key_list = jax.random.split(jax.random.key(seed), 7)
    queries = draw_queries(jax.random.fold_in(key_list[6], 71), 0)
    key_rows = draw_key_rows(jax.random.fold_in(key_list[6], 71), 0)
    value_rows = centred(key_list[2], (TOKENS, HEADS * HD), 1.0, 6.0, ((0, 8), (1, 4)))
    out_weight = centred(key_list[3], (HEADS * HD, D), (HEADS * HD) ** -0.5, 0.125, ((0, 4),))
    cotangent = centred(key_list[4], (TOKENS, D), 1.0, 6.0, ((0, 8), (1, 4)))
    offsets = draw_offsets(jax.random.fold_in(key_list[6], 71), 0)
    return dict(queries=queries, key_rows=key_rows, value_rows=value_rows, out_weight=out_weight, cotangent=cotangent, offsets=offsets)


NEG_FILL = -1e+30

def episode_ids(positions, offsets):
    hit_count = lax.optimization_barrier(jnp.sum((offsets[None, :] <= positions[:, None]).astype(jnp.int32), axis=1))
    return (hit_count - 1).astype(jnp.int32)

def rounded(values):
    return lax.optimization_barrier(values.astype(jnp.bfloat16)).astype(jnp.float32)

def reference(queries, key_rows, value_rows, out_weight, cotangent, offsets):
    head_cols = HEADS * HD
    key_span = (REACH + 1) * T_DEV
    pad_rows = REACH * T_DEV
    score_scale = 1.0 / math.sqrt(HD)
    keys_padded = jnp.concatenate([jnp.zeros((pad_rows, head_cols), key_rows.dtype), key_rows], axis=0)
    values_padded = jnp.concatenate([jnp.zeros((pad_rows, head_cols), value_rows.dtype), value_rows], axis=0)

    def scan_step(grad_carry, block_index):
        grad_keys, grad_values = grad_carry
        start_row = (block_index * T_DEV).astype(jnp.int32)
        query_block = lax.dynamic_slice_in_dim(queries, start_row, T_DEV, 0)
        grad_block = lax.dynamic_slice_in_dim(cotangent, start_row, T_DEV, 0)
        key_block = lax.dynamic_slice_in_dim(keys_padded, start_row, key_span, 0)
        value_block = lax.dynamic_slice_in_dim(values_padded, start_row, key_span, 0)
        query_pos = start_row + jnp.arange(T_DEV, dtype=jnp.int32)
        key_pos = start_row - pad_rows + jnp.arange(key_span, dtype=jnp.int32)
        query_ep = episode_ids(query_pos, offsets)
        key_ep = episode_ids(key_pos, offsets)
        allowed = (key_pos[None, :] <= query_pos[:, None]) & (key_pos[None, :] >= 0) & (query_ep[:, None] - key_ep[None, :] <= PREV)
        query_heads = query_block.astype(jnp.float32).reshape(T_DEV, HEADS, HD)
        key_heads = key_block.astype(jnp.float32).reshape(key_span, HEADS, HD)
        value_heads = value_block.astype(jnp.float32).reshape(key_span, HEADS, HD)
        scores = jnp.einsum('qhd,khd->hqk', query_heads, key_heads) * score_scale
        scores = jnp.where(allowed[None], scores, NEG_FILL)
        row_max = lax.optimization_barrier(jnp.max(scores, axis=2, keepdims=True))
        row_total = lax.optimization_barrier(jnp.sum(jnp.exp(scores - row_max), axis=2, keepdims=True))
        log_total = row_max + jnp.log(row_total)
        attn_probs = jnp.where(allowed[None], jnp.exp(scores - log_total), 0.0)
        probs_b = rounded(attn_probs)
        attended = jnp.einsum('hqk,khd->qhd', probs_b, value_heads).reshape(T_DEV, head_cols)
        attended_b = attended.astype(jnp.bfloat16)
        mixed_block = jnp.dot(attended_b, out_weight, preferred_element_type=jnp.float32).astype(jnp.bfloat16)
        grad_out = jnp.dot(grad_block, out_weight.T, preferred_element_type=jnp.float32).astype(jnp.bfloat16)
        grad_heads = grad_out.astype(jnp.float32).reshape(T_DEV, HEADS, HD)
        attended_heads = attended_b.astype(jnp.float32).reshape(T_DEV, HEADS, HD)
        row_delta = jnp.einsum('qhd,qhd->hq', grad_heads, attended_heads)[:, :, None]
        grad_probs = jnp.einsum('qhd,khd->hqk', grad_heads, value_heads)
        grad_scores = rounded(score_scale * attn_probs * (grad_probs - row_delta))
        grad_query = jnp.einsum('hqk,khd->qhd', grad_scores, key_heads).reshape(T_DEV, head_cols).astype(jnp.bfloat16)
        part_keys = jnp.einsum('hqk,qhd->khd', grad_scores, query_heads).reshape(key_span, head_cols)
        part_values = jnp.einsum('hqk,qhd->khd', probs_b, grad_heads).reshape(key_span, head_cols)
        old_keys = lax.dynamic_slice_in_dim(grad_keys, start_row, key_span, 0)
        grad_keys = lax.dynamic_update_slice_in_dim(grad_keys, old_keys + part_keys, start_row, 0)
        old_values = lax.dynamic_slice_in_dim(grad_values, start_row, key_span, 0)
        grad_values = lax.dynamic_update_slice_in_dim(grad_values, old_values + part_values, start_row, 0)
        return ((grad_keys, grad_values), (mixed_block, grad_query))
    blocks = TOKENS // T_DEV
    start_carry = (jnp.zeros((TOKENS + pad_rows, head_cols), jnp.float32), jnp.zeros((TOKENS + pad_rows, head_cols), jnp.float32))
    final_carry, outputs = lax.scan(scan_step, start_carry, jnp.arange(blocks, dtype=jnp.int32))
    mixed = outputs[0].reshape(TOKENS, D)
    grad_queries = outputs[1].reshape(TOKENS, head_cols)
    grad_keys = final_carry[0][pad_rows:].astype(jnp.bfloat16)
    grad_values = final_carry[1][pad_rows:].astype(jnp.bfloat16)
    return (mixed, grad_queries, grad_keys, grad_values)
```

```python
import functools
import math

import jax
import jax.numpy as jnp
from jax import lax
from jax.experimental import pallas as pl
from jax.experimental.pallas import tpu as pltpu
from jax.sharding import PartitionSpec as P

HD = 128
REACH = 2
PREV = 3
ROWS = 128
NEG_FILL = -1e30
SCALE = 1.0 / math.sqrt(HD)
LOG2E = 1.4426950408889634
F32 = jnp.float32
BF16 = jnp.bfloat16


NT = (((1,), (1,)), ((), ()))
NN = (((1,), (0,)), ((), ()))


def passed_along(shard, axis, by):
    length = lax.axis_size(axis)
    pairs = [(i, i + by) for i in range(length) if 0 <= i + by < length]
    return lax.ppermute(shard, axis, pairs)


def swapped(shard, axis, bit):
    length = lax.axis_size(axis)
    return lax.ppermute(shard, axis, [(i, i ^ bit) for i in range(length)])


def window_starts(positions, offsets):
    later, first = offsets[PREV:], offsets[:-PREV]
    reached = jnp.where(later[None, :] <= positions[:, None], first[None, :], 0)
    return jnp.max(reached, axis=1)


def mm(a, b, dims):
    return lax.dot_general(a, b, dims, preferred_element_type=F32)


def grad_out_kernel(me_ref, c0, c1, c2, c3, w_ref, out_ref):
    cols = c0.shape[1]
    total = None
    for s, c in enumerate((c0, c1, c2, c3)):
        start = pl.multiple_of((me_ref[0] ^ s) * cols, cols)
        part = mm(c[...], w_ref[:, pl.ds(start, cols)], NT)
        total = part if total is None else total + part
    out_ref[...] = total.astype(BF16)


def grad_out_call(me, shards, weight):
    rows, cols = shards[0].shape
    whole = pl.BlockSpec((rows, cols), lambda h, me: (0, 0))
    return pl.pallas_call(
        grad_out_kernel,
        name="grad_out",
        out_shape=jax.ShapeDtypeStruct((rows, cols), BF16),
        grid_spec=pltpu.PrefetchScalarGridSpec(
            num_scalar_prefetch=1,
            grid=(cols // HD,),
            in_specs=[whole] * 4 + [pl.BlockSpec((HD, weight.shape[1]), lambda h, me: (h, 0))],
            out_specs=pl.BlockSpec((rows, HD), lambda h, me: (0, h)),
        ),
        cost_estimate=pl.CostEstimate(
            flops=2 * rows * cols * weight.shape[1], bytes_accessed=6 << 20, transcendentals=0
        ),
    )(me, *shards, weight)


def key_pieces(block, rows):
    first, last = block * ROWS, (block + 1) * ROWS
    return ((2, first, rows, -2 * rows), (1, 0, rows, -rows), (0, 0, last, 0))


def attend_kernel(lo_ref, q, k0, k1, k2, v0, v1, v2, g, att_ref, prob_ref, stat_ref):
    rows = q.shape[0]
    keys, values = (k0, k1, k2), (v0, v1, v2)
    for b in range(rows // ROWS):
        mine = slice(b * ROWS, (b + 1) * ROWS)
        qb = q[mine, :]
        lo = lo_ref[mine, :]
        scores = []
        for tile, first, last, off in key_pieces(b, rows):
            raw = mm(qb, keys[tile][first:last, :], NT)
            pos = off + first + lax.broadcasted_iota(jnp.int32, raw.shape, 1)
            ok = pos >= lo
            if tile == 0:
                ok &= pos <= b * ROWS + lax.broadcasted_iota(jnp.int32, raw.shape, 0)
            scores.append(jnp.where(ok, raw, NEG_FILL))
        top = functools.reduce(
            jnp.maximum, [jnp.max(s, axis=1, keepdims=True) for s in scores]
        )
        shift = top * (SCALE * LOG2E)
        exps = [jnp.exp2(s * (SCALE * LOG2E) - shift) for s in scores]
        total = functools.reduce(jnp.add, [jnp.sum(e, axis=1, keepdims=True) for e in exps])
        inverse = 1.0 / total
        mixed = None
        column = 0
        for e, (tile, first, last, off) in zip(exps, key_pieces(b, rows)):
            prob = (e * inverse).astype(BF16)
            prob_ref[0, mine, column : column + last - first] = prob
            column += last - first
            part = mm(prob, values[tile][first:last, :], NN)
            mixed = part if mixed is None else mixed + part
        attended = mixed.astype(BF16)
        att_ref[mine, :] = attended
        delta = jnp.sum(attended.astype(F32) * g[mine, :].astype(F32), axis=1, keepdims=True)
        log_total = shift + jnp.log2(total)
        lane = lax.broadcasted_iota(jnp.int32, (ROWS, ROWS), 1)
        stats = jnp.where(lane == 0, log_total, delta).T
        stat_ref[0, :, mine] = stats[0:2, :]


def attend_call(lo, q, keys, values, g):
    rows, cols = q.shape
    heads = cols // HD
    tile = pl.BlockSpec((rows, HD), lambda h: (0, h))
    span = REACH * rows + ROWS
    return pl.pallas_call(
        attend_kernel,
        name="attend",
        out_shape=(
            jax.ShapeDtypeStruct((rows, cols), BF16),
            jax.ShapeDtypeStruct((heads, rows, span), BF16),
            jax.ShapeDtypeStruct((heads, 2, rows), F32),
        ),
        grid=(heads,),
        in_specs=[pl.BlockSpec((rows, 1), lambda h: (0, 0))] + [tile] * 8,
        out_specs=(
            tile,
            pl.BlockSpec((1, rows, span), lambda h: (h, 0, 0)),
            pl.BlockSpec((1, 2, rows), lambda h: (h, 0, 0)),
        ),
        cost_estimate=pl.CostEstimate(
            flops=4 * heads * rows * span * HD, bytes_accessed=8 << 20,
            transcendentals=heads * rows * span,
        ),
    )(lo, q, *keys, *values, g)


def project_kernel(me_ref, a_ref, w_ref, out_ref):
    out_ref[...] = mm(a_ref[...], w_ref[...], NN).astype(out_ref.dtype)


def project_call(me, attended, weight, swaps, dtype):
    rows, cols = attended.shape
    base, step = swaps

    return pl.pallas_call(
        project_kernel,
        name="project",
        out_shape=jax.ShapeDtypeStruct((rows, 2 * cols), dtype),
        grid_spec=pltpu.PrefetchScalarGridSpec(
            num_scalar_prefetch=1,
            grid=(2,),
            in_specs=[
                pl.BlockSpec((rows, cols), lambda s, me: (0, 0)),
                pl.BlockSpec((cols, cols), lambda s, me: (0, me[0] ^ (base + step * s))),
            ],
            out_specs=pl.BlockSpec((rows, cols), lambda s, me: (0, s)),
        ),
        cost_estimate=pl.CostEstimate(
            flops=4 * rows * cols * cols, bytes_accessed=3 << 20, transcendentals=0
        ),
    )(me, attended, weight)


def query_grad_kernel(prob_ref, att, k0, k1, k2, v0, v1, v2, g, out_ref):
    rows = g.shape[0]
    keys, values = (k0, k1, k2), (v0, v1, v2)
    for b in range(rows // ROWS):
        mine = slice(b * ROWS, (b + 1) * ROWS)
        gb = g[mine, :]
        delta = jnp.sum(att[mine, :].astype(F32) * gb.astype(F32), axis=1, keepdims=True)
        total = None
        column = 0
        for tile, first, last, off in key_pieces(b, rows):
            prob = prob_ref[0, mine, column : column + last - first].astype(F32)
            column += last - first
            grad_prob = mm(gb, values[tile][first:last, :], NT)
            grad_score = (prob * (grad_prob - delta)).astype(BF16)
            part = mm(grad_score, keys[tile][first:last, :], NN)
            total = part if total is None else total + part
        out_ref[mine, :] = (total * SCALE).astype(BF16)


def query_grad_call(prob, att, keys, values, g):
    rows, cols = g.shape
    heads = cols // HD
    tile = pl.BlockSpec((rows, HD), lambda h: (0, h))
    span = REACH * rows + ROWS
    return pl.pallas_call(
        query_grad_kernel,
        name="query_grad",
        out_shape=jax.ShapeDtypeStruct((rows, cols), BF16),
        grid=(heads,),
        in_specs=[pl.BlockSpec((1, rows, span), lambda h: (h, 0, 0))] + [tile] * 8,
        out_specs=tile,
        cost_estimate=pl.CostEstimate(
            flops=4 * heads * rows * span * HD, bytes_accessed=8 << 20, transcendentals=0
        ),
    )(prob, att, *keys, *values, g)


def key_grad_kernel(lo_ref, k, v, q0, q1, q2, g0, g1, g2, s0, s1, s2, dk_ref, dv_ref):
    rows = k.shape[0]
    queries, grads, stats = (q0, q1, q2), (g0, g1, g2), (s0, s1, s2)
    for b in range(rows // ROWS):
        mine = slice(b * ROWS, (b + 1) * ROWS)
        kb, vb = k[mine, :], v[mine, :]
        dk = dv = None
        pieces = ((0, b * ROWS, rows), (1, 0, rows), (2, 0, (b + 1) * ROWS))
        for tile, first, last in pieces:
            qt, gt = queries[tile][first:last, :], grads[tile][first:last, :]
            raw = mm(kb, qt, NT)
            pos = b * ROWS + lax.broadcasted_iota(jnp.int32, raw.shape, 0)
            ok = pos >= lo_ref[tile : tile + 1, first:last]
            if tile == 0:
                ok &= pos <= first + lax.broadcasted_iota(jnp.int32, raw.shape, 1)
            log_total = stats[tile][0, 0:1, first:last]
            delta = stats[tile][0, 1:2, first:last]
            prob = jnp.where(ok, jnp.exp2(raw * (SCALE * LOG2E) - log_total), 0.0)
            grad_prob = mm(vb, gt, NT)
            grad_score = (prob * (grad_prob - delta)).astype(BF16)
            part_k = mm(grad_score, qt, NN)
            part_v = mm(prob.astype(BF16), gt, NN)
            dk = part_k if dk is None else dk + part_k
            dv = part_v if dv is None else dv + part_v
        dk_ref[mine, :] = (dk * SCALE).astype(BF16)
        dv_ref[mine, :] = dv.astype(BF16)


def key_grad_call(lo, k, v, queries, grads, stats):
    rows, cols = k.shape
    heads = cols // HD
    tile = pl.BlockSpec((rows, HD), lambda h: (0, h))
    stat = pl.BlockSpec((1, 2, rows), lambda h: (h, 0, 0))
    span = REACH * rows + ROWS
    return pl.pallas_call(
        key_grad_kernel,
        name="key_grad",
        out_shape=(jax.ShapeDtypeStruct((rows, cols), BF16),) * 2,
        grid=(heads,),
        in_specs=[pl.BlockSpec((REACH + 1, rows), lambda h: (0, 0))] + [tile] * 8 + [stat] * 3,
        out_specs=(tile, tile),
        cost_estimate=pl.CostEstimate(
            flops=8 * heads * rows * span * HD, bytes_accessed=5 << 20,
            transcendentals=heads * rows * span,
        ),
    )(lo, k, v, *queries, *grads, *stats)


def per_device(queries, key_rows, value_rows, out_weight, cotangent, offsets):
    rows, cols = queries.shape
    base = lax.axis_index("ctx") * rows
    me = lax.axis_index("head").astype(jnp.int32).reshape(1)

    cot_far = swapped(cotangent, "head", 2)
    cot_near = swapped(cotangent, "head", 1)
    keys = [key_rows] + [passed_along(key_rows, "ctx", n) for n in (1, 2)]
    values = [value_rows] + [passed_along(value_rows, "ctx", n) for n in (1, 2)]
    later_q = [queries] + [passed_along(queries, "ctx", -n) for n in (1, 2)]
    cot_both = swapped(cot_far, "head", 1)

    positions = base + jnp.arange((REACH + 1) * rows, dtype=jnp.int32)
    lo = (window_starts(positions, offsets) - base).reshape(REACH + 1, rows)

    g = grad_out_call(me, (cotangent, cot_near, cot_far, cot_both), out_weight)
    later_g = [g] + [passed_along(g, "ctx", -n) for n in (1, 2)]

    attended, prob, stat = attend_call(lo[0].reshape(rows, 1), queries, keys, values, g)
    later_stat = [stat] + [passed_along(stat, "ctx", -n) for n in (1, 2)]

    sent = project_call(me, attended, out_weight, (1, 2), BF16)
    came = swapped(sent, "head", 1)
    kept = project_call(me, attended, out_weight, (0, 2), F32)
    both = kept + came.astype(F32)
    mine, other = both[:, :cols], both[:, cols:].astype(BF16)
    mixed = (mine + swapped(other, "head", 2).astype(F32)).astype(BF16)

    grad_queries = query_grad_call(prob, attended, keys, values, g)
    grad_keys, grad_values = key_grad_call(lo, key_rows, value_rows, later_q, later_g, later_stat)
    return (mixed, grad_queries, grad_keys, grad_values)


def solution(mesh):
    in_specs = (
        P("ctx", "head"),
        P("ctx", "head"),
        P("ctx", "head"),
        P("head", None),
        P("ctx", "head"),
        P(),
    )
    out_specs = (P("ctx", "head"), P("ctx", "head"), P("ctx", "head"), P("ctx", "head"))
    return jax.shard_map(
        per_device, mesh=mesh, in_specs=in_specs, out_specs=out_specs, check_vma=False
    )
```

```python
import functools
import math

import jax
import jax.numpy as jnp
from jax import lax
from jax.experimental import pallas as pl
from jax.experimental.pallas import tpu as pltpu
from jax.sharding import PartitionSpec as P


HD = 128
REACH = 2
PREV = 3
ROWS = 128
NEG_FILL = -1e30
SCALE = 1.0 / math.sqrt(HD)
LOG2E = 1.4426950408889634
VMEM_BYTES = 67043328
F32 = jnp.float32
BF16 = jnp.bfloat16


NT = (((1,), (1,)), ((), ()))
NN = (((1,), (0,)), ((), ()))


def passed_along(shard, axis, by):
    length = lax.axis_size(axis)
    pairs = [(i, i + by) for i in range(length) if 0 <= i + by < length]
    return lax.ppermute(shard, axis, pairs)


def swapped(shard, axis, bit):
    length = lax.axis_size(axis)
    return lax.ppermute(shard, axis, [(i, i ^ bit) for i in range(length)])


def window_starts(positions, offsets):
    later, first = offsets[PREV:], offsets[:-PREV]
    reached = jnp.where(later[None, :] <= positions[:, None], first[None, :], 0)
    return jnp.max(reached, axis=1)


def mm(a, b, dims):
    return lax.dot_general(a, b, dims, preferred_element_type=F32)


def grad_out_kernel(me_ref, c0, c1, c2, c3, w_ref, out_ref):
    cols = c0.shape[1]
    total = None
    for s, c in enumerate((c0, c1, c2, c3)):
        start = pl.multiple_of((me_ref[0] ^ s) * cols, cols)
        part = mm(c[...], w_ref[:, pl.ds(start, cols)], NT)
        total = part if total is None else total + part
    out_ref[...] = total.astype(BF16)


def grad_out_call(me, shards, weight):
    rows, cols = shards[0].shape
    whole = pl.BlockSpec((rows, cols), lambda h, me: (0, 0))
    return pl.pallas_call(
        grad_out_kernel,
        name="grad_out",
        out_shape=jax.ShapeDtypeStruct((rows, cols), BF16),
        grid_spec=pltpu.PrefetchScalarGridSpec(
            num_scalar_prefetch=1,
            grid=(cols // HD,),
            in_specs=[whole] * 4 + [pl.BlockSpec((HD, weight.shape[1]), lambda h, me: (h, 0))],
            out_specs=pl.BlockSpec((rows, HD), lambda h, me: (0, h)),
        ),
        compiler_params=pltpu.CompilerParams(vmem_limit_bytes=VMEM_BYTES),
        cost_estimate=pl.CostEstimate(
            flops=2 * rows * cols * weight.shape[1], bytes_accessed=6 << 20, transcendentals=0
        ),
    )(me, *shards, weight)


def key_pieces(block, rows):
    first, last = block * ROWS, (block + 1) * ROWS
    return ((2, first, rows, -2 * rows), (1, 0, rows, -rows), (0, 0, last, 0))


def pick(odd, even_ref, odd_ref, into):
    @pl.when(odd == 0)
    def _():
        into[...] = even_ref[...]

    @pl.when(odd == 1)
    def _():
        into[...] = odd_ref[...]


def attend_kernel(odd_ref, lo_ref, q, k0, k2, v0, v2, r1, r2, r3, g, att_ref, prob_ref, stat_ref, k1, v1):
    rows = q.shape[0]
    pick(odd_ref[0], r2, r1, k1)
    pick(odd_ref[0], r3, r2, v1)
    keys, values = (k0, k1, k2), (v0, v1, v2)
    for b in range(rows // ROWS):
        mine = slice(b * ROWS, (b + 1) * ROWS)
        qb = q[mine, :]
        lo = lo_ref[mine, :]
        scores = []
        for tile, first, last, off in key_pieces(b, rows):
            raw = mm(qb, keys[tile][first:last, :], NT)
            pos = off + first + lax.broadcasted_iota(jnp.int32, raw.shape, 1)
            ok = pos >= lo
            if tile == 0:
                ok &= pos <= b * ROWS + lax.broadcasted_iota(jnp.int32, raw.shape, 0)
            scores.append(jnp.where(ok, raw, NEG_FILL))
        top = functools.reduce(
            jnp.maximum, [jnp.max(s, axis=1, keepdims=True) for s in scores]
        )
        shift = top * (SCALE * LOG2E)
        exps = [jnp.exp2(s * (SCALE * LOG2E) - shift) for s in scores]
        total = functools.reduce(jnp.add, [jnp.sum(e, axis=1, keepdims=True) for e in exps])
        inverse = 1.0 / total
        mixed = None
        column = 0
        for e, (tile, first, last, off) in zip(exps, key_pieces(b, rows)):
            prob = (e * inverse).astype(BF16)
            prob_ref[0, mine, column : column + last - first] = prob
            column += last - first
            part = mm(prob, values[tile][first:last, :], NN)
            mixed = part if mixed is None else mixed + part
        attended = mixed.astype(BF16)
        att_ref[mine, :] = attended
        delta = jnp.sum(attended.astype(F32) * g[mine, :].astype(F32), axis=1, keepdims=True)
        log_total = shift + jnp.log2(total)
        lane = lax.broadcasted_iota(jnp.int32, (ROWS, ROWS), 1)
        stats = jnp.where(lane == 0, log_total, delta).T
        stat_ref[0, :, mine] = stats[0:2, :]


def tile_specs(rows):
    tile = pl.BlockSpec((rows, HD), lambda h, odd: (0, h))
    on_odd = pl.BlockSpec((rows, HD), lambda h, odd: (0, h * odd[0]))
    on_even = pl.BlockSpec((rows, HD), lambda h, odd: (0, h * (1 - odd[0])))
    return tile, on_odd, on_even


def attend_call(odd, lo, q, k0, k2, v0, v2, r1, r2, r3, g):
    rows, cols = q.shape
    heads = cols // HD
    tile, on_odd, on_even = tile_specs(rows)
    span = REACH * rows + ROWS
    return pl.pallas_call(
        attend_kernel,
        name="attend",
        out_shape=(
            jax.ShapeDtypeStruct((rows, cols), BF16),
            jax.ShapeDtypeStruct((heads, rows, span), BF16),
            jax.ShapeDtypeStruct((heads, 2, rows), F32),
        ),
        grid_spec=pltpu.PrefetchScalarGridSpec(
            num_scalar_prefetch=1,
            grid=(heads,),
            in_specs=[pl.BlockSpec((rows, 1), lambda h, odd: (0, 0))]
            + [tile] * 5
            + [on_odd, tile, on_even, tile],
            out_specs=(
                tile,
                pl.BlockSpec((1, rows, span), lambda h, odd: (h, 0, 0)),
                pl.BlockSpec((1, 2, rows), lambda h, odd: (h, 0, 0)),
            ),
            scratch_shapes=[pltpu.VMEM((rows, HD), BF16)] * 2,
        ),
        compiler_params=pltpu.CompilerParams(vmem_limit_bytes=VMEM_BYTES),
        cost_estimate=pl.CostEstimate(
            flops=4 * heads * rows * span * HD, bytes_accessed=8 << 20,
            transcendentals=heads * rows * span,
        ),
    )(odd, lo, q, k0, k2, v0, v2, r1, r2, r3, g)


def project_kernel(me_ref, a_ref, w_ref, out_ref):
    out_ref[...] = mm(a_ref[...], w_ref[...], NN).astype(out_ref.dtype)


def project_call(me, attended, weight, swaps, dtype):
    rows, cols = attended.shape
    base, step = swaps

    return pl.pallas_call(
        project_kernel,
        name="project",
        out_shape=jax.ShapeDtypeStruct((rows, 2 * cols), dtype),
        grid_spec=pltpu.PrefetchScalarGridSpec(
            num_scalar_prefetch=1,
            grid=(2,),
            in_specs=[
                pl.BlockSpec((rows, cols), lambda s, me: (0, 0)),
                pl.BlockSpec((cols, cols), lambda s, me: (0, me[0] ^ (base + step * s))),
            ],
            out_specs=pl.BlockSpec((rows, cols), lambda s, me: (0, s)),
        ),
        compiler_params=pltpu.CompilerParams(vmem_limit_bytes=VMEM_BYTES),
        cost_estimate=pl.CostEstimate(
            flops=4 * rows * cols * cols, bytes_accessed=3 << 20, transcendentals=0
        ),
    )(me, attended, weight)


def query_grad_kernel(odd_ref, prob_ref, att, k0, k2, v0, v2, r1, r2, r3, g, out_ref, k1, v1):
    rows = g.shape[0]
    pick(odd_ref[0], r2, r1, k1)
    pick(odd_ref[0], r3, r2, v1)
    keys, values = (k0, k1, k2), (v0, v1, v2)
    for b in range(rows // ROWS):
        mine = slice(b * ROWS, (b + 1) * ROWS)
        gb = g[mine, :]
        delta = jnp.sum(att[mine, :].astype(F32) * gb.astype(F32), axis=1, keepdims=True)
        total = None
        column = 0
        for tile, first, last, off in key_pieces(b, rows):
            prob = prob_ref[0, mine, column : column + last - first].astype(F32)
            column += last - first
            grad_prob = mm(gb, values[tile][first:last, :], NT)
            grad_score = (prob * (grad_prob - delta)).astype(BF16)
            part = mm(grad_score, keys[tile][first:last, :], NN)
            total = part if total is None else total + part
        out_ref[mine, :] = (total * SCALE).astype(BF16)


def query_grad_call(odd, prob, att, k0, k2, v0, v2, r1, r2, r3, g):
    rows, cols = g.shape
    heads = cols // HD
    tile, on_odd, on_even = tile_specs(rows)
    span = REACH * rows + ROWS
    return pl.pallas_call(
        query_grad_kernel,
        name="query_grad",
        out_shape=jax.ShapeDtypeStruct((rows, cols), BF16),
        grid_spec=pltpu.PrefetchScalarGridSpec(
            num_scalar_prefetch=1,
            grid=(heads,),
            in_specs=[pl.BlockSpec((1, rows, span), lambda h, odd: (h, 0, 0))]
            + [tile] * 5
            + [on_odd, tile, on_even, tile],
            out_specs=tile,
            scratch_shapes=[pltpu.VMEM((rows, HD), BF16)] * 2,
        ),
        compiler_params=pltpu.CompilerParams(vmem_limit_bytes=VMEM_BYTES),
        cost_estimate=pl.CostEstimate(
            flops=4 * heads * rows * span * HD, bytes_accessed=8 << 20, transcendentals=0
        ),
    )(odd, prob, att, k0, k2, v0, v2, r1, r2, r3, g)


def key_grad_kernel(
    odd_ref, lo_ref, k, v, q0, q2, r1, r3, g0, g1, g2, s0, s1, s2, dk_ref, dv_ref, q1
):
    rows = k.shape[0]
    pick(odd_ref[0], r1, r3, q1)
    queries, grads, stats = (q0, q1, q2), (g0, g1, g2), (s0, s1, s2)
    for b in range(rows // ROWS):
        mine = slice(b * ROWS, (b + 1) * ROWS)
        kb, vb = k[mine, :], v[mine, :]
        dk = dv = None
        pieces = ((0, b * ROWS, rows), (1, 0, rows), (2, 0, (b + 1) * ROWS))
        for tile, first, last in pieces:
            qt, gt = queries[tile][first:last, :], grads[tile][first:last, :]
            raw = mm(kb, qt, NT)
            pos = b * ROWS + lax.broadcasted_iota(jnp.int32, raw.shape, 0)
            ok = pos >= lo_ref[tile : tile + 1, first:last]
            if tile == 0:
                ok &= pos <= first + lax.broadcasted_iota(jnp.int32, raw.shape, 1)
            log_total = stats[tile][0, 0:1, first:last]
            delta = stats[tile][0, 1:2, first:last]
            prob = jnp.where(ok, jnp.exp2(raw * (SCALE * LOG2E) - log_total), 0.0)
            grad_prob = mm(vb, gt, NT)
            grad_score = (prob * (grad_prob - delta)).astype(BF16)
            part_k = mm(grad_score, qt, NN)
            part_v = mm(prob.astype(BF16), gt, NN)
            dk = part_k if dk is None else dk + part_k
            dv = part_v if dv is None else dv + part_v
        dk_ref[mine, :] = (dk * SCALE).astype(BF16)
        dv_ref[mine, :] = dv.astype(BF16)


def key_grad_call(odd, lo, k, v, q0, q2, r1, r3, grads, stats):
    rows, cols = k.shape
    heads = cols // HD
    tile, on_odd, on_even = tile_specs(rows)
    stat = pl.BlockSpec((1, 2, rows), lambda h, odd: (h, 0, 0))
    span = REACH * rows + ROWS
    return pl.pallas_call(
        key_grad_kernel,
        name="key_grad",
        out_shape=(jax.ShapeDtypeStruct((rows, cols), BF16),) * 2,
        grid_spec=pltpu.PrefetchScalarGridSpec(
            num_scalar_prefetch=1,
            grid=(heads,),
            in_specs=[pl.BlockSpec((REACH + 1, rows), lambda h, odd: (0, 0))]
            + [tile] * 4
            + [on_even, on_odd]
            + [tile] * 3
            + [stat] * 3,
            out_specs=(tile, tile),
            scratch_shapes=[pltpu.VMEM((rows, HD), BF16)],
        ),
        compiler_params=pltpu.CompilerParams(vmem_limit_bytes=VMEM_BYTES),
        cost_estimate=pl.CostEstimate(
            flops=8 * heads * rows * span * HD, bytes_accessed=5 << 20,
            transcendentals=heads * rows * span,
        ),
    )(odd, lo, k, v, q0, q2, r1, r3, *grads, *stats)


def layer(queries, key_rows, value_rows, out_weight, cotangent, offsets):
    rows, cols = queries.shape
    count = lax.axis_size("ctx")
    index = lax.axis_index("ctx")
    base = index * rows
    odd = (index % 2).astype(jnp.int32).reshape(1)
    me = lax.axis_index("head").astype(jnp.int32).reshape(1)

    def along(shard, by):
        return passed_along(shard, "ctx", by)

    def across(shard, bit):
        return swapped(shard, "head", bit)

    def pair(from_even, from_odd):
        return swapped(jnp.where(index % 2 == 0, from_even, from_odd), "ctx", 1)

    def turned(shard, by):
        return lax.ppermute(shard, "ctx", [(i, (i + by) % count) for i in range(count)])

    cot_far = across(cotangent, 2)
    cot_near = across(cotangent, 1)
    k2 = along(key_rows, 2)
    r1 = pair(key_rows, queries)
    q2 = along(queries, -2)
    v2 = along(value_rows, 2)
    cot_both = across(cot_far, 1)

    positions = base + jnp.arange((REACH + 1) * rows, dtype=jnp.int32)
    lo = window_starts(positions, offsets) - base
    lo = jnp.where(positions < count * rows, lo, (REACH + 1) * rows).reshape(REACH + 1, rows)

    g = grad_out_call(me, (cotangent, cot_near, cot_far, cot_both), out_weight)
    g2 = along(g, -2)
    r2 = pair(value_rows, k2)
    r3 = pair(q2, v2)
    g1 = pair(g2, g)

    attended, prob, stat = attend_call(
        odd, lo[0].reshape(rows, 1), queries, key_rows, k2, value_rows, v2, r1, r2, r3, g
    )
    stat1 = turned(stat, -1)
    stat2 = turned(stat, -2)

    sent = project_call(me, attended, out_weight, (1, 2), BF16)
    came = across(sent, 1)
    kept = project_call(me, attended, out_weight, (0, 2), F32)
    both = kept + came.astype(F32)
    mine, other = both[:, :cols], both[:, cols:].astype(BF16)
    far = across(other, 2)
    grad_queries = query_grad_call(
        odd, prob, attended, key_rows, k2, value_rows, v2, r1, r2, r3, g
    )
    grad_keys, grad_values = key_grad_call(
        odd, lo, key_rows, value_rows, queries, q2, r1, r3, (g, g1, g2), (stat, stat1, stat2)
    )
    mixed = (mine + far.astype(F32)).astype(BF16)
    return (mixed, grad_queries, grad_keys, grad_values)


def solution(mesh):
    in_specs = (
        P("ctx", "head"),
        P("ctx", "head"),
        P("ctx", "head"),
        P("head", None),
        P("ctx", "head"),
        P(),
    )
    out_specs = (P("ctx", "head"), P("ctx", "head"), P("ctx", "head"), P("ctx", "head"))
    return jax.shard_map(layer, mesh=mesh, in_specs=in_specs, out_specs=out_specs, check_vma=False)
```

```python
import functools
import math

import jax
import jax.numpy as jnp
from jax import lax
from jax.experimental import pallas as pl
from jax.experimental.pallas import tpu as pltpu
from jax.sharding import PartitionSpec as P


HD = 128
REACH = 2
PREV = 3
ROWS = 128
NEG_FILL = -1e30
SCALE = 1.0 / math.sqrt(HD)
LOG2E = 1.4426950408889634
VMEM_BYTES = 32 << 20
F32 = jnp.float32
BF16 = jnp.bfloat16


NT = (((1,), (1,)), ((), ()))
NN = (((1,), (0,)), ((), ()))


def passed_along(shard, axis, by):
    length = lax.axis_size(axis)
    pairs = [(i, i + by) for i in range(length) if 0 <= i + by < length]
    return lax.ppermute(shard, axis, pairs)


def swapped(shard, axis, bit):
    length = lax.axis_size(axis)
    return lax.ppermute(shard, axis, [(i, i ^ bit) for i in range(length)])


def windows_kernel(base_ref, offsets_ref, col_ref, row_ref):
    tiles, rows = row_ref.shape
    lines = tiles * rows // HD
    place = HD * lax.broadcasted_iota(jnp.int32, (lines, HD), 0) + lax.broadcasted_iota(
        jnp.int32, (lines, HD), 1
    )
    position = base_ref[0] + place

    def step(m, first):
        return jnp.where(offsets_ref[m + PREV] <= position, offsets_ref[m], first)

    first = lax.fori_loop(
        0, offsets_ref.shape[0] - PREV, step, jnp.zeros_like(position), unroll=4
    )
    first = jnp.where(position < base_ref[1], first - base_ref[0], tiles * rows)
    for line in range(lines):
        tile, start = divmod(line * HD, rows)
        row_ref[tile : tile + 1, start : start + HD] = first[line : line + 1, :]
        if tile == 0:
            spread = jnp.broadcast_to(first[line : line + 1, :], (HD, HD))
            col_ref[start : start + HD, :] = spread.T


def windows_call(base, offsets, rows):
    return pl.pallas_call(
        windows_kernel,
        name="windows",
        out_shape=(
            jax.ShapeDtypeStruct((rows, HD), jnp.int32),
            jax.ShapeDtypeStruct((REACH + 1, rows), jnp.int32),
        ),
        in_specs=[pl.BlockSpec(memory_space=pltpu.SMEM)] * 2,
        compiler_params=pltpu.CompilerParams(vmem_limit_bytes=VMEM_BYTES),
        cost_estimate=pl.CostEstimate(flops=1 << 20, bytes_accessed=1 << 18, transcendentals=0),
    )(base, offsets)


def mm(a, b, dims):
    return lax.dot_general(a, b, dims, preferred_element_type=F32)


def grad_out_kernel(me_ref, c0, c1, c2, c3, w_ref, out_ref):
    cols = c0.shape[1]
    total = None
    for s, c in enumerate((c0, c1, c2, c3)):
        start = pl.multiple_of((me_ref[0] ^ s) * cols, cols)
        part = mm(c[...], w_ref[:, pl.ds(start, cols)], NT)
        total = part if total is None else total + part
    out_ref[...] = total.astype(BF16)


def grad_out_call(me, shards, weight):
    rows, cols = shards[0].shape
    whole = pl.BlockSpec((rows, cols), lambda h, me: (0, 0))
    return pl.pallas_call(
        grad_out_kernel,
        name="grad_out",
        out_shape=jax.ShapeDtypeStruct((rows, cols), BF16),
        grid_spec=pltpu.PrefetchScalarGridSpec(
            num_scalar_prefetch=1,
            grid=(cols // (2 * HD),),
            in_specs=[whole] * 4
            + [pl.BlockSpec((2 * HD, weight.shape[1]), lambda h, me: (h, 0))],
            out_specs=pl.BlockSpec((rows, 2 * HD), lambda h, me: (0, h)),
        ),
        compiler_params=pltpu.CompilerParams(vmem_limit_bytes=VMEM_BYTES),
        cost_estimate=pl.CostEstimate(
            flops=2 * rows * cols * weight.shape[1], bytes_accessed=6 << 20, transcendentals=0
        ),
    )(me, *shards, weight)


def key_pieces(block, rows):
    first, last = block * ROWS, (block + 1) * ROWS
    return ((2, first, rows, -2 * rows), (1, 0, rows, -rows), (0, 0, last, 0))


def pick(odd, even_ref, odd_ref, into):
    @pl.when(odd == 0)
    def _():
        into[...] = even_ref[...]

    @pl.when(odd == 1)
    def _():
        into[...] = odd_ref[...]


def attend_kernel(
    odd_ref, me_ref, lo_ref, q, k0, k2, v0, v2, r1, r2, r3, g, w_ref,
    att_ref, prob_ref, stat_ref, sent_ref, mine_ref, far_ref, k1, v1,
):
    rows = q.shape[0]
    head = pl.program_id(0)
    pick(odd_ref[0], r2, r1, k1)
    pick(odd_ref[0], r3, r2, v1)
    keys, values = (k0, k1, k2), (v0, v1, v2)
    for b in range(rows // ROWS):
        mine = slice(b * ROWS, (b + 1) * ROWS)
        qb = q[mine, :]
        lo = lo_ref[mine, :]
        scores = []
        for tile, first, last, off in key_pieces(b, rows):
            raw = mm(qb, keys[tile][first:last, :], NT)
            for c in range(0, last - first, HD):
                part = raw[:, c : c + HD]
                pos = off + first + c + lax.broadcasted_iota(jnp.int32, part.shape, 1)
                ok = pos >= lo
                if tile == 0 and first + c == b * ROWS:
                    ok &= pos <= b * ROWS + lax.broadcasted_iota(jnp.int32, part.shape, 0)
                scores.append(jnp.where(ok, part, NEG_FILL))
        top = jnp.max(functools.reduce(jnp.maximum, scores), axis=1, keepdims=True)
        shift = jnp.broadcast_to(top * (SCALE * LOG2E), (ROWS, HD))
        exps = [jnp.exp2(s * (SCALE * LOG2E) - shift) for s in scores]
        total = jnp.sum(functools.reduce(jnp.add, exps), axis=1, keepdims=True)
        inverse = jnp.broadcast_to(1.0 / total, (ROWS, HD))
        mixed = None
        for n, e in enumerate(exps):
            prob_ref[0, mine, n * HD : (n + 1) * HD] = (e * inverse).astype(BF16)
        column = 0
        for tile, first, last, off in key_pieces(b, rows):
            prob = prob_ref[0, mine, column : column + last - first]
            column += last - first
            part = mm(prob, values[tile][first:last, :], NN)
            mixed = part if mixed is None else mixed + part
        attended = mixed.astype(BF16)
        att_ref[mine, pl.ds(pl.multiple_of(head * HD, HD), HD)] = attended
        delta = jnp.sum(attended.astype(F32) * g[mine, :].astype(F32), axis=1, keepdims=True)
        log_total = shift + jnp.log2(total)
        lane = lax.broadcasted_iota(jnp.int32, (ROWS, ROWS), 1)
        stats = jnp.where(lane == 0, log_total, delta).T
        stat_ref[0, :, mine] = stats[0:2, :]

    @pl.when(head == pl.num_programs(0) - 1)
    def _():
        cols = att_ref.shape[1]

        def project(group):
            start = pl.multiple_of((me_ref[0] ^ group) * cols, cols)
            return mm(att_ref[...], w_ref[:, pl.ds(start, cols)], NN)

        sent_ref[:, 0:cols] = project(1).astype(BF16)
        sent_ref[:, cols : 2 * cols] = project(3).astype(BF16)
        far_ref[...] = project(2)
        mine_ref[...] = project(0)


def tile_specs(rows):
    tile = pl.BlockSpec((rows, HD), lambda h, odd, *_: (0, h))
    on_odd = pl.BlockSpec((rows, HD), lambda h, odd, *_: (0, h * odd[0]))
    on_even = pl.BlockSpec((rows, HD), lambda h, odd, *_: (0, h * (1 - odd[0])))
    return tile, on_odd, on_even


def attend_call(odd, me, lo, q, k0, k2, v0, v2, r1, r2, r3, g, weight):
    rows, cols = q.shape
    heads = cols // HD
    tile, on_odd, on_even = tile_specs(rows)
    span = REACH * rows + ROWS
    whole = pl.BlockSpec((rows, cols), lambda h, odd, me: (0, 0))
    return pl.pallas_call(
        attend_kernel,
        name="attend",
        out_shape=(
            jax.ShapeDtypeStruct((rows, cols), BF16),
            jax.ShapeDtypeStruct((heads, rows, span), BF16),
            jax.ShapeDtypeStruct((heads, 2, rows), F32),
            jax.ShapeDtypeStruct((rows, 2 * cols), BF16),
            jax.ShapeDtypeStruct((rows, cols), F32),
            jax.ShapeDtypeStruct((rows, cols), F32),
        ),
        grid_spec=pltpu.PrefetchScalarGridSpec(
            num_scalar_prefetch=2,
            grid=(heads,),
            in_specs=[pl.BlockSpec((rows, HD), lambda h, odd, me: (0, 0))]
            + [tile] * 5
            + [on_odd, tile, on_even, tile]
            + [pl.BlockSpec(weight.shape, lambda h, odd, me: (0, 0))],
            out_specs=(
                whole,
                pl.BlockSpec((1, rows, span), lambda h, odd, me: (h, 0, 0)),
                pl.BlockSpec((1, 2, rows), lambda h, odd, me: (h, 0, 0)),
                pl.BlockSpec((rows, 2 * cols), lambda h, odd, me: (0, 0)),
                whole,
                whole,
            ),
            scratch_shapes=[pltpu.VMEM((rows, HD), BF16)] * 2,
        ),
        compiler_params=pltpu.CompilerParams(vmem_limit_bytes=VMEM_BYTES),
        cost_estimate=pl.CostEstimate(
            flops=8 * heads * rows * span * HD, bytes_accessed=12 << 20,
            transcendentals=heads * rows * span,
        ),
    )(odd, me, lo, q, k0, k2, v0, v2, r1, r2, r3, g, weight)


def query_grad_kernel(odd_ref, prob_ref, att, k0, k2, v0, v2, r1, r2, r3, g, out_ref, k1, v1):
    rows = g.shape[0]
    pick(odd_ref[0], r2, r1, k1)
    pick(odd_ref[0], r3, r2, v1)
    keys, values = (k0, k1, k2), (v0, v1, v2)
    for b in range(rows // ROWS):
        mine = slice(b * ROWS, (b + 1) * ROWS)
        gb = g[mine, :]
        delta = jnp.sum(att[mine, :].astype(F32) * gb.astype(F32), axis=1, keepdims=True)
        total = None
        column = 0
        for tile, first, last, off in key_pieces(b, rows):
            prob = prob_ref[0, mine, column : column + last - first].astype(F32)
            column += last - first
            grad_prob = mm(gb, values[tile][first:last, :], NT)
            grad_score = (prob * (grad_prob - delta)).astype(BF16)
            part = mm(grad_score, keys[tile][first:last, :], NN)
            total = part if total is None else total + part
        out_ref[mine, :] = (total * SCALE).astype(BF16)


def query_grad_call(odd, prob, att, k0, k2, v0, v2, r1, r2, r3, g):
    rows, cols = g.shape
    heads = cols // HD
    tile, on_odd, on_even = tile_specs(rows)
    span = REACH * rows + ROWS
    return pl.pallas_call(
        query_grad_kernel,
        name="query_grad",
        out_shape=jax.ShapeDtypeStruct((rows, cols), BF16),
        grid_spec=pltpu.PrefetchScalarGridSpec(
            num_scalar_prefetch=1,
            grid=(heads,),
            in_specs=[pl.BlockSpec((1, rows, span), lambda h, odd: (h, 0, 0))]
            + [tile] * 5
            + [on_odd, tile, on_even, tile],
            out_specs=tile,
            scratch_shapes=[pltpu.VMEM((rows, HD), BF16)] * 2,
        ),
        compiler_params=pltpu.CompilerParams(vmem_limit_bytes=VMEM_BYTES),
        cost_estimate=pl.CostEstimate(
            flops=4 * heads * rows * span * HD, bytes_accessed=8 << 20, transcendentals=0
        ),
    )(odd, prob, att, k0, k2, v0, v2, r1, r2, r3, g)


def key_grad_kernel(
    odd_ref, lo_ref, k, v, q0, q2, r1, r3, g0, g1, g2, s0, s1, s2, dk_ref, dv_ref, q1
):
    rows = k.shape[0]
    pick(odd_ref[0], r1, r3, q1)
    queries, grads, stats = (q0, q1, q2), (g0, g1, g2), (s0, s1, s2)
    for b in range(rows // ROWS):
        mine = slice(b * ROWS, (b + 1) * ROWS)
        kb, vb = k[mine, :], v[mine, :]
        dk = dv = None
        pieces = ((0, b * ROWS, rows), (1, 0, rows), (2, 0, (b + 1) * ROWS))
        for tile, first, last in pieces:
            qt, gt = queries[tile][first:last, :], grads[tile][first:last, :]
            raw = mm(kb, qt, NT)
            pos = b * ROWS + lax.broadcasted_iota(jnp.int32, raw.shape, 0)
            ok = pos >= lo_ref[tile : tile + 1, first:last]
            if tile == 0:
                ok &= pos <= first + lax.broadcasted_iota(jnp.int32, raw.shape, 1)
            log_total = stats[tile][0, 0:1, first:last]
            delta = stats[tile][0, 1:2, first:last]
            prob = jnp.where(ok, jnp.exp2(raw * (SCALE * LOG2E) - log_total), 0.0)
            grad_prob = mm(vb, gt, NT)
            grad_score = (prob * (grad_prob - delta)).astype(BF16)
            part_k = mm(grad_score, qt, NN)
            part_v = mm(prob.astype(BF16), gt, NN)
            dk = part_k if dk is None else dk + part_k
            dv = part_v if dv is None else dv + part_v
        dk_ref[mine, :] = (dk * SCALE).astype(BF16)
        dv_ref[mine, :] = dv.astype(BF16)


def key_grad_call(odd, lo, k, v, q0, q2, r1, r3, grads, stats):
    rows, cols = k.shape
    heads = cols // HD
    tile, on_odd, on_even = tile_specs(rows)
    stat = pl.BlockSpec((1, 2, rows), lambda h, odd: (h, 0, 0))
    span = REACH * rows + ROWS
    return pl.pallas_call(
        key_grad_kernel,
        name="key_grad",
        out_shape=(jax.ShapeDtypeStruct((rows, cols), BF16),) * 2,
        grid_spec=pltpu.PrefetchScalarGridSpec(
            num_scalar_prefetch=1,
            grid=(heads,),
            in_specs=[pl.BlockSpec((REACH + 1, rows), lambda h, odd: (0, 0))]
            + [tile] * 4
            + [on_even, on_odd]
            + [tile] * 3
            + [stat] * 3,
            out_specs=(tile, tile),
            scratch_shapes=[pltpu.VMEM((rows, HD), BF16)],
        ),
        compiler_params=pltpu.CompilerParams(vmem_limit_bytes=VMEM_BYTES),
        cost_estimate=pl.CostEstimate(
            flops=8 * heads * rows * span * HD, bytes_accessed=5 << 20,
            transcendentals=heads * rows * span,
        ),
    )(odd, lo, k, v, q0, q2, r1, r3, *grads, *stats)


def layer(queries, key_rows, value_rows, out_weight, cotangent, offsets):
    rows, cols = queries.shape
    count = lax.axis_size("ctx")
    index = lax.axis_index("ctx")
    base = index * rows
    odd = (index % 2).astype(jnp.int32).reshape(1)
    me = lax.axis_index("head").astype(jnp.int32).reshape(1)

    def along(shard, by):
        return passed_along(shard, "ctx", by)

    def across(shard, bit):
        return swapped(shard, "head", bit)

    def pair(from_even, from_odd):
        return swapped(jnp.where(index % 2 == 0, from_even, from_odd), "ctx", 1)

    def turned(shard, by):
        return lax.ppermute(shard, "ctx", [(i, (i + by) % count) for i in range(count)])

    cot_far = across(cotangent, 2)
    cot_near = across(cotangent, 1)
    k2 = along(key_rows, 2)
    r1 = pair(key_rows, queries)
    v2 = along(value_rows, 2)
    cot_both = across(cot_far, 1)
    q2 = along(queries, -2)
    r2 = pair(value_rows, k2)

    g = grad_out_call(me, (cotangent, cot_near, cot_far, cot_both), out_weight)
    g2 = along(g, -2)
    bounds = jnp.stack([base, count * rows]).astype(jnp.int32)
    lo_col, lo_row = windows_call(bounds, offsets, rows)
    r3 = pair(q2, v2)
    g1 = pair(g2, g)

    attended, prob, stat, sent, kept, kept_far = attend_call(
        odd, me, lo_col, queries, key_rows, k2, value_rows, v2, r1, r2, r3, g, out_weight
    )
    stat1 = turned(stat, -1)
    stat2 = turned(stat, -2)
    came = across(sent, 1)
    far = across((kept_far + came[:, cols:].astype(F32)).astype(BF16), 2)

    grad_queries = query_grad_call(
        odd, prob, attended, key_rows, k2, value_rows, v2, r1, r2, r3, g
    )
    grad_keys, grad_values = key_grad_call(
        odd, lo_row, key_rows, value_rows, queries, q2, r1, r3, (g, g1, g2), (stat, stat1, stat2)
    )
    mixed = (kept + came[:, :cols].astype(F32) + far.astype(F32)).astype(BF16)
    return (mixed, grad_queries, grad_keys, grad_values)


def solution(mesh):
    in_specs = (
        P("ctx", "head"),
        P("ctx", "head"),
        P("ctx", "head"),
        P("head", None),
        P("ctx", "head"),
        P(),
    )
    out_specs = (P("ctx", "head"), P("ctx", "head"), P("ctx", "head"), P("ctx", "head"))
    return jax.shard_map(layer, mesh=mesh, in_specs=in_specs, out_specs=out_specs, check_vma=False)
```

```python
import functools
import math

import jax
import jax.numpy as jnp
from jax import lax
from jax.experimental import pallas as pl
from jax.experimental.pallas import tpu as pltpu
from jax.sharding import PartitionSpec as P


HD = 128
REACH = 2
PREV = 3
ROWS = 128
NEG_FILL = -1e30
SCALE = 1.0 / math.sqrt(HD)
LOG2E = 1.4426950408889634
VMEM_BYTES = 32 << 20
F32 = jnp.float32
BF16 = jnp.bfloat16


NT = (((1,), (1,)), ((), ()))
NN = (((1,), (0,)), ((), ()))


def passed_along(shard, axis, by):
    length = lax.axis_size(axis)
    pairs = [(i, i + by) for i in range(length) if 0 <= i + by < length]
    return lax.ppermute(shard, axis, pairs)


def swapped(shard, axis, bit):
    length = lax.axis_size(axis)
    return lax.ppermute(shard, axis, [(i, i ^ bit) for i in range(length)])


def windows_kernel(base_ref, offsets_ref, col_ref, row_ref):
    tiles, rows = row_ref.shape
    lines = tiles * rows // HD
    place = HD * lax.broadcasted_iota(jnp.int32, (lines, HD), 0) + lax.broadcasted_iota(
        jnp.int32, (lines, HD), 1
    )
    position = base_ref[0] + place

    def step(m, first):
        return jnp.where(offsets_ref[m + PREV] <= position, offsets_ref[m], first)

    first = lax.fori_loop(
        0, offsets_ref.shape[0] - PREV, step, jnp.zeros_like(position), unroll=4
    )
    first = jnp.where(position < base_ref[1], first - base_ref[0], tiles * rows)
    for line in range(lines):
        tile, start = divmod(line * HD, rows)
        row_ref[tile : tile + 1, start : start + HD] = first[line : line + 1, :]
        if tile == 0:
            spread = jnp.broadcast_to(first[line : line + 1, :], (HD, HD))
            col_ref[start : start + HD, :] = spread.T


def windows_call(base, offsets, rows):
    return pl.pallas_call(
        windows_kernel,
        name="windows",
        out_shape=(
            jax.ShapeDtypeStruct((rows, HD), jnp.int32),
            jax.ShapeDtypeStruct((REACH + 1, rows), jnp.int32),
        ),
        in_specs=[pl.BlockSpec(memory_space=pltpu.SMEM)] * 2,
        compiler_params=pltpu.CompilerParams(vmem_limit_bytes=VMEM_BYTES),
        cost_estimate=pl.CostEstimate(flops=1 << 20, bytes_accessed=1 << 18, transcendentals=0),
    )(base, offsets)


def in_hbm(*arrays):
    return [pltpu.with_memory_space_constraint(x, pltpu.HBM) for x in arrays]


def in_vmem(*arrays):
    return [pltpu.with_memory_space_constraint(x, pltpu.VMEM) for x in arrays]


def mm(a, b, dims):
    return lax.dot_general(a, b, dims, preferred_element_type=F32)


def grad_out_kernel(me_ref, c0, c1, c2, c3, w_ref, out_ref):
    cols = c0.shape[1]
    total = None
    for s, c in enumerate((c0, c1, c2, c3)):
        start = pl.multiple_of((me_ref[0] ^ s) * cols, cols)
        part = mm(c[...], w_ref[:, pl.ds(start, cols)], NT)
        total = part if total is None else total + part
    out_ref[...] = total.astype(BF16)


def grad_out_call(me, shards, weight):
    rows, cols = shards[0].shape
    whole = pl.BlockSpec((rows, cols), lambda h, me: (0, 0))
    return pl.pallas_call(
        grad_out_kernel,
        name="grad_out",
        out_shape=jax.ShapeDtypeStruct((rows, cols), BF16),
        grid_spec=pltpu.PrefetchScalarGridSpec(
            num_scalar_prefetch=1,
            grid=(cols // (2 * HD),),
            in_specs=[whole] * 4
            + [pl.BlockSpec((2 * HD, weight.shape[1]), lambda h, me: (h, 0))],
            out_specs=pl.BlockSpec((rows, 2 * HD), lambda h, me: (0, h)),
        ),
        compiler_params=pltpu.CompilerParams(vmem_limit_bytes=VMEM_BYTES),
        cost_estimate=pl.CostEstimate(
            flops=2 * rows * cols * weight.shape[1], bytes_accessed=6 << 20, transcendentals=0
        ),
    )(me, *in_hbm(shards[0]), *in_vmem(*shards[1:]), *in_hbm(weight))


def key_pieces(block, rows):
    first, last = block * ROWS, (block + 1) * ROWS
    return ((2, first, rows, -2 * rows), (1, 0, rows, -rows), (0, 0, last, 0))


def pick(odd, even_ref, odd_ref, into):
    @pl.when(odd == 0)
    def _():
        into[...] = even_ref[...]

    @pl.when(odd == 1)
    def _():
        into[...] = odd_ref[...]


def attend_kernel(
    odd_ref, me_ref, lo_ref, q, k0, k2, v0, v2, r1, r2, r3, g, w_ref,
    att_ref, prob_ref, stat_ref, sent_ref, mine_ref, far_ref, k1, v1,
):
    rows = q.shape[0]
    head = pl.program_id(0)
    pick(odd_ref[0], r2, r1, k1)
    pick(odd_ref[0], r3, r2, v1)
    keys, values = (k0, k1, k2), (v0, v1, v2)
    for b in range(rows // ROWS):
        mine = slice(b * ROWS, (b + 1) * ROWS)
        qb = q[mine, :]
        lo = lo_ref[mine, :]
        scores = []
        for tile, first, last, off in key_pieces(b, rows):
            raw = mm(qb, keys[tile][first:last, :], NT)
            for c in range(0, last - first, HD):
                part = raw[:, c : c + HD]
                pos = off + first + c + lax.broadcasted_iota(jnp.int32, part.shape, 1)
                ok = pos >= lo
                if tile == 0 and first + c == b * ROWS:
                    ok &= pos <= b * ROWS + lax.broadcasted_iota(jnp.int32, part.shape, 0)
                scores.append(jnp.where(ok, part, NEG_FILL))
        top = jnp.max(functools.reduce(jnp.maximum, scores), axis=1, keepdims=True)
        shift = jnp.broadcast_to(top * (SCALE * LOG2E), (ROWS, HD))
        exps = [jnp.exp2(s * (SCALE * LOG2E) - shift) for s in scores]
        total = jnp.sum(functools.reduce(jnp.add, exps), axis=1, keepdims=True)
        inverse = jnp.broadcast_to(1.0 / total, (ROWS, HD))
        mixed = None
        for n, e in enumerate(exps):
            prob_ref[0, mine, n * HD : (n + 1) * HD] = (e * inverse).astype(BF16)
        column = 0
        for tile, first, last, off in key_pieces(b, rows):
            prob = prob_ref[0, mine, column : column + last - first]
            column += last - first
            part = mm(prob, values[tile][first:last, :], NN)
            mixed = part if mixed is None else mixed + part
        attended = mixed.astype(BF16)
        att_ref[mine, pl.ds(pl.multiple_of(head * HD, HD), HD)] = attended
        delta = jnp.sum(attended.astype(F32) * g[mine, :].astype(F32), axis=1, keepdims=True)
        log_total = shift + jnp.log2(total)
        lane = lax.broadcasted_iota(jnp.int32, (ROWS, ROWS), 1)
        stats = jnp.where(lane == 0, log_total, delta).T
        stat_ref[0, :, mine] = stats[0:2, :]

    @pl.when(head == pl.num_programs(0) - 1)
    def _():
        cols = att_ref.shape[1]

        def project(group):
            start = pl.multiple_of((me_ref[0] ^ group) * cols, cols)
            return mm(att_ref[...], w_ref[:, pl.ds(start, cols)], NN)

        sent_ref[:, 0:cols] = project(1).astype(BF16)
        sent_ref[:, cols : 2 * cols] = project(3).astype(BF16)
        far_ref[...] = project(2)
        mine_ref[...] = project(0)


def tile_specs(rows):
    tile = pl.BlockSpec((rows, HD), lambda h, odd, *_: (0, h))
    on_odd = pl.BlockSpec((rows, HD), lambda h, odd, *_: (0, h * odd[0]))
    on_even = pl.BlockSpec((rows, HD), lambda h, odd, *_: (0, h * (1 - odd[0])))
    return tile, on_odd, on_even


def attend_call(odd, me, lo, q, k0, k2, v0, v2, r1, r2, r3, g, weight):
    rows, cols = q.shape
    heads = cols // HD
    tile, on_odd, on_even = tile_specs(rows)
    span = REACH * rows + ROWS
    whole = pl.BlockSpec((rows, cols), lambda h, odd, me: (0, 0))
    return pl.pallas_call(
        attend_kernel,
        name="attend",
        out_shape=(
            jax.ShapeDtypeStruct((rows, cols), BF16),
            jax.ShapeDtypeStruct((heads, rows, span), BF16),
            jax.ShapeDtypeStruct((heads, 2, rows), F32),
            jax.ShapeDtypeStruct((rows, 2 * cols), BF16),
            jax.ShapeDtypeStruct((rows, cols), F32),
            jax.ShapeDtypeStruct((rows, cols), F32),
        ),
        grid_spec=pltpu.PrefetchScalarGridSpec(
            num_scalar_prefetch=2,
            grid=(heads,),
            in_specs=[pl.BlockSpec((rows, HD), lambda h, odd, me: (0, 0))]
            + [tile] * 5
            + [on_odd, tile, on_even, tile]
            + [pl.BlockSpec(weight.shape, lambda h, odd, me: (0, 0))],
            out_specs=(
                whole,
                pl.BlockSpec((1, rows, span), lambda h, odd, me: (h, 0, 0)),
                pl.BlockSpec((1, 2, rows), lambda h, odd, me: (h, 0, 0)),
                pl.BlockSpec((rows, 2 * cols), lambda h, odd, me: (0, 0)),
                whole,
                whole,
            ),
            scratch_shapes=[pltpu.VMEM((rows, HD), BF16)] * 2,
        ),
        compiler_params=pltpu.CompilerParams(vmem_limit_bytes=VMEM_BYTES),
        cost_estimate=pl.CostEstimate(
            flops=8 * heads * rows * span * HD, bytes_accessed=12 << 20,
            transcendentals=heads * rows * span,
        ),
    )(odd, me, lo, *in_hbm(q, k0), *in_vmem(k2), *in_hbm(v0), *in_vmem(v2, r1, r2, r3, g), *in_hbm(weight))


def query_grad_kernel(odd_ref, prob_ref, att, k0, k2, v0, v2, r1, r2, r3, g, out_ref, k1, v1):
    rows = g.shape[0]
    pick(odd_ref[0], r2, r1, k1)
    pick(odd_ref[0], r3, r2, v1)
    keys, values = (k0, k1, k2), (v0, v1, v2)
    for b in range(rows // ROWS):
        mine = slice(b * ROWS, (b + 1) * ROWS)
        gb = g[mine, :]
        delta = jnp.sum(att[mine, :].astype(F32) * gb.astype(F32), axis=1, keepdims=True)
        total = None
        column = 0
        for tile, first, last, off in key_pieces(b, rows):
            prob = prob_ref[0, mine, column : column + last - first].astype(F32)
            column += last - first
            grad_prob = mm(gb, values[tile][first:last, :], NT)
            grad_score = (prob * (grad_prob - delta)).astype(BF16)
            part = mm(grad_score, keys[tile][first:last, :], NN)
            total = part if total is None else total + part
        out_ref[mine, :] = (total * SCALE).astype(BF16)


def query_grad_call(odd, prob, att, k0, k2, v0, v2, r1, r2, r3, g):
    rows, cols = g.shape
    heads = cols // HD
    tile, on_odd, on_even = tile_specs(rows)
    span = REACH * rows + ROWS
    return pl.pallas_call(
        query_grad_kernel,
        name="query_grad",
        out_shape=jax.ShapeDtypeStruct((rows, cols), BF16),
        grid_spec=pltpu.PrefetchScalarGridSpec(
            num_scalar_prefetch=1,
            grid=(heads,),
            in_specs=[pl.BlockSpec((1, rows, span), lambda h, odd: (h, 0, 0))]
            + [tile] * 5
            + [on_odd, tile, on_even, tile],
            out_specs=tile,
            scratch_shapes=[pltpu.VMEM((rows, HD), BF16)] * 2,
        ),
        compiler_params=pltpu.CompilerParams(vmem_limit_bytes=VMEM_BYTES),
        cost_estimate=pl.CostEstimate(
            flops=4 * heads * rows * span * HD, bytes_accessed=8 << 20, transcendentals=0
        ),
    )(odd, prob, att, *in_hbm(k0), *in_vmem(k2), *in_hbm(v0), *in_vmem(v2, r1, r2, r3, g))


def key_grad_kernel(
    odd_ref, me_ref, lo_ref, k, v, q0, q2, r1, r3, g0, g1, g2, s0, s10, s11, s20, s21,
    dk_ref, dv_ref, q1, s1, s2,
):
    rows = k.shape[0]
    pick(odd_ref[0], r1, r3, q1)
    pick(me_ref[0] & 1, s10, s11, s1)
    pick(me_ref[0] & 1, s20, s21, s2)
    queries, grads, stats = (q0, q1, q2), (g0, g1, g2), (s0, s1, s2)
    for b in range(rows // ROWS):
        mine = slice(b * ROWS, (b + 1) * ROWS)
        kb, vb = k[mine, :], v[mine, :]
        dk = dv = None
        pieces = ((0, b * ROWS, rows), (1, 0, rows), (2, 0, (b + 1) * ROWS))
        for tile, first, last in pieces:
            qt, gt = queries[tile][first:last, :], grads[tile][first:last, :]
            raw = mm(kb, qt, NT)
            pos = b * ROWS + lax.broadcasted_iota(jnp.int32, raw.shape, 0)
            ok = pos >= lo_ref[tile : tile + 1, first:last]
            if tile == 0:
                ok &= pos <= first + lax.broadcasted_iota(jnp.int32, raw.shape, 1)
            log_total = stats[tile][0, 0:1, first:last]
            delta = stats[tile][0, 1:2, first:last]
            prob = jnp.where(ok, jnp.exp2(raw * (SCALE * LOG2E) - log_total), 0.0)
            grad_prob = mm(vb, gt, NT)
            grad_score = (prob * (grad_prob - delta)).astype(BF16)
            part_k = mm(grad_score, qt, NN)
            part_v = mm(prob.astype(BF16), gt, NN)
            dk = part_k if dk is None else dk + part_k
            dv = part_v if dv is None else dv + part_v
        dk_ref[mine, :] = (dk * SCALE).astype(BF16)
        dv_ref[mine, :] = dv.astype(BF16)


def key_grad_call(odd, me, lo, k, v, q0, q2, r1, r3, grads, stats):
    rows, cols = k.shape
    heads = cols // HD
    tile, on_odd, on_even = tile_specs(rows)
    stat = pl.BlockSpec((1, 2, rows), lambda h, odd, me: (h, 0, 0))
    span = REACH * rows + ROWS
    return pl.pallas_call(
        key_grad_kernel,
        name="key_grad",
        out_shape=(jax.ShapeDtypeStruct((rows, cols), BF16),) * 2,
        grid_spec=pltpu.PrefetchScalarGridSpec(
            num_scalar_prefetch=2,
            grid=(heads,),
            in_specs=[pl.BlockSpec((REACH + 1, rows), lambda h, odd, me: (0, 0))]
            + [tile] * 4
            + [on_even, on_odd]
            + [tile] * 3
            + [stat] * 5,
            out_specs=(tile, tile),
            scratch_shapes=[pltpu.VMEM((rows, HD), BF16)] + [pltpu.VMEM((1, 2, rows), F32)] * 2,
        ),
        compiler_params=pltpu.CompilerParams(vmem_limit_bytes=VMEM_BYTES),
        cost_estimate=pl.CostEstimate(
            flops=8 * heads * rows * span * HD, bytes_accessed=5 << 20,
            transcendentals=heads * rows * span,
        ),
    )(odd, me, lo, *in_hbm(k, v, q0), *in_vmem(q2, r1, r3, *grads), *stats)


def layer(queries, key_rows, value_rows, out_weight, cotangent, offsets):
    rows, cols = queries.shape
    count = lax.axis_size("ctx")
    index = lax.axis_index("ctx")
    base = index * rows
    odd = (index % 2).astype(jnp.int32).reshape(1)
    me = lax.axis_index("head").astype(jnp.int32).reshape(1)

    def along(shard, by):
        return passed_along(shard, "ctx", by)

    def across(shard, bit):
        return swapped(shard, "head", bit)

    def pair(from_even, from_odd):
        return swapped(jnp.where(index % 2 == 0, from_even, from_odd), "ctx", 1)

    def ringed(shard, by, bit):
        groups = lax.axis_size("head")
        pairs = []
        for i in range(count):
            for h in range(groups):
                to = i - by if (h & 1) == bit else i + by
                here = i * groups + h
                pairs.append((here, to * groups + h if 0 <= to < count else here ^ 1))
        return lax.ppermute(shard, ("ctx", "head"), pairs)

    cot_far = across(cotangent, 2)
    cot_near = across(cotangent, 1)
    k2 = along(key_rows, 2)
    r1 = pair(key_rows, queries)
    v2 = along(value_rows, 2)
    cot_both = across(cot_far, 1)
    q2 = along(queries, -2)
    r2 = pair(value_rows, k2)

    g = grad_out_call(me, (cotangent, cot_near, cot_far, cot_both), out_weight)
    g2 = along(g, -2)
    bounds = jnp.stack([base, count * rows]).astype(jnp.int32)
    lo_col, lo_row = windows_call(bounds, offsets, rows)
    r3 = pair(q2, v2)
    g1 = pair(g2, g)

    attended, prob, stat, sent, kept, kept_far = attend_call(
        odd, me, lo_col, queries, key_rows, k2, value_rows, v2, r1, r2, r3, g, out_weight
    )
    stats = [stat] + [ringed(stat, n, bit) for n in (1, 2) for bit in (0, 1)]
    came = across(sent, 1)
    far = across((kept_far + came[:, cols:].astype(F32)).astype(BF16), 2)

    grad_queries = query_grad_call(
        odd, prob, attended, key_rows, k2, value_rows, v2, r1, r2, r3, g
    )
    grad_keys, grad_values = key_grad_call(
        odd, me, lo_row, key_rows, value_rows, queries, q2, r1, r3, (g, g1, g2), stats
    )
    mixed = (kept + came[:, :cols].astype(F32) + far.astype(F32)).astype(BF16)
    return (mixed, grad_queries, grad_keys, grad_values)


def solution(mesh):
    in_specs = (
        P("ctx", "head"),
        P("ctx", "head"),
        P("ctx", "head"),
        P("head", None),
        P("ctx", "head"),
        P(),
    )
    out_specs = (P("ctx", "head"), P("ctx", "head"), P("ctx", "head"), P("ctx", "head"))
    return jax.shard_map(layer, mesh=mesh, in_specs=in_specs, out_specs=out_specs, check_vma=False)
```

```python
import functools
import math

import jax
import jax.numpy as jnp
from jax import lax
from jax.experimental import pallas as pl
from jax.experimental.pallas import tpu as pltpu
from jax.sharding import PartitionSpec as P


HD = 128
REACH = 2
PREV = 3
ROWS = 128
NEG_FILL = -1e30
SCALE = 1.0 / math.sqrt(HD)
LOG2E = 1.4426950408889634
VMEM_BYTES = 32 << 20
F32 = jnp.float32
BF16 = jnp.bfloat16


NT = (((1,), (1,)), ((), ()))
NN = (((1,), (0,)), ((), ()))


def passed_along(shard, axis, by):
    length = lax.axis_size(axis)
    pairs = [(i, i + by) for i in range(length) if 0 <= i + by < length]
    return lax.ppermute(shard, axis, pairs)


def swapped(shard, axis, bit):
    length = lax.axis_size(axis)
    return lax.ppermute(shard, axis, [(i, i ^ bit) for i in range(length)])


def windows_kernel(base_ref, offsets_ref, col_ref, row_ref):
    tiles, rows = row_ref.shape
    lines = tiles * rows // HD
    place = HD * lax.broadcasted_iota(jnp.int32, (lines, HD), 0) + lax.broadcasted_iota(
        jnp.int32, (lines, HD), 1
    )
    position = base_ref[0] + place

    def step(m, first):
        return jnp.where(offsets_ref[m + PREV] <= position, offsets_ref[m], first)

    first = lax.fori_loop(
        0, offsets_ref.shape[0] - PREV, step, jnp.zeros_like(position), unroll=4
    )
    first = jnp.where(position < base_ref[1], first - base_ref[0], tiles * rows)
    for line in range(lines):
        tile, start = divmod(line * HD, rows)
        row_ref[tile : tile + 1, start : start + HD] = first[line : line + 1, :]
        if tile == 0:
            spread = jnp.broadcast_to(first[line : line + 1, :], (HD, HD))
            col_ref[start : start + HD, :] = spread.T


def windows_call(base, offsets, rows):
    return pl.pallas_call(
        windows_kernel,
        name="windows",
        out_shape=(
            jax.ShapeDtypeStruct((rows, HD), jnp.int32),
            jax.ShapeDtypeStruct((REACH + 1, rows), jnp.int32),
        ),
        in_specs=[pl.BlockSpec(memory_space=pltpu.SMEM)] * 2,
        compiler_params=pltpu.CompilerParams(vmem_limit_bytes=VMEM_BYTES),
        cost_estimate=pl.CostEstimate(flops=1 << 20, bytes_accessed=1 << 18, transcendentals=0),
    )(base, offsets)


def in_hbm(*arrays):
    return [pltpu.with_memory_space_constraint(x, pltpu.HBM) for x in arrays]


def in_vmem(*arrays):
    return [pltpu.with_memory_space_constraint(x, pltpu.VMEM) for x in arrays]


def mm(a, b, dims):
    return lax.dot_general(a, b, dims, preferred_element_type=F32)


def grad_out_kernel(me_ref, c0, c1, c2, c3, w_ref, out_ref):
    cols = c0.shape[1]
    total = None
    for s, c in enumerate((c0, c1, c2, c3)):
        start = pl.multiple_of((me_ref[0] ^ s) * cols, cols)
        part = mm(c[...], w_ref[:, pl.ds(start, cols)], NT)
        total = part if total is None else total + part
    out_ref[...] = total.astype(BF16)


def grad_out_call(me, shards, weight):
    rows, cols = shards[0].shape
    whole = pl.BlockSpec((rows, cols), lambda h, me: (0, 0))
    return pl.pallas_call(
        grad_out_kernel,
        name="grad_out",
        out_shape=jax.ShapeDtypeStruct((rows, cols), BF16),
        grid_spec=pltpu.PrefetchScalarGridSpec(
            num_scalar_prefetch=1,
            grid=(cols // (2 * HD),),
            in_specs=[whole] * 4
            + [pl.BlockSpec((2 * HD, weight.shape[1]), lambda h, me: (h, 0))],
            out_specs=pl.BlockSpec((rows, 2 * HD), lambda h, me: (0, h)),
        ),
        compiler_params=pltpu.CompilerParams(vmem_limit_bytes=VMEM_BYTES),
        cost_estimate=pl.CostEstimate(
            flops=2 * rows * cols * weight.shape[1], bytes_accessed=6 << 20, transcendentals=0
        ),
    )(me, *in_hbm(shards[0]), *in_vmem(*shards[1:]), *in_hbm(weight))


def key_pieces(block, rows):
    first, last = block * ROWS, (block + 1) * ROWS
    return ((2, first, rows, -2 * rows), (1, 0, rows, -rows), (0, 0, last, 0))


def pick(odd, even_ref, odd_ref, into):
    into[...] = jnp.where(odd == 0, even_ref[...], odd_ref[...])


def attend_kernel(
    odd_ref, me_ref, lo_ref, q, k0, k2, v0, v2, r1, r2, r3, g, w_ref,
    att_ref, prob_ref, stat_ref, sent_ref, mine_ref, far_ref, k1, v1,
):
    rows = q.shape[0]
    head = pl.program_id(0)
    pick(odd_ref[0], r2, r1, k1)
    pick(odd_ref[0], r3, r2, v1)
    keys, values = (k0, k1, k2), (v0, v1, v2)
    for b in range(rows // ROWS):
        mine = slice(b * ROWS, (b + 1) * ROWS)
        qb = q[mine, :]
        lo = lo_ref[mine, :]
        scores, places = [], []
        for tile, first, last, off in key_pieces(b, rows):
            raw = mm(qb, keys[tile][first:last, :], NT)
            for c in range(0, last - first, HD):
                part = raw[:, c : c + HD]
                pos = off + first + c + lax.broadcasted_iota(jnp.int32, part.shape, 1)
                ok = pos >= lo
                if tile == 0 and first + c == b * ROWS:
                    ok &= pos <= b * ROWS + lax.broadcasted_iota(jnp.int32, part.shape, 0)
                scores.append(jnp.where(ok, part, NEG_FILL))
                places.append(tile * rows + first + c)
        top = jnp.max(functools.reduce(jnp.maximum, scores), axis=1, keepdims=True)
        shift = jnp.broadcast_to(top * (SCALE * LOG2E), (ROWS, HD))
        exps = [jnp.exp2(s * (SCALE * LOG2E) - shift) for s in scores]
        total = jnp.sum(functools.reduce(jnp.add, exps), axis=1, keepdims=True)
        inverse = jnp.broadcast_to(1.0 / total, (ROWS, HD))
        mixed = None
        for e, place in zip(exps, places):
            prob_ref[0, mine, place : place + HD] = (e * inverse).astype(BF16)
        for tile, first, last, off in key_pieces(b, rows):
            prob = prob_ref[0, mine, tile * rows + first : tile * rows + last]
            part = mm(prob, values[tile][first:last, :], NN)
            mixed = part if mixed is None else mixed + part
        attended = mixed.astype(BF16)
        att_ref[mine, pl.ds(pl.multiple_of(head * HD, HD), HD)] = attended
        delta = jnp.sum(attended.astype(F32) * g[mine, :].astype(F32), axis=1, keepdims=True)
        log_total = shift + jnp.log2(total)
        lane = lax.broadcasted_iota(jnp.int32, (ROWS, ROWS), 1)
        stats = jnp.where(lane == 0, log_total, delta).T
        stat_ref[0, :, mine] = stats[0:2, :]

    @pl.when(head == pl.num_programs(0) - 1)
    def _():
        cols = att_ref.shape[1]

        def project(group):
            start = pl.multiple_of((me_ref[0] ^ group) * cols, cols)
            return mm(att_ref[...], w_ref[:, pl.ds(start, cols)], NN)

        sent_ref[:, 0:cols] = project(1).astype(BF16)
        sent_ref[:, cols : 2 * cols] = project(3).astype(BF16)
        far_ref[...] = project(2)
        mine_ref[...] = project(0)


def tile_specs(rows):
    tile = pl.BlockSpec((rows, HD), lambda h, odd, *_: (0, h))
    on_odd = pl.BlockSpec((rows, HD), lambda h, odd, *_: (0, h * odd[0]))
    on_even = pl.BlockSpec((rows, HD), lambda h, odd, *_: (0, h * (1 - odd[0])))
    return tile, on_odd, on_even


def attend_call(odd, me, lo, q, k0, k2, v0, v2, r1, r2, r3, g, weight):
    rows, cols = q.shape
    heads = cols // HD
    tile, on_odd, on_even = tile_specs(rows)
    span = REACH * rows + ROWS
    whole = pl.BlockSpec((rows, cols), lambda h, odd, me: (0, 0))
    return pl.pallas_call(
        attend_kernel,
        name="attend",
        out_shape=(
            jax.ShapeDtypeStruct((rows, cols), BF16),
            jax.ShapeDtypeStruct((heads, rows, (REACH + 1) * rows), BF16),
            jax.ShapeDtypeStruct((heads, 2, rows), F32),
            jax.ShapeDtypeStruct((rows, 2 * cols), BF16),
            jax.ShapeDtypeStruct((rows, cols), F32),
            jax.ShapeDtypeStruct((rows, cols), F32),
        ),
        grid_spec=pltpu.PrefetchScalarGridSpec(
            num_scalar_prefetch=2,
            grid=(heads,),
            in_specs=[pl.BlockSpec((rows, HD), lambda h, odd, me: (0, 0))]
            + [tile] * 5
            + [on_odd, tile, on_even, tile]
            + [pl.BlockSpec(weight.shape, lambda h, odd, me: (0, 0))],
            out_specs=(
                whole,
                pl.BlockSpec((1, rows, (REACH + 1) * rows), lambda h, odd, me: (h, 0, 0)),
                pl.BlockSpec((1, 2, rows), lambda h, odd, me: (h, 0, 0)),
                pl.BlockSpec((rows, 2 * cols), lambda h, odd, me: (0, 0)),
                whole,
                whole,
            ),
            scratch_shapes=[pltpu.VMEM((rows, HD), BF16)] * 2,
        ),
        compiler_params=pltpu.CompilerParams(vmem_limit_bytes=VMEM_BYTES),
        cost_estimate=pl.CostEstimate(
            flops=8 * heads * rows * span * HD, bytes_accessed=12 << 20,
            transcendentals=heads * rows * span,
        ),
    )(odd, me, lo, *in_hbm(q, k0), *in_vmem(k2), *in_hbm(v0), *in_vmem(v2, r1, r2, r3, g), *in_hbm(weight))


def grads_kernel(
    odd_ref, me_ref, lo_ref, prob_ref, att, k0, k2, v0, v2, q0, q2, r1, r2, r3, g0, g1, g2,
    s0, s10, s11, s20, s21, dq_ref, dk_ref, dv_ref,
    kc, qc, gc, v1, s1, s2, probs, grad_s, grad_q,
):
    rows = g0.shape[0]
    blocks = range(0, rows, ROWS)

    @pl.when(pl.program_id(0) == 0)
    def _():
        nothing = jnp.zeros((ROWS, ROWS), BF16)
        for early in blocks:
            for late in range(early + ROWS, rows, ROWS):
                far = 2 * rows
                for into in (probs, grad_s):
                    into[late : late + ROWS, early : early + ROWS] = nothing
                    into[early : early + ROWS, far + late : far + late + ROWS] = nothing
                grad_q[early : early + ROWS, late : late + ROWS] = nothing
                grad_q[late : late + ROWS, far + early : far + early + ROWS] = nothing

    odd, group = odd_ref[0], me_ref[0] & 1
    tiles = [slice(t * rows, (t + 1) * rows) for t in range(REACH + 1)]
    pick(odd, r2, r1, kc.at[tiles[1], :])
    pick(odd, r3, r2, v1)
    pick(odd, r1, r3, qc.at[tiles[1], :])
    pick(group, s10, s11, s1)
    pick(group, s20, s21, s2)
    for into, t, ref in (
        (kc, 0, k0), (kc, 2, k2), (qc, 0, q0), (qc, 2, q2), (gc, 0, g0), (gc, 1, g1), (gc, 2, g2)
    ):
        into[tiles[t], :] = ref[...]
    values, stats = (v0, v1, v2), (s0, s1, s2)

    for t in (0, 2, 1):
        for c in blocks:
            first, last = {0: (0, c + ROWS), 1: (0, rows), 2: (c, rows)}[t]
            at = t * rows + c
            asked = qc[at : at + ROWS, :]
            grad = gc[at : at + ROWS, :]
            raw = mm(k0[first:last, :], asked, NT)
            grad_prob = mm(values[0][first:last, :], grad, NT)
            lo = lo_ref[t : t + 1, c : c + ROWS]
            log_total = stats[t][0, 0:1, c : c + ROWS]
            delta = stats[t][0, 1:2, c : c + ROWS]
            for r in range(first, last, ROWS):
                here = slice(r - first, r - first + ROWS)
                part = raw[here, :]
                pos = r + lax.broadcasted_iota(jnp.int32, part.shape, 0)
                ok = pos >= lo
                if t == 0 and r == c:
                    ok &= pos <= c + lax.broadcasted_iota(jnp.int32, part.shape, 1)
                prob = jnp.where(ok, jnp.exp2(part * (SCALE * LOG2E) - log_total), 0.0)
                probs[r : r + ROWS, at : at + ROWS] = prob.astype(BF16)
                grad_s[r : r + ROWS, at : at + ROWS] = (
                    prob * (grad_prob[here, :] - delta)
                ).astype(BF16)
    dk_ref[...] = (mm(grad_s[...], qc[...], NN) * SCALE).astype(BF16)
    dv_ref[...] = mm(probs[...], gc[...], NN).astype(BF16)

    product = att[...].astype(F32) * g0[...].astype(F32)
    delta = jnp.broadcast_to(jnp.sum(product, axis=1, keepdims=True), (rows, HD))
    for t in (0, 2, 1):
        for c in blocks:
            first, last = {0: (c, rows), 1: (0, rows), 2: (0, c + ROWS)}[t]
            at = t * rows + c
            grad_prob = mm(g0[first:last, :], values[t][c : c + ROWS, :], NT)
            prob = prob_ref[0, first:last, at : at + ROWS].astype(F32)
            grad_q[first:last, at : at + ROWS] = (
                prob * (grad_prob - delta[first:last, :])
            ).astype(BF16)
    dq_ref[...] = (mm(grad_q[...], kc[...], NN) * SCALE).astype(BF16)


def grads_call(odd, me, lo, prob, att, k, v, q, received, grads, stats):
    rows, cols = q[0].shape
    heads = cols // HD
    tile, _, _ = tile_specs(rows)
    span = (REACH + 1) * rows
    stat = pl.BlockSpec((1, 2, rows), lambda h, odd, me: (h, 0, 0))
    hbm = in_hbm(k[0], v[0], q[0])
    vmem = in_vmem(k[1], v[1], q[1], *received, *grads)
    return pl.pallas_call(
        grads_kernel,
        name="grads",
        out_shape=(jax.ShapeDtypeStruct((rows, cols), BF16),) * 3,
        grid_spec=pltpu.PrefetchScalarGridSpec(
            num_scalar_prefetch=2,
            grid=(heads,),
            in_specs=[
                pl.BlockSpec((REACH + 1, rows), lambda h, odd, me: (0, 0)),
                pl.BlockSpec((1, rows, span), lambda h, odd, me: (h, 0, 0)),
            ]
            + [tile] * 13
            + [stat] * 5,
            out_specs=(tile,) * 3,
            scratch_shapes=[pltpu.VMEM((span, HD), BF16)] * 3
            + [pltpu.VMEM((rows, HD), BF16)]
            + [pltpu.VMEM((1, 2, rows), F32)] * 2
            + [pltpu.VMEM((rows, span), BF16)] * 3,
        ),
        compiler_params=pltpu.CompilerParams(vmem_limit_bytes=VMEM_BYTES),
        cost_estimate=pl.CostEstimate(
            flops=12 * heads * rows * span * HD, bytes_accessed=10 << 20,
            transcendentals=heads * rows * span,
        ),
    )(
        odd, me, lo, prob, att, hbm[0], vmem[0], hbm[1], vmem[1], hbm[2], vmem[2], *vmem[3:], *stats
    )


def layer(queries, key_rows, value_rows, out_weight, cotangent, offsets):
    rows, cols = queries.shape
    count = lax.axis_size("ctx")
    index = lax.axis_index("ctx")
    base = index * rows
    odd = (index % 2).astype(jnp.int32).reshape(1)
    me = lax.axis_index("head").astype(jnp.int32).reshape(1)

    def along(shard, by):
        return passed_along(shard, "ctx", by)

    def across(shard, bit):
        return swapped(shard, "head", bit)

    def pair(from_even, from_odd):
        return swapped(jnp.where(index % 2 == 0, from_even, from_odd), "ctx", 1)

    def ringed(shard, by, bit):
        groups = lax.axis_size("head")
        pairs = []
        for i in range(count):
            for h in range(groups):
                to = i - by if (h & 1) == bit else i + by
                here = i * groups + h
                pairs.append((here, to * groups + h if 0 <= to < count else here ^ 1))
        return lax.ppermute(shard, ("ctx", "head"), pairs)

    cot_far = across(cotangent, 2)
    cot_near = across(cotangent, 1)
    k2 = along(key_rows, 2)
    r1 = pair(key_rows, queries)
    v2 = along(value_rows, 2)
    cot_both = across(cot_far, 1)
    q2 = along(queries, -2)
    r2 = pair(value_rows, k2)

    g = grad_out_call(me, (cotangent, cot_near, cot_far, cot_both), out_weight)
    g2 = along(g, -2)
    bounds = jnp.stack([base, count * rows]).astype(jnp.int32)
    lo_col, lo_row = windows_call(bounds, offsets, rows)
    r3 = pair(q2, v2)
    g1 = pair(g2, g)

    attended, prob, stat, sent, kept, kept_far = attend_call(
        odd, me, lo_col, queries, key_rows, k2, value_rows, v2, r1, r2, r3, g, out_weight
    )
    stats = [stat] + [ringed(stat, n, bit) for n in (1, 2) for bit in (0, 1)]
    came = across(sent, 1)
    far = across((kept_far + came[:, cols:].astype(F32)).astype(BF16), 2)

    grad_queries, grad_keys, grad_values = grads_call(
        odd, me, lo_row, prob, attended, (key_rows, k2), (value_rows, v2), (queries, q2),
        (r1, r2, r3), (g, g1, g2), stats,
    )
    mixed = (kept + came[:, :cols].astype(F32) + far.astype(F32)).astype(BF16)
    return (mixed, grad_queries, grad_keys, grad_values)


def solution(mesh):
    in_specs = (
        P("ctx", "head"),
        P("ctx", "head"),
        P("ctx", "head"),
        P("head", None),
        P("ctx", "head"),
        P(),
    )
    out_specs = (P("ctx", "head"), P("ctx", "head"), P("ctx", "head"), P("ctx", "head"))
    return jax.shard_map(layer, mesh=mesh, in_specs=in_specs, out_specs=out_specs, check_vma=False)
```

```python
import functools
import math

import jax
import jax.numpy as jnp
from jax import lax
from jax.experimental import pallas as pl
from jax.experimental.pallas import tpu as pltpu
from jax.sharding import PartitionSpec as P


HD = 128
REACH = 2
PREV = 3
ROWS = 128
NEG_FILL = -1e30
SCALE = 1.0 / math.sqrt(HD)
LOG2E = 1.4426950408889634
VMEM_BYTES = 32 << 20
F32 = jnp.float32
BF16 = jnp.bfloat16


NT = (((1,), (1,)), ((), ()))
NN = (((1,), (0,)), ((), ()))


def passed_along(shard, axis, by):
    length = lax.axis_size(axis)
    pairs = [(i, i + by) for i in range(length) if 0 <= i + by < length]
    return lax.ppermute(shard, axis, pairs)


def swapped(shard, axis, bit):
    length = lax.axis_size(axis)
    return lax.ppermute(shard, axis, [(i, i ^ bit) for i in range(length)])


def windows_kernel(base_ref, offsets_ref, col_ref, row_ref):
    tiles, rows = row_ref.shape
    lines = tiles * rows // HD
    place = HD * lax.broadcasted_iota(jnp.int32, (lines, HD), 0) + lax.broadcasted_iota(
        jnp.int32, (lines, HD), 1
    )
    position = base_ref[0] + place

    def step(m, first):
        return jnp.where(offsets_ref[m + PREV] <= position, offsets_ref[m], first)

    first = lax.fori_loop(
        0, offsets_ref.shape[0] - PREV, step, jnp.zeros_like(position), unroll=4
    )
    first = jnp.where(position < base_ref[1], first - base_ref[0], tiles * rows)
    for line in range(lines):
        tile, start = divmod(line * HD, rows)
        row_ref[tile : tile + 1, start : start + HD] = first[line : line + 1, :]
        if tile == 0:
            spread = jnp.broadcast_to(first[line : line + 1, :], (HD, HD))
            col_ref[start : start + HD, :] = spread.T


def windows_call(base, offsets, rows):
    return pl.pallas_call(
        windows_kernel,
        name="windows",
        out_shape=(
            jax.ShapeDtypeStruct((rows, HD), jnp.int32),
            jax.ShapeDtypeStruct((REACH + 1, rows), jnp.int32),
        ),
        in_specs=[pl.BlockSpec(memory_space=pltpu.SMEM)] * 2,
        compiler_params=pltpu.CompilerParams(vmem_limit_bytes=VMEM_BYTES),
        cost_estimate=pl.CostEstimate(flops=1 << 20, bytes_accessed=1 << 18, transcendentals=0),
    )(base, offsets)


def in_hbm(*arrays):
    return [pltpu.with_memory_space_constraint(x, pltpu.HBM) for x in arrays]


def in_vmem(*arrays):
    return [pltpu.with_memory_space_constraint(x, pltpu.VMEM) for x in arrays]


def mm(a, b, dims):
    return lax.dot_general(a, b, dims, preferred_element_type=F32)


def payload_kernel(table, kinds, staged, odd_ref, me_ref, *refs):
    sources, outs, sems = refs[:kinds], refs[kinds : kinds + len(table)], refs[-1]
    seat = 2 * odd_ref[0] + (me_ref[0] & 1)
    if staged:
        stage, stage_sems = refs[-3], refs[-2]
        loads = [
            pltpu.make_async_copy(ref, stage.at[kind], stage_sems.at[kind])
            for kind, ref in enumerate(sources)
        ]
        for load in loads:
            load.start()
        for load in loads:
            load.wait()
        sources = [stage.at[kind] for kind in range(kinds)]
    for n, into in enumerate(outs):
        for kind in range(kinds):
            hits = [seat == place for place in range(4) if table[n][place] == kind]
            if hits:

                @pl.when(functools.reduce(jnp.logical_or, hits))
                def _():
                    pltpu.make_async_copy(sources[kind], into, sems.at[n]).start()

    for n, into in enumerate(outs):
        pltpu.make_async_copy(sources[0], into, sems.at[n]).wait()


def payload_call(odd, me, table, *arrays, staged=False):
    smem, anywhere = pl.BlockSpec(memory_space=pltpu.SMEM), pl.BlockSpec(memory_space=pl.ANY)
    shape = arrays[0].shape
    staging = []
    if staged:
        staging = [
            pltpu.VMEM((len(arrays),) + shape, BF16), pltpu.SemaphoreType.DMA((len(arrays),))
        ]
    return pl.pallas_call(
        functools.partial(payload_kernel, table, len(arrays), staged),
        name="payload",
        out_shape=(jax.ShapeDtypeStruct(shape, BF16),) * len(table),
        in_specs=[smem, smem] + [anywhere] * len(arrays),
        out_specs=(anywhere,) * len(table),
        scratch_shapes=staging + [pltpu.SemaphoreType.DMA((len(table),))],
        compiler_params=pltpu.CompilerParams(vmem_limit_bytes=2 << 20),
        cost_estimate=pl.CostEstimate(
            flops=0, bytes_accessed=4 * len(table) * shape[0] * shape[1], transcendentals=0
        ),
    )(odd, me, *arrays)


def grad_out_kernel(me_ref, c0, c1, c2, c3, w_ref, out_ref):
    cols = c0.shape[1]
    total = None
    for s, c in enumerate((c0, c1, c2, c3)):
        start = pl.multiple_of((me_ref[0] ^ s) * cols, cols)
        part = mm(c[...], w_ref[:, pl.ds(start, cols)], NT)
        total = part if total is None else total + part
    out_ref[...] = total.astype(BF16)


def grad_out_call(me, shards, weight):
    rows, cols = shards[0].shape
    whole = pl.BlockSpec((rows, cols), lambda h, me: (0, 0))
    return pl.pallas_call(
        grad_out_kernel,
        name="grad_out",
        out_shape=jax.ShapeDtypeStruct((rows, cols), BF16),
        grid_spec=pltpu.PrefetchScalarGridSpec(
            num_scalar_prefetch=1,
            grid=(cols // (2 * HD),),
            in_specs=[whole] * 4
            + [pl.BlockSpec((2 * HD, weight.shape[1]), lambda h, me: (h, 0))],
            out_specs=pl.BlockSpec((rows, 2 * HD), lambda h, me: (0, h)),
        ),
        compiler_params=pltpu.CompilerParams(vmem_limit_bytes=VMEM_BYTES),
        cost_estimate=pl.CostEstimate(
            flops=2 * rows * cols * weight.shape[1], bytes_accessed=6 << 20, transcendentals=0
        ),
    )(me, *in_hbm(shards[0]), *in_vmem(*shards[1:]), *in_hbm(weight))


def key_pieces(block, rows):
    first, last = block * ROWS, (block + 1) * ROWS
    return ((2, first, rows, -2 * rows), (1, 0, rows, -rows), (0, 0, last, 0))


def pick(odd, even_ref, odd_ref, into):
    into[...] = jnp.where(odd == 0, even_ref[...], odd_ref[...])


def attend_kernel(
    odd_ref, me_ref, lo_ref, q, k0, up, down, v0, v2, r1, r2, r3, g, w_ref,
    att_ref, prob_ref, stat_ref, sent_ref, mine_ref, far_ref, k1, v1, k2,
):
    rows = q.shape[0]
    head = pl.program_id(0)
    pick(me_ref[0] & 1, up, down, k2)
    pick(odd_ref[0], r2, r1, k1)
    pick(odd_ref[0], r3, r2, v1)
    keys, values = (k0, k1, k2), (v0, v1, v2)
    for b in range(rows // ROWS):
        mine = slice(b * ROWS, (b + 1) * ROWS)
        qb = q[mine, :]
        lo = lo_ref[mine, :]
        scores, places = [], []
        for tile, first, last, off in key_pieces(b, rows):
            raw = mm(qb, keys[tile][first:last, :], NT)
            for c in range(0, last - first, HD):
                part = raw[:, c : c + HD]
                pos = off + first + c + lax.broadcasted_iota(jnp.int32, part.shape, 1)
                ok = pos >= lo
                if tile == 0 and first + c == b * ROWS:
                    ok &= pos <= b * ROWS + lax.broadcasted_iota(jnp.int32, part.shape, 0)
                scores.append(jnp.where(ok, part, NEG_FILL))
                places.append(tile * rows + first + c)
        top = jnp.max(functools.reduce(jnp.maximum, scores), axis=1, keepdims=True)
        shift = jnp.broadcast_to(top * (SCALE * LOG2E), (ROWS, HD))
        exps = [jnp.exp2(s * (SCALE * LOG2E) - shift) for s in scores]
        total = jnp.sum(functools.reduce(jnp.add, exps), axis=1, keepdims=True)
        inverse = jnp.broadcast_to(1.0 / total, (ROWS, HD))
        mixed = None
        for e, place in zip(exps, places):
            prob_ref[0, mine, place : place + HD] = (e * inverse).astype(BF16)
        for tile, first, last, off in key_pieces(b, rows):
            prob = prob_ref[0, mine, tile * rows + first : tile * rows + last]
            part = mm(prob, values[tile][first:last, :], NN)
            mixed = part if mixed is None else mixed + part
        attended = mixed.astype(BF16)
        att_ref[mine, pl.ds(pl.multiple_of(head * HD, HD), HD)] = attended
        delta = jnp.sum(attended.astype(F32) * g[mine, :].astype(F32), axis=1, keepdims=True)
        log_total = shift + jnp.log2(total)
        lane = lax.broadcasted_iota(jnp.int32, (ROWS, ROWS), 1)
        stats = jnp.where(lane == 0, log_total, delta).T
        stat_ref[0, :, mine] = stats[0:2, :]

    @pl.when(head == pl.num_programs(0) - 1)
    def _():
        cols = att_ref.shape[1]

        def project(group):
            start = pl.multiple_of((me_ref[0] ^ group) * cols, cols)
            return mm(att_ref[...], w_ref[:, pl.ds(start, cols)], NN)

        sent_ref[:, 0:cols] = project(1).astype(BF16)
        sent_ref[:, cols : 2 * cols] = project(3).astype(BF16)
        far_ref[...] = project(2)
        mine_ref[...] = project(0)


def tile_specs(rows):
    tile = pl.BlockSpec((rows, HD), lambda h, odd, *_: (0, h))
    on_odd = pl.BlockSpec((rows, HD), lambda h, odd, *_: (0, h * odd[0]))
    on_even = pl.BlockSpec((rows, HD), lambda h, odd, *_: (0, h * (1 - odd[0])))
    return tile, on_odd, on_even


def attend_call(odd, me, lo, q, k0, up, down, v0, v2, r1, r2, r3, g, weight):
    rows, cols = q.shape
    heads = cols // HD
    tile, on_odd, on_even = tile_specs(rows)
    span = REACH * rows + ROWS
    whole = pl.BlockSpec((rows, cols), lambda h, odd, me: (0, 0))
    return pl.pallas_call(
        attend_kernel,
        name="attend",
        out_shape=(
            jax.ShapeDtypeStruct((rows, cols), BF16),
            jax.ShapeDtypeStruct((heads, rows, (REACH + 1) * rows), BF16),
            jax.ShapeDtypeStruct((heads, 2, rows), F32),
            jax.ShapeDtypeStruct((rows, 2 * cols), BF16),
            jax.ShapeDtypeStruct((rows, cols), F32),
            jax.ShapeDtypeStruct((rows, cols), F32),
        ),
        grid_spec=pltpu.PrefetchScalarGridSpec(
            num_scalar_prefetch=2,
            grid=(heads,),
            in_specs=[pl.BlockSpec((rows, HD), lambda h, odd, me: (0, 0))]
            + [tile] * 6
            + [on_odd, tile, on_even, tile]
            + [pl.BlockSpec(weight.shape, lambda h, odd, me: (0, 0))],
            out_specs=(
                whole,
                pl.BlockSpec((1, rows, (REACH + 1) * rows), lambda h, odd, me: (h, 0, 0)),
                pl.BlockSpec((1, 2, rows), lambda h, odd, me: (h, 0, 0)),
                pl.BlockSpec((rows, 2 * cols), lambda h, odd, me: (0, 0)),
                whole,
                whole,
            ),
            scratch_shapes=[pltpu.VMEM((rows, HD), BF16)] * 3,
        ),
        compiler_params=pltpu.CompilerParams(vmem_limit_bytes=VMEM_BYTES),
        cost_estimate=pl.CostEstimate(
            flops=8 * heads * rows * span * HD, bytes_accessed=12 << 20,
            transcendentals=heads * rows * span,
        ),
    )(odd, me, lo, *in_hbm(q, k0), *in_vmem(up, down), *in_hbm(v0), *in_vmem(v2, r1, r2, r3, g), *in_hbm(weight))


def grads_kernel(
    odd_ref, me_ref, lo_ref, prob_ref, att, k0, up, v0, v2, q0, down, r1, r2, r3, g0, g1, g2,
    s0, s10, s11, s20, s21, dq_ref, dk_ref, dv_ref,
    kc, qc, gc, v1, s1, s2, probs, grad_s, grad_q,
):
    rows = g0.shape[0]
    blocks = range(0, rows, ROWS)

    @pl.when(pl.program_id(0) == 0)
    def _():
        nothing = jnp.zeros((ROWS, ROWS), BF16)
        for early in blocks:
            for late in range(early + ROWS, rows, ROWS):
                far = 2 * rows
                for into in (probs, grad_s):
                    into[late : late + ROWS, early : early + ROWS] = nothing
                    into[early : early + ROWS, far + late : far + late + ROWS] = nothing
                grad_q[early : early + ROWS, late : late + ROWS] = nothing
                grad_q[late : late + ROWS, far + early : far + early + ROWS] = nothing

    odd, group = odd_ref[0], me_ref[0] & 1
    tiles = [slice(t * rows, (t + 1) * rows) for t in range(REACH + 1)]
    pick(odd, r2, r1, kc.at[tiles[1], :])
    pick(odd, r3, r2, v1)
    pick(odd, r1, r3, qc.at[tiles[1], :])
    pick(group, s10, s11, s1)
    pick(group, s20, s21, s2)
    pick(group, up, down, kc.at[tiles[2], :])
    pick(group, down, up, qc.at[tiles[2], :])
    for into, t, ref in (
        (kc, 0, k0), (qc, 0, q0), (gc, 0, g0), (gc, 1, g1), (gc, 2, g2)
    ):
        into[tiles[t], :] = ref[...]
    values, stats = (v0, v1, v2), (s0, s1, s2)

    for t in (0, 2, 1):
        for c in blocks:
            first, last = {0: (0, c + ROWS), 1: (0, rows), 2: (c, rows)}[t]
            at = t * rows + c
            asked = qc[at : at + ROWS, :]
            grad = gc[at : at + ROWS, :]
            raw = mm(k0[first:last, :], asked, NT)
            grad_prob = mm(values[0][first:last, :], grad, NT)
            lo = lo_ref[t : t + 1, c : c + ROWS]
            log_total = stats[t][0, 0:1, c : c + ROWS]
            delta = stats[t][0, 1:2, c : c + ROWS]
            for r in range(first, last, ROWS):
                here = slice(r - first, r - first + ROWS)
                part = raw[here, :]
                pos = r + lax.broadcasted_iota(jnp.int32, part.shape, 0)
                ok = pos >= lo
                if t == 0 and r == c:
                    ok &= pos <= c + lax.broadcasted_iota(jnp.int32, part.shape, 1)
                prob = jnp.where(ok, jnp.exp2(part * (SCALE * LOG2E) - log_total), 0.0)
                probs[r : r + ROWS, at : at + ROWS] = prob.astype(BF16)
                grad_s[r : r + ROWS, at : at + ROWS] = (
                    prob * (grad_prob[here, :] - delta)
                ).astype(BF16)
    dk_ref[...] = (mm(grad_s[...], qc[...], NN) * SCALE).astype(BF16)
    dv_ref[...] = mm(probs[...], gc[...], NN).astype(BF16)

    product = att[...].astype(F32) * g0[...].astype(F32)
    delta = jnp.broadcast_to(jnp.sum(product, axis=1, keepdims=True), (rows, HD))
    for t in (0, 2, 1):
        for c in blocks:
            first, last = {0: (c, rows), 1: (0, rows), 2: (0, c + ROWS)}[t]
            at = t * rows + c
            grad_prob = mm(g0[first:last, :], values[t][c : c + ROWS, :], NT)
            prob = prob_ref[0, first:last, at : at + ROWS].astype(F32)
            grad_q[first:last, at : at + ROWS] = (
                prob * (grad_prob - delta[first:last, :])
            ).astype(BF16)
    dq_ref[...] = (mm(grad_q[...], kc[...], NN) * SCALE).astype(BF16)


def grads_call(odd, me, lo, prob, att, k, v, q, received, grads, stats):
    rows, cols = q[0].shape
    heads = cols // HD
    tile, _, _ = tile_specs(rows)
    span = (REACH + 1) * rows
    stat = pl.BlockSpec((1, 2, rows), lambda h, odd, me: (h, 0, 0))
    hbm = in_hbm(k[0], v[0], q[0])
    vmem = in_vmem(k[1], v[1], q[1], *received, *grads)
    return pl.pallas_call(
        grads_kernel,
        name="grads",
        out_shape=(jax.ShapeDtypeStruct((rows, cols), BF16),) * 3,
        grid_spec=pltpu.PrefetchScalarGridSpec(
            num_scalar_prefetch=2,
            grid=(heads,),
            in_specs=[
                pl.BlockSpec((REACH + 1, rows), lambda h, odd, me: (0, 0)),
                pl.BlockSpec((1, rows, span), lambda h, odd, me: (h, 0, 0)),
            ]
            + [tile] * 13
            + [stat] * 5,
            out_specs=(tile,) * 3,
            scratch_shapes=[pltpu.VMEM((span, HD), BF16)] * 3
            + [pltpu.VMEM((rows, HD), BF16)]
            + [pltpu.VMEM((1, 2, rows), F32)] * 2
            + [pltpu.VMEM((rows, span), BF16)] * 3,
        ),
        compiler_params=pltpu.CompilerParams(vmem_limit_bytes=VMEM_BYTES),
        cost_estimate=pl.CostEstimate(
            flops=12 * heads * rows * span * HD, bytes_accessed=10 << 20,
            transcendentals=heads * rows * span,
        ),
    )(
        odd, me, lo, prob, att, hbm[0], vmem[0], hbm[1], vmem[1], hbm[2], vmem[2], *vmem[3:], *stats
    )


def layer(queries, key_rows, value_rows, out_weight, cotangent, offsets):
    rows, cols = queries.shape
    count = lax.axis_size("ctx")
    index = lax.axis_index("ctx")
    base = index * rows
    odd = (index % 2).astype(jnp.int32).reshape(1)
    me = lax.axis_index("head").astype(jnp.int32).reshape(1)

    def along(shard, by):
        return passed_along(shard, "ctx", by)

    def across(shard, bit):
        return swapped(shard, "head", bit)

    def exchanged(shard):
        return swapped(shard, "ctx", 1)

    def ringed(shard, by, bit):
        groups = lax.axis_size("head")
        pairs = []
        for i in range(count):
            for h in range(groups):
                to = i - by if (h & 1) == bit else i + by
                here = i * groups + h
                pairs.append((here, to * groups + h if 0 <= to < count else here ^ 1))
        return lax.ppermute(shard, ("ctx", "head"), pairs)

    cot_far = across(cotangent, 2)
    cot_near = across(cotangent, 1)
    side, up, down = payload_call(
        odd, me, ((0, 0, 1, 1), (0, 1, 0, 1), (1, 0, 1, 0)), *in_hbm(key_rows, queries),
        staged=True,
    )
    up = ringed(up, 2, 1)
    down = ringed(down, 2, 0)
    r1 = exchanged(side)
    v2 = along(value_rows, 2)
    cot_both = across(cot_far, 1)
    values = in_hbm(value_rows)
    r2 = exchanged(*payload_call(odd, me, ((0, 0, 1, 2),), *values, *in_vmem(up, down)))

    g = grad_out_call(me, (cotangent, cot_near, cot_far, cot_both), out_weight)
    g2 = along(g, -2)
    bounds = jnp.stack([base, count * rows]).astype(jnp.int32)
    lo_col, lo_row = windows_call(bounds, offsets, rows)
    r3 = exchanged(*payload_call(odd, me, ((1, 0, 2, 2),), *in_vmem(up, down, v2)))
    g1 = exchanged(*payload_call(odd, me, ((0, 0, 1, 1),), *in_vmem(g2, g)))

    attended, prob, stat, sent, kept, kept_far = attend_call(
        odd, me, lo_col, queries, key_rows, up, down, value_rows, v2, r1, r2, r3, g, out_weight
    )
    stats = [stat] + [ringed(stat, n, bit) for n in (1, 2) for bit in (0, 1)]
    came = across(sent, 1)
    far = across((kept_far + came[:, cols:].astype(F32)).astype(BF16), 2)

    grad_queries, grad_keys, grad_values = grads_call(
        odd, me, lo_row, prob, attended, (key_rows, up), (value_rows, v2), (queries, down),
        (r1, r2, r3), (g, g1, g2), stats,
    )
    mixed = (kept + came[:, :cols].astype(F32) + far.astype(F32)).astype(BF16)
    return (mixed, grad_queries, grad_keys, grad_values)


def solution(mesh):
    in_specs = (
        P("ctx", "head"),
        P("ctx", "head"),
        P("ctx", "head"),
        P("head", None),
        P("ctx", "head"),
        P(),
    )
    out_specs = (P("ctx", "head"), P("ctx", "head"), P("ctx", "head"), P("ctx", "head"))
    return jax.shard_map(layer, mesh=mesh, in_specs=in_specs, out_specs=out_specs, check_vma=False)
```

```python
import functools
import math

import jax
import jax.numpy as jnp
from jax import lax
from jax.experimental import pallas as pl
from jax.experimental.pallas import tpu as pltpu
from jax.sharding import PartitionSpec as P


HD = 128
REACH = 2
PREV = 3
ROWS = 128
NEG_FILL = -1e30
SCALE = 1.0 / math.sqrt(HD)
LOG2E = 1.4426950408889634
VMEM_BYTES = 32 << 20
F32 = jnp.float32
BF16 = jnp.bfloat16


NT = (((1,), (1,)), ((), ()))
NN = (((1,), (0,)), ((), ()))


def passed_along(shard, axis, by):
    length = lax.axis_size(axis)
    pairs = [(i, i + by) for i in range(length) if 0 <= i + by < length]
    return lax.ppermute(shard, axis, pairs)


def swapped(shard, axis, bit):
    length = lax.axis_size(axis)
    return lax.ppermute(shard, axis, [(i, i ^ bit) for i in range(length)])


def windows_kernel(base_ref, offsets_ref, col_ref, row_ref):
    tiles, rows = row_ref.shape
    lines = tiles * rows // HD
    place = HD * lax.broadcasted_iota(jnp.int32, (lines, HD), 0) + lax.broadcasted_iota(
        jnp.int32, (lines, HD), 1
    )
    position = base_ref[0] + place

    def step(m, first):
        return jnp.where(offsets_ref[m + PREV] <= position, offsets_ref[m], first)

    first = lax.fori_loop(
        0, offsets_ref.shape[0] - PREV, step, jnp.zeros_like(position), unroll=4
    )
    first = jnp.where(position < base_ref[1], first - base_ref[0], tiles * rows)
    for line in range(lines):
        tile, start = divmod(line * HD, rows)
        row_ref[tile : tile + 1, start : start + HD] = first[line : line + 1, :]
        if tile == 0:
            spread = jnp.broadcast_to(first[line : line + 1, :], (HD, HD))
            col_ref[start : start + HD, :] = spread.T


def windows_call(base, offsets, rows):
    return pl.pallas_call(
        windows_kernel,
        name="windows",
        out_shape=(
            jax.ShapeDtypeStruct((rows, HD), jnp.int32),
            jax.ShapeDtypeStruct((REACH + 1, rows), jnp.int32),
        ),
        in_specs=[pl.BlockSpec(memory_space=pltpu.SMEM)] * 2,
        compiler_params=pltpu.CompilerParams(vmem_limit_bytes=VMEM_BYTES),
        cost_estimate=pl.CostEstimate(flops=1 << 20, bytes_accessed=1 << 18, transcendentals=0),
    )(base, offsets)


def in_hbm(*arrays):
    return [pltpu.with_memory_space_constraint(x, pltpu.HBM) for x in arrays]


def in_vmem(*arrays):
    return [pltpu.with_memory_space_constraint(x, pltpu.VMEM) for x in arrays]


def mm(a, b, dims):
    return lax.dot_general(a, b, dims, preferred_element_type=F32)


def payload_kernel(table, kinds, staged, odd_ref, me_ref, *refs):
    sources, outs, sems = refs[:kinds], refs[kinds : kinds + len(table)], refs[-1]
    seat = 2 * odd_ref[0] + (me_ref[0] & 1)
    if staged:
        stage, stage_sems = refs[-3], refs[-2]
        loads = [
            pltpu.make_async_copy(ref, stage.at[kind], stage_sems.at[kind])
            for kind, ref in enumerate(sources)
        ]
        for load in loads:
            load.start()
        for load in loads:
            load.wait()
        sources = [stage.at[kind] for kind in range(kinds)]
    for n, into in enumerate(outs):
        for kind in range(kinds):
            hits = [seat == place for place in range(4) if table[n][place] == kind]
            if hits:

                @pl.when(functools.reduce(jnp.logical_or, hits))
                def _():
                    pltpu.make_async_copy(sources[kind], into, sems.at[n]).start()

    for n, into in enumerate(outs):
        pltpu.make_async_copy(sources[0], into, sems.at[n]).wait()


def payload_call(odd, me, table, *arrays, staged=False):
    smem, anywhere = pl.BlockSpec(memory_space=pltpu.SMEM), pl.BlockSpec(memory_space=pl.ANY)
    shape = arrays[0].shape
    staging = []
    if staged:
        staging = [
            pltpu.VMEM((len(arrays),) + shape, BF16), pltpu.SemaphoreType.DMA((len(arrays),))
        ]
    return pl.pallas_call(
        functools.partial(payload_kernel, table, len(arrays), staged),
        name="payload",
        out_shape=(jax.ShapeDtypeStruct(shape, BF16),) * len(table),
        in_specs=[smem, smem] + [anywhere] * len(arrays),
        out_specs=(anywhere,) * len(table),
        scratch_shapes=staging + [pltpu.SemaphoreType.DMA((len(table),))],
        compiler_params=pltpu.CompilerParams(vmem_limit_bytes=2 << 20),
        cost_estimate=pl.CostEstimate(
            flops=0, bytes_accessed=4 * len(table) * shape[0] * shape[1], transcendentals=0
        ),
    )(odd, me, *arrays)


def grad_out_kernel(me_ref, c0, c1, c2, c3, w_ref, out_ref):
    cols = c0.shape[1]
    total = None
    for s, c in enumerate((c0, c1, c2, c3)):
        start = pl.multiple_of((me_ref[0] ^ s) * cols, cols)
        part = mm(c[...], w_ref[:, pl.ds(start, cols)], NT)
        total = part if total is None else total + part
    out_ref[...] = total.astype(BF16)


def grad_out_call(me, shards, weight):
    rows, cols = shards[0].shape
    whole = pl.BlockSpec((rows, cols), lambda h, me: (0, 0))
    return pl.pallas_call(
        grad_out_kernel,
        name="grad_out",
        out_shape=jax.ShapeDtypeStruct((rows, cols), BF16),
        grid_spec=pltpu.PrefetchScalarGridSpec(
            num_scalar_prefetch=1,
            grid=(cols // (2 * HD),),
            in_specs=[whole] * 4
            + [pl.BlockSpec((2 * HD, weight.shape[1]), lambda h, me: (h, 0))],
            out_specs=pl.BlockSpec((rows, 2 * HD), lambda h, me: (0, h)),
        ),
        compiler_params=pltpu.CompilerParams(vmem_limit_bytes=VMEM_BYTES),
        cost_estimate=pl.CostEstimate(
            flops=2 * rows * cols * weight.shape[1], bytes_accessed=6 << 20, transcendentals=0
        ),
    )(me, *in_hbm(shards[0]), *in_vmem(*shards[1:]), *in_hbm(weight))


def pick(odd, even_ref, odd_ref, into):
    into[...] = jnp.where(odd == 0, even_ref[...], odd_ref[...])


def spread(column):
    return jnp.broadcast_to(column, (column.shape[0], HD))


def near_kernel(
    me_ref, lo_ref, q, k0, up, down, v0, v2, prob_ref, top_ref, total_ref, sum_ref, k2
):
    rows = q.shape[0]
    blocks = range(0, rows, ROWS)
    pick(me_ref[0] & 1, up, down, k2)
    own = [mm(q[c:rows, :], k0[c : c + ROWS, :], NT) for c in blocks]
    far = [mm(q[0 : c + ROWS, :], k2[c : c + ROWS, :], NT) for c in blocks]
    for b in blocks:
        mine = slice(b, b + ROWS)
        lo = lo_ref[mine, :]
        scores = []
        for c in blocks:
            lane = lax.broadcasted_iota(jnp.int32, (ROWS, HD), 1)
            if c <= b:
                ok = lane + c >= lo
                if c == b:
                    ok &= lane <= lax.broadcasted_iota(jnp.int32, (ROWS, HD), 0)
                part = own[c // ROWS][b - c : b - c + ROWS, :]
                scores.append((c, jnp.where(ok, part, NEG_FILL)))
            if c >= b:
                ok = lane + (c - REACH * rows) >= lo
                part = far[c // ROWS][mine, :]
                scores.append((rows + c, jnp.where(ok, part, NEG_FILL)))
        top = jnp.max(functools.reduce(jnp.maximum, [x for _, x in scores]), axis=1, keepdims=True)
        shift = spread(top * (SCALE * LOG2E))
        exps = [jnp.exp2(x * (SCALE * LOG2E) - shift) for _, x in scores]
        total = jnp.sum(functools.reduce(jnp.add, exps), axis=1, keepdims=True)
        for (place, _), e in zip(scores, exps):
            prob_ref[0, mine, place : place + HD] = e.astype(BF16)
        sum_ref[mine, :] = mm(prob_ref[0, mine, 0 : b + ROWS], v0[0 : b + ROWS, :], NN) + mm(
            prob_ref[0, mine, rows + b : 2 * rows], v2[b:rows, :], NN
        )
        top_ref[mine, :] = shift
        total_ref[mine, :] = spread(total)


def near_call(me, lo, q, k0, up, down, v0, v2):
    rows, cols = q.shape
    heads = cols // HD
    tile = pl.BlockSpec((rows, HD), lambda h, me: (0, h))
    return pl.pallas_call(
        near_kernel,
        name="near",
        out_shape=(jax.ShapeDtypeStruct((heads, rows, 2 * rows), BF16),)
        + (jax.ShapeDtypeStruct((rows, cols), F32),) * 3,
        grid_spec=pltpu.PrefetchScalarGridSpec(
            num_scalar_prefetch=1,
            grid=(heads,),
            in_specs=[pl.BlockSpec((rows, HD), lambda h, me: (0, 0))] + [tile] * 6,
            out_specs=(pl.BlockSpec((1, rows, 2 * rows), lambda h, me: (h, 0, 0)),) + (tile,) * 3,
            scratch_shapes=[pltpu.VMEM((rows, HD), BF16)],
        ),
        compiler_params=pltpu.CompilerParams(vmem_limit_bytes=VMEM_BYTES),
        cost_estimate=pl.CostEstimate(
            flops=16 * heads * rows * rows * HD, bytes_accessed=10 << 20,
            transcendentals=2 * heads * rows * rows,
        ),
    )(me, lo, *in_hbm(q, k0), *in_vmem(up, down), *in_hbm(v0), *in_vmem(v2))


def attend_kernel(
    odd_ref, me_ref, lo_ref, q, r1, r2, r3, g, near_top, near_total, near_sum, w_ref,
    att_ref, prob_ref, factor_ref, stat_ref, sent_ref, mine_ref, far_ref, k1, v1,
):
    rows = q.shape[0]
    head = pl.program_id(0)
    pick(odd_ref[0], r2, r1, k1)
    pick(odd_ref[0], r3, r2, v1)
    raw = mm(q[...], k1[...], NT)
    for b in range(0, rows, ROWS):
        mine = slice(b, b + ROWS)
        lo = lo_ref[mine, :]
        scores = []
        for c in range(0, rows, ROWS):
            lane = lax.broadcasted_iota(jnp.int32, (ROWS, HD), 1)
            scores.append(jnp.where(lane + (c - rows) >= lo, raw[mine, c : c + HD], NEG_FILL))
        top = jnp.max(functools.reduce(jnp.maximum, scores), axis=1, keepdims=True)
        shift = jnp.maximum(spread(top * (SCALE * LOG2E)), near_top[mine, :])
        exps = [jnp.exp2(s * (SCALE * LOG2E) - shift) for s in scores]
        rescale = jnp.exp2(near_top[mine, :] - shift)
        total = rescale * near_total[mine, :] + spread(
            jnp.sum(functools.reduce(jnp.add, exps), axis=1, keepdims=True)
        )
        inverse = 1.0 / total
        factor = rescale * inverse
        for n, e in enumerate(exps):
            prob_ref[0, mine, n * HD : (n + 1) * HD] = (e * inverse).astype(BF16)
        attended = (near_sum[mine, :] * factor + mm(prob_ref[0, mine, :], v1[...], NN)).astype(BF16)
        att_ref[mine, pl.ds(pl.multiple_of(head * HD, HD), HD)] = attended
        factor_ref[mine, :] = factor
        delta = jnp.sum(attended.astype(F32) * g[mine, :].astype(F32), axis=1, keepdims=True)
        log_total = shift + jnp.log2(total)
        lane = lax.broadcasted_iota(jnp.int32, (ROWS, ROWS), 1)
        stats = jnp.where(lane == 0, log_total, delta).T
        stat_ref[0, :, mine] = stats[0:2, :]

    @pl.when(head == pl.num_programs(0) - 1)
    def _():
        cols = att_ref.shape[1]

        def project(group):
            start = pl.multiple_of((me_ref[0] ^ group) * cols, cols)
            return mm(att_ref[...], w_ref[:, pl.ds(start, cols)], NN)

        sent_ref[:, 0:cols] = project(1).astype(BF16)
        sent_ref[:, cols : 2 * cols] = project(3).astype(BF16)
        far_ref[...] = project(2)
        mine_ref[...] = project(0)


def tile_specs(rows):
    tile = pl.BlockSpec((rows, HD), lambda h, odd, *_: (0, h))
    on_odd = pl.BlockSpec((rows, HD), lambda h, odd, *_: (0, h * odd[0]))
    on_even = pl.BlockSpec((rows, HD), lambda h, odd, *_: (0, h * (1 - odd[0])))
    return tile, on_odd, on_even


def attend_call(odd, me, lo, q, r1, r2, r3, g, near, weight):
    rows, cols = q.shape
    heads = cols // HD
    tile, on_odd, on_even = tile_specs(rows)
    whole = pl.BlockSpec((rows, cols), lambda h, odd, me: (0, 0))
    return pl.pallas_call(
        attend_kernel,
        name="attend",
        out_shape=(
            jax.ShapeDtypeStruct((rows, cols), BF16),
            jax.ShapeDtypeStruct((heads, rows, rows), BF16),
            jax.ShapeDtypeStruct((rows, cols), F32),
            jax.ShapeDtypeStruct((heads, 2, rows), F32),
            jax.ShapeDtypeStruct((rows, 2 * cols), BF16),
            jax.ShapeDtypeStruct((rows, cols), F32),
            jax.ShapeDtypeStruct((rows, cols), F32),
        ),
        grid_spec=pltpu.PrefetchScalarGridSpec(
            num_scalar_prefetch=2,
            grid=(heads,),
            in_specs=[pl.BlockSpec((rows, HD), lambda h, odd, me: (0, 0))]
            + [tile, on_odd, tile, on_even, tile, tile, tile, tile]
            + [pl.BlockSpec(weight.shape, lambda h, odd, me: (0, 0))],
            out_specs=(
                whole,
                pl.BlockSpec((1, rows, rows), lambda h, odd, me: (h, 0, 0)),
                tile,
                pl.BlockSpec((1, 2, rows), lambda h, odd, me: (h, 0, 0)),
                pl.BlockSpec((rows, 2 * cols), lambda h, odd, me: (0, 0)),
                whole,
                whole,
            ),
            scratch_shapes=[pltpu.VMEM((rows, HD), BF16)] * 2,
        ),
        compiler_params=pltpu.CompilerParams(vmem_limit_bytes=VMEM_BYTES),
        cost_estimate=pl.CostEstimate(
            flops=8 * heads * rows * rows * HD, bytes_accessed=12 << 20,
            transcendentals=heads * rows * rows,
        ),
    )(odd, me, lo, *in_hbm(q), *in_vmem(r1, r2, r3, g), *near, *in_vmem(weight))


def grads_kernel(
    odd_ref, me_ref, lo_ref, near_ref, prob_ref, factor_ref, att, k0, up, v0, v2, q0, down, r1, r2, r3, g0, g1, g2,
    s0, s10, s11, s20, s21, dq_ref, dk_ref, dv_ref,
    kc, qc, gc, v1, s1, s2, probs, grad_s, grad_q,
):
    rows = g0.shape[0]
    blocks = range(0, rows, ROWS)

    @pl.when(pl.program_id(0) == 0)
    def _():
        nothing = jnp.zeros((ROWS, ROWS), BF16)
        for early in blocks:
            for late in range(early + ROWS, rows, ROWS):
                far = 2 * rows
                for into in (probs, grad_s):
                    into[late : late + ROWS, early : early + ROWS] = nothing
                    into[early : early + ROWS, far + late : far + late + ROWS] = nothing
                grad_q[early : early + ROWS, late : late + ROWS] = nothing
                grad_q[late : late + ROWS, rows + early : rows + early + ROWS] = nothing

    odd, group = odd_ref[0], me_ref[0] & 1
    tiles = [slice(t * rows, (t + 1) * rows) for t in range(REACH + 1)]
    pick(odd, r2, r1, kc.at[tiles[2], :])
    pick(odd, r3, r2, v1)
    pick(odd, r1, r3, qc.at[tiles[1], :])
    pick(group, s10, s11, s1)
    pick(group, s20, s21, s2)
    pick(group, up, down, kc.at[tiles[1], :])
    pick(group, down, up, qc.at[tiles[2], :])
    for into, t, ref in (
        (kc, 0, k0), (qc, 0, q0), (gc, 0, g0), (gc, 1, g1), (gc, 2, g2)
    ):
        into[tiles[t], :] = ref[...]
    values, stats = (v0, v1, v2), (s0, s1, s2)

    for t in (0, 2, 1):
        for c in blocks:
            first, last = {0: (0, c + ROWS), 1: (0, rows), 2: (c, rows)}[t]
            at = t * rows + c
            asked = qc[at : at + ROWS, :]
            grad = gc[at : at + ROWS, :]
            raw = mm(k0[first:last, :], asked, NT)
            grad_prob = mm(values[0][first:last, :], grad, NT)
            lo = lo_ref[t : t + 1, c : c + ROWS]
            log_total = stats[t][0, 0:1, c : c + ROWS]
            delta = stats[t][0, 1:2, c : c + ROWS]
            for r in range(first, last, ROWS):
                here = slice(r - first, r - first + ROWS)
                part = raw[here, :]
                pos = r + lax.broadcasted_iota(jnp.int32, part.shape, 0)
                ok = pos >= lo
                if t == 0 and r == c:
                    ok &= pos <= c + lax.broadcasted_iota(jnp.int32, part.shape, 1)
                prob = jnp.where(ok, jnp.exp2(part * (SCALE * LOG2E) - log_total), 0.0)
                probs[r : r + ROWS, at : at + ROWS] = prob.astype(BF16)
                grad_s[r : r + ROWS, at : at + ROWS] = (
                    prob * (grad_prob[here, :] - delta)
                ).astype(BF16)
    dk_ref[...] = (mm(grad_s[...], qc[...], NN) * SCALE).astype(BF16)
    dv_ref[...] = mm(probs[...], gc[...], NN).astype(BF16)

    product = att[...].astype(F32) * g0[...].astype(F32)
    delta = jnp.broadcast_to(jnp.sum(product, axis=1, keepdims=True), (rows, HD))
    for t in (0, 2, 1):
        for c in blocks:
            first, last = {0: (c, rows), 1: (0, rows), 2: (0, c + ROWS)}[t]
            grad_prob = mm(g0[first:last, :], values[t][c : c + ROWS, :], NT)
            into = {0: 0, 2: rows, 1: 2 * rows}[t] + c
            if t == 1:
                prob = prob_ref[0, first:last, c : c + ROWS].astype(F32)
            else:
                prob = near_ref[0, first:last, into : into + ROWS].astype(F32)
            grad_q[first:last, into : into + ROWS] = (
                prob * (grad_prob - delta[first:last, :])
            ).astype(BF16)
    near = mm(grad_q[:, 0 : 2 * rows], kc[0 : 2 * rows, :], NN)
    last = mm(grad_q[:, 2 * rows :], kc[2 * rows :, :], NN)
    dq_ref[...] = ((near * factor_ref[...] + last) * SCALE).astype(BF16)


def grads_call(odd, me, lo, near, prob, factor, att, k, v, q, received, grads, stats):
    rows, cols = q[0].shape
    heads = cols // HD
    tile, _, _ = tile_specs(rows)
    span = (REACH + 1) * rows
    stat = pl.BlockSpec((1, 2, rows), lambda h, odd, me: (h, 0, 0))
    hbm = in_hbm(k[0], v[0], q[0])
    vmem = in_vmem(k[1], v[1], q[1], *received, *grads)
    return pl.pallas_call(
        grads_kernel,
        name="grads",
        out_shape=(jax.ShapeDtypeStruct((rows, cols), BF16),) * 3,
        grid_spec=pltpu.PrefetchScalarGridSpec(
            num_scalar_prefetch=2,
            grid=(heads,),
            in_specs=[
                pl.BlockSpec((REACH + 1, rows), lambda h, odd, me: (0, 0)),
                pl.BlockSpec((1, rows, 2 * rows), lambda h, odd, me: (h, 0, 0)),
                pl.BlockSpec((1, rows, rows), lambda h, odd, me: (h, 0, 0)),
                tile,
            ]
            + [tile] * 13
            + [stat] * 5,
            out_specs=(tile,) * 3,
            scratch_shapes=[pltpu.VMEM((span, HD), BF16)] * 3
            + [pltpu.VMEM((rows, HD), BF16)]
            + [pltpu.VMEM((1, 2, rows), F32)] * 2
            + [pltpu.VMEM((rows, span), BF16)] * 3,
        ),
        compiler_params=pltpu.CompilerParams(vmem_limit_bytes=VMEM_BYTES),
        cost_estimate=pl.CostEstimate(
            flops=12 * heads * rows * span * HD, bytes_accessed=10 << 20,
            transcendentals=heads * rows * span,
        ),
    )(
        odd, me, lo, near, prob, factor, att, hbm[0], vmem[0], hbm[1], vmem[1], hbm[2], vmem[2], *vmem[3:], *stats
    )


def layer(queries, key_rows, value_rows, out_weight, cotangent, offsets):
    rows, cols = queries.shape
    count = lax.axis_size("ctx")
    index = lax.axis_index("ctx")
    base = index * rows
    odd = (index % 2).astype(jnp.int32).reshape(1)
    me = lax.axis_index("head").astype(jnp.int32).reshape(1)

    def along(shard, by):
        return passed_along(shard, "ctx", by)

    def across(shard, bit):
        return swapped(shard, "head", bit)

    def exchanged(shard):
        return swapped(shard, "ctx", 1)

    def ringed(shard, by, bit):
        groups = lax.axis_size("head")
        pairs = []
        for i in range(count):
            for h in range(groups):
                to = i - by if (h & 1) == bit else i + by
                here = i * groups + h
                pairs.append((here, to * groups + h if 0 <= to < count else here ^ 1))
        return lax.ppermute(shard, ("ctx", "head"), pairs)

    cot_far = across(cotangent, 2)
    cot_near = across(cotangent, 1)
    side, up, down = payload_call(
        odd, me, ((0, 0, 1, 1), (0, 1, 0, 1), (1, 0, 1, 0)), *in_hbm(key_rows, queries),
        staged=True,
    )
    up = ringed(up, 2, 1)
    down = ringed(down, 2, 0)
    r1 = exchanged(side)
    v2 = along(value_rows, 2)
    cot_both = across(cot_far, 1)
    values = in_hbm(value_rows)
    r2 = exchanged(*payload_call(odd, me, ((0, 0, 1, 2),), *values, *in_vmem(up, down)))

    g = grad_out_call(me, (cotangent, cot_near, cot_far, cot_both), out_weight)
    g2 = along(g, -2)
    bounds = jnp.stack([base, count * rows]).astype(jnp.int32)
    lo_col, lo_row = windows_call(bounds, offsets, rows)
    r3 = exchanged(*payload_call(odd, me, ((1, 0, 2, 2),), *in_vmem(up, down, v2)))
    g1 = exchanged(*payload_call(odd, me, ((0, 0, 1, 1),), *in_vmem(g2, g)))

    near, *near_rows = near_call(
        me, lo_col, queries, key_rows, up, down, value_rows, v2
    )
    attended, prob, factor, stat, sent, kept, kept_far = attend_call(
        odd, me, lo_col, queries, r1, r2, r3, g, near_rows, out_weight
    )
    stats = [stat] + [ringed(stat, n, bit) for n in (1, 2) for bit in (0, 1)]
    came = across(sent, 1)
    far = across((kept_far + came[:, cols:].astype(F32)).astype(BF16), 2)

    grad_queries, grad_keys, grad_values = grads_call(
        odd, me, lo_row, near, prob, factor, attended, (key_rows, up), (value_rows, v2), (queries, down),
        (r1, r2, r3), (g, g1, g2), stats,
    )
    mixed = (kept + came[:, :cols].astype(F32) + far.astype(F32)).astype(BF16)
    return (mixed, grad_queries, grad_keys, grad_values)


def solution(mesh):
    in_specs = (
        P("ctx", "head"),
        P("ctx", "head"),
        P("ctx", "head"),
        P("head", None),
        P("ctx", "head"),
        P(),
    )
    out_specs = (P("ctx", "head"), P("ctx", "head"), P("ctx", "head"), P("ctx", "head"))
    return jax.shard_map(layer, mesh=mesh, in_specs=in_specs, out_specs=out_specs, check_vma=False)
```

```python
import functools
import math

import jax
import jax.numpy as jnp
from jax import lax
from jax.experimental import pallas as pl
from jax.experimental.pallas import tpu as pltpu
from jax.sharding import PartitionSpec as P


HD = 128
REACH = 2
PREV = 3
ROWS = 128
NEG_FILL = -1e30
SCALE = 1.0 / math.sqrt(HD)
LOG2E = 1.4426950408889634
VMEM_BYTES = 32 << 20
F32 = jnp.float32
BF16 = jnp.bfloat16


NT = (((1,), (1,)), ((), ()))
NN = (((1,), (0,)), ((), ()))


def passed_along(shard, axis, by):
    length = lax.axis_size(axis)
    pairs = [(i, i + by) for i in range(length) if 0 <= i + by < length]
    return lax.ppermute(shard, axis, pairs)


def swapped(shard, axis, bit):
    length = lax.axis_size(axis)
    return lax.ppermute(shard, axis, [(i, i ^ bit) for i in range(length)])


RESIDENT = pl.BlockSpec(memory_space=pltpu.VMEM)


def windows_kernel(base_ref, offsets_ref, col_ref, row_ref):
    tiles, rows = row_ref.shape
    lines = tiles * rows // HD
    place = HD * lax.broadcasted_iota(jnp.int32, (lines, HD), 0) + lax.broadcasted_iota(
        jnp.int32, (lines, HD), 1
    )
    position = base_ref[0] + place

    def step(m, first):
        return jnp.where(offsets_ref[m + PREV] <= position, offsets_ref[m], first)

    first = lax.fori_loop(
        0, offsets_ref.shape[0] - PREV, step, jnp.zeros_like(position), unroll=4
    )
    first = jnp.where(position < base_ref[1], first - base_ref[0], tiles * rows)
    for line in range(lines):
        tile, start = divmod(line * HD, rows)
        row_ref[tile : tile + 1, start : start + HD] = first[line : line + 1, :]
        if tile == 0:
            spread = jnp.broadcast_to(first[line : line + 1, :], (HD, HD))
            col_ref[start : start + HD, :] = spread.T


def windows_call(base, offsets, rows):
    return pl.pallas_call(
        windows_kernel,
        name="windows",
        out_shape=(
            jax.ShapeDtypeStruct((rows, HD), jnp.int32),
            jax.ShapeDtypeStruct((REACH + 1, rows), jnp.int32),
        ),
        in_specs=[pl.BlockSpec(memory_space=pltpu.SMEM)] * 2,
        compiler_params=pltpu.CompilerParams(vmem_limit_bytes=VMEM_BYTES),
        cost_estimate=pl.CostEstimate(flops=1 << 20, bytes_accessed=1 << 18, transcendentals=0),
    )(base, offsets)


def in_hbm(*arrays):
    return [pltpu.with_memory_space_constraint(x, pltpu.HBM) for x in arrays]


def in_vmem(*arrays):
    return [pltpu.with_memory_space_constraint(x, pltpu.VMEM) for x in arrays]


def mm(a, b, dims):
    return lax.dot_general(a, b, dims, preferred_element_type=F32)


def payload_kernel(table, kinds, odd_ref, me_ref, *refs):
    sources, outs, sems = refs[:kinds], refs[kinds : kinds + len(table)], refs[-1]
    seat = 2 * odd_ref[0] + (me_ref[0] & 1)
    for n, into in enumerate(outs):
        for kind in range(kinds):
            hits = [seat == place for place in range(4) if table[n][place] == kind]
            if hits:

                @pl.when(functools.reduce(jnp.logical_or, hits))
                def _():
                    pltpu.make_async_copy(sources[kind], into, sems.at[n]).start()

    for n, into in enumerate(outs):
        pltpu.make_async_copy(sources[0], into, sems.at[n]).wait()


def payload_call(odd, me, table, *arrays):
    smem, anywhere = pl.BlockSpec(memory_space=pltpu.SMEM), pl.BlockSpec(memory_space=pl.ANY)
    shape = arrays[0].shape
    return pl.pallas_call(
        functools.partial(payload_kernel, table, len(arrays)),
        name="payload",
        out_shape=(jax.ShapeDtypeStruct(shape, BF16),) * len(table),
        in_specs=[smem, smem] + [anywhere] * len(arrays),
        out_specs=(anywhere,) * len(table),
        scratch_shapes=[pltpu.SemaphoreType.DMA((len(table),))],
        compiler_params=pltpu.CompilerParams(vmem_limit_bytes=1 << 20),
        cost_estimate=pl.CostEstimate(
            flops=0, bytes_accessed=4 * len(table) * shape[0] * shape[1], transcendentals=0
        ),
    )(odd, me, *arrays)


def grad_out_kernel(me_ref, c0, c1, c2, c3, w_ref, out_ref):
    cols = c0.shape[1]
    total = None
    for s, c in enumerate((c0, c1, c2, c3)):
        start = pl.multiple_of((me_ref[0] ^ s) * cols, cols)
        part = mm(c[...], w_ref[:, pl.ds(start, cols)], NT)
        total = part if total is None else total + part
    out_ref[...] = total.astype(BF16)


def grad_out_call(me, shards, weight):
    rows, cols = shards[0].shape
    whole = pl.BlockSpec((rows, cols), lambda h, me: (0, 0))
    return pl.pallas_call(
        grad_out_kernel,
        name="grad_out",
        out_shape=jax.ShapeDtypeStruct((rows, cols), BF16),
        grid_spec=pltpu.PrefetchScalarGridSpec(
            num_scalar_prefetch=1,
            grid=(cols // (2 * HD),),
            in_specs=[whole] + [RESIDENT] * 3
            + [pl.BlockSpec((2 * HD, weight.shape[1]), lambda h, me: (h, 0))],
            out_specs=pl.BlockSpec((rows, 2 * HD), lambda h, me: (0, h)),
        ),
        compiler_params=pltpu.CompilerParams(vmem_limit_bytes=VMEM_BYTES),
        cost_estimate=pl.CostEstimate(
            flops=2 * rows * cols * weight.shape[1], bytes_accessed=6 << 20, transcendentals=0
        ),
    )(me, *in_hbm(shards[0]), *in_vmem(*shards[1:]), *in_hbm(weight))


def pick(odd, even_ref, odd_ref, into):
    into[...] = jnp.where(odd == 0, even_ref[...], odd_ref[...])


def head_cols():
    return pl.ds(pl.multiple_of(pl.program_id(0) * HD, HD), HD)


def spread(column):
    return jnp.broadcast_to(column, (column.shape[0], HD))


def near_kernel(
    me_ref, lo_ref, q, k0, up, down, v0, v2, prob_ref, top_ref, total_ref, sum_ref, k2
):
    rows = q.shape[0]
    blocks = range(0, rows, ROWS)
    cols = head_cols()
    head = pl.program_id(0)
    up, down, v2 = up.at[:, cols], down.at[:, cols], v2.at[:, cols]
    top_ref, total_ref, sum_ref = (x.at[:, cols] for x in (top_ref, total_ref, sum_ref))
    prob_ref = prob_ref.at[head]
    pick(me_ref[0] & 1, up, down, k2)
    own = [mm(q[c:rows, :], k0[c : c + ROWS, :], NT) for c in blocks]
    far = [mm(q[0 : c + ROWS, :], k2[c : c + ROWS, :], NT) for c in blocks]
    for b in blocks:
        mine = slice(b, b + ROWS)
        lo = lo_ref[mine, :]
        scores = []
        for c in blocks:
            lane = lax.broadcasted_iota(jnp.int32, (ROWS, HD), 1)
            if c <= b:
                ok = lane + c >= lo
                if c == b:
                    ok &= lane <= lax.broadcasted_iota(jnp.int32, (ROWS, HD), 0)
                part = own[c // ROWS][b - c : b - c + ROWS, :]
                scores.append((c, jnp.where(ok, part, NEG_FILL)))
            if c >= b:
                ok = lane + (c - REACH * rows) >= lo
                part = far[c // ROWS][mine, :]
                scores.append((rows + c, jnp.where(ok, part, NEG_FILL)))
        top = jnp.max(functools.reduce(jnp.maximum, [x for _, x in scores]), axis=1, keepdims=True)
        shift = spread(top * (SCALE * LOG2E))
        exps = [jnp.exp2(x * (SCALE * LOG2E) - shift) for _, x in scores]
        total = jnp.sum(functools.reduce(jnp.add, exps), axis=1, keepdims=True)
        for (place, _), e in zip(scores, exps):
            prob_ref[mine, place : place + HD] = e.astype(BF16)
        sum_ref[mine, :] = mm(prob_ref[mine, 0 : b + ROWS], v0[0 : b + ROWS, :], NN) + mm(
            prob_ref[mine, rows + b : 2 * rows], v2[b:rows, :], NN
        )
        top_ref[mine, :] = shift
        total_ref[mine, :] = spread(total)


def near_call(me, lo, q, k0, up, down, v0, v2):
    rows, cols = q.shape
    heads = cols // HD
    tile = pl.BlockSpec((rows, HD), lambda h, me: (0, h))
    return pl.pallas_call(
        near_kernel,
        name="near",
        out_shape=(jax.ShapeDtypeStruct((heads, rows, 2 * rows), BF16),)
        + (jax.ShapeDtypeStruct((rows, cols), F32),) * 3,
        grid_spec=pltpu.PrefetchScalarGridSpec(
            num_scalar_prefetch=1,
            grid=(heads,),
            in_specs=[RESIDENT, tile, tile, RESIDENT, RESIDENT, tile, RESIDENT],
            out_specs=(RESIDENT,) * 4,
            scratch_shapes=[pltpu.VMEM((rows, HD), BF16)],
        ),
        compiler_params=pltpu.CompilerParams(vmem_limit_bytes=VMEM_BYTES),
        cost_estimate=pl.CostEstimate(
            flops=16 * heads * rows * rows * HD, bytes_accessed=10 << 20,
            transcendentals=2 * heads * rows * rows,
        ),
    )(me, *in_vmem(lo), *in_hbm(q, k0), *in_vmem(up, down), *in_hbm(v0), *in_vmem(v2))


def attend_kernel(
    odd_ref, me_ref, lo_ref, q, r1, r2, r3, g, near_top, near_total, near_sum, w_ref,
    att_ref, prob_ref, factor_ref, stat_ref, sent_ref, mine_ref, far_ref, k1, v1,
):
    rows = q.shape[0]
    head = pl.program_id(0)
    cols = head_cols()
    r1, r2, r3, g, near_top, near_total, near_sum, factor_ref = (
        x.at[:, cols] for x in (r1, r2, r3, g, near_top, near_total, near_sum, factor_ref)
    )
    prob_ref, stat_ref = prob_ref.at[head], stat_ref.at[head]
    pick(odd_ref[0], r2, r1, k1)
    pick(odd_ref[0], r3, r2, v1)
    raw = mm(q[...], k1[...], NT)
    for b in range(0, rows, ROWS):
        mine = slice(b, b + ROWS)
        lo = lo_ref[mine, :]
        scores = []
        for c in range(0, rows, ROWS):
            lane = lax.broadcasted_iota(jnp.int32, (ROWS, HD), 1)
            scores.append(jnp.where(lane + (c - rows) >= lo, raw[mine, c : c + HD], NEG_FILL))
        top = jnp.max(functools.reduce(jnp.maximum, scores), axis=1, keepdims=True)
        shift = jnp.maximum(spread(top * (SCALE * LOG2E)), near_top[mine, :])
        exps = [jnp.exp2(s * (SCALE * LOG2E) - shift) for s in scores]
        rescale = jnp.exp2(near_top[mine, :] - shift)
        total = rescale * near_total[mine, :] + spread(
            jnp.sum(functools.reduce(jnp.add, exps), axis=1, keepdims=True)
        )
        inverse = 1.0 / total
        factor = rescale * inverse
        for n, e in enumerate(exps):
            prob_ref[mine, n * HD : (n + 1) * HD] = (e * inverse).astype(BF16)
        attended = (near_sum[mine, :] * factor + mm(prob_ref[mine, :], v1[...], NN)).astype(BF16)
        att_ref[mine, cols] = attended
        factor_ref[mine, :] = factor
        delta = jnp.sum(attended.astype(F32) * g[mine, :].astype(F32), axis=1, keepdims=True)
        log_total = shift + jnp.log2(total)
        lane = lax.broadcasted_iota(jnp.int32, (ROWS, ROWS), 1)
        stats = jnp.where(lane == 0, log_total, delta).T
        stat_ref[:, mine] = stats[0:2, :]

    @pl.when(head == pl.num_programs(0) - 1)
    def _():
        cols = att_ref.shape[1]

        def project(group):
            start = pl.multiple_of((me_ref[0] ^ group) * cols, cols)
            return mm(att_ref[...], w_ref[:, pl.ds(start, cols)], NN)

        sent_ref[:, 0:cols] = project(1).astype(BF16)
        sent_ref[:, cols : 2 * cols] = project(3).astype(BF16)
        far_ref[...] = project(2)
        mine_ref[...] = project(0)


def attend_call(odd, me, lo, q, r1, r2, r3, g, near, weight):
    rows, cols = q.shape
    heads = cols // HD
    tile = pl.BlockSpec((rows, HD), lambda h, odd, me: (0, h))
    return pl.pallas_call(
        attend_kernel,
        name="attend",
        out_shape=(
            jax.ShapeDtypeStruct((rows, cols), BF16),
            jax.ShapeDtypeStruct((heads, rows, rows), BF16),
            jax.ShapeDtypeStruct((rows, cols), F32),
            jax.ShapeDtypeStruct((heads, 2, rows), F32),
            jax.ShapeDtypeStruct((rows, 2 * cols), BF16),
            jax.ShapeDtypeStruct((rows, cols), F32),
            jax.ShapeDtypeStruct((rows, cols), F32),
        ),
        grid_spec=pltpu.PrefetchScalarGridSpec(
            num_scalar_prefetch=2,
            grid=(heads,),
            in_specs=[RESIDENT, tile] + [RESIDENT] * 8,
            out_specs=(RESIDENT,) * 7,
            scratch_shapes=[pltpu.VMEM((rows, HD), BF16)] * 2,
        ),
        compiler_params=pltpu.CompilerParams(vmem_limit_bytes=VMEM_BYTES),
        cost_estimate=pl.CostEstimate(
            flops=8 * heads * rows * rows * HD, bytes_accessed=12 << 20,
            transcendentals=heads * rows * rows,
        ),
    )(odd, me, *in_vmem(lo), *in_hbm(q), *in_vmem(r1, r2, r3, g, *near, weight))


def grads_kernel(
    odd_ref, me_ref, lo_ref, near_ref, prob_ref, factor_ref, att, k0, up, v0, v2, q0, down, r1, r2, r3, g0, g1, g2,
    s0, s10, s11, s20, s21, dq_ref, dk_ref, dv_ref,
    kc, qc, gc, v1, s1, s2, probs, grad_s, grad_q,
):
    rows = g0.shape[0]
    blocks = range(0, rows, ROWS)
    cols = head_cols()
    head = pl.program_id(0)
    factor_ref, att, up, v2, down, r1, r2, r3, g0, g1, g2 = (
        x.at[:, cols] for x in (factor_ref, att, up, v2, down, r1, r2, r3, g0, g1, g2)
    )
    near_ref, prob_ref, s0, s10, s11, s20, s21 = (
        x.at[head] for x in (near_ref, prob_ref, s0, s10, s11, s20, s21)
    )

    @pl.when(pl.program_id(0) == 0)
    def _():
        nothing = jnp.zeros((ROWS, ROWS), BF16)
        for early in blocks:
            for late in range(early + ROWS, rows, ROWS):
                far = 2 * rows
                for into in (probs, grad_s):
                    into[late : late + ROWS, early : early + ROWS] = nothing
                    into[early : early + ROWS, far + late : far + late + ROWS] = nothing
                grad_q[early : early + ROWS, late : late + ROWS] = nothing
                grad_q[late : late + ROWS, rows + early : rows + early + ROWS] = nothing

    odd, group = odd_ref[0], me_ref[0] & 1
    tiles = [slice(t * rows, (t + 1) * rows) for t in range(REACH + 1)]
    pick(odd, r2, r1, kc.at[tiles[2], :])
    pick(odd, r3, r2, v1)
    pick(odd, r1, r3, qc.at[tiles[1], :])
    pick(group, s10, s11, s1)
    pick(group, s20, s21, s2)
    pick(group, up, down, kc.at[tiles[1], :])
    pick(group, down, up, qc.at[tiles[2], :])
    for into, t, ref in (
        (kc, 0, k0), (qc, 0, q0), (gc, 0, g0), (gc, 1, g1), (gc, 2, g2)
    ):
        into[tiles[t], :] = ref[...]
    values, stats = (v0, v1, v2), (s0, s1, s2)

    for t in (0, 2, 1):
        for c in blocks:
            first, last = {0: (0, c + ROWS), 1: (0, rows), 2: (c, rows)}[t]
            at = t * rows + c
            asked = qc[at : at + ROWS, :]
            grad = gc[at : at + ROWS, :]
            raw = mm(k0[first:last, :], asked, NT)
            grad_prob = mm(values[0][first:last, :], grad, NT)
            lo = lo_ref[t : t + 1, c : c + ROWS]
            log_total = stats[t][0:1, c : c + ROWS]
            delta = stats[t][1:2, c : c + ROWS]
            for r in range(first, last, ROWS):
                here = slice(r - first, r - first + ROWS)
                part = raw[here, :]
                pos = r + lax.broadcasted_iota(jnp.int32, part.shape, 0)
                ok = pos >= lo
                if t == 0 and r == c:
                    ok &= pos <= c + lax.broadcasted_iota(jnp.int32, part.shape, 1)
                prob = jnp.where(ok, jnp.exp2(part * (SCALE * LOG2E) - log_total), 0.0)
                probs[r : r + ROWS, at : at + ROWS] = prob.astype(BF16)
                grad_s[r : r + ROWS, at : at + ROWS] = (
                    prob * (grad_prob[here, :] - delta)
                ).astype(BF16)
    dk_ref[...] = (mm(grad_s[...], qc[...], NN) * SCALE).astype(BF16)
    dv_ref[...] = mm(probs[...], gc[...], NN).astype(BF16)

    product = att[...].astype(F32) * g0[...].astype(F32)
    delta = jnp.broadcast_to(jnp.sum(product, axis=1, keepdims=True), (rows, HD))
    for t in (0, 2, 1):
        for c in blocks:
            first, last = {0: (c, rows), 1: (0, rows), 2: (0, c + ROWS)}[t]
            grad_prob = mm(g0[first:last, :], values[t][c : c + ROWS, :], NT)
            into = {0: 0, 2: rows, 1: 2 * rows}[t] + c
            if t == 1:
                prob = prob_ref[first:last, c : c + ROWS].astype(F32)
            else:
                prob = near_ref[first:last, into : into + ROWS].astype(F32)
            grad_q[first:last, into : into + ROWS] = (
                prob * (grad_prob - delta[first:last, :])
            ).astype(BF16)
    near = mm(grad_q[:, 0 : 2 * rows], kc[0 : 2 * rows, :], NN)
    last = mm(grad_q[:, 2 * rows :], kc[2 * rows :, :], NN)
    dq_ref[...] = ((near * factor_ref[...] + last) * SCALE).astype(BF16)


def grads_call(odd, me, lo, near, prob, factor, att, k, v, q, received, grads, stats):
    rows, cols = q[0].shape
    heads = cols // HD
    tile = pl.BlockSpec((rows, HD), lambda h, odd, me: (0, h))
    span = (REACH + 1) * rows
    hbm = in_hbm(k[0], v[0], q[0])
    vmem = in_vmem(k[1], v[1], q[1], *received, *grads)
    return pl.pallas_call(
        grads_kernel,
        name="grads",
        out_shape=(jax.ShapeDtypeStruct((rows, cols), BF16),) * 3,
        grid_spec=pltpu.PrefetchScalarGridSpec(
            num_scalar_prefetch=2,
            grid=(heads,),
            in_specs=[RESIDENT] * 5
            + [tile, RESIDENT, tile, RESIDENT, tile, RESIDENT]
            + [RESIDENT] * 11,
            out_specs=(tile,) * 3,
            scratch_shapes=[pltpu.VMEM((span, HD), BF16)] * 3
            + [pltpu.VMEM((rows, HD), BF16)]
            + [pltpu.VMEM((2, rows), F32)] * 2
            + [pltpu.VMEM((rows, span), BF16)] * 3,
        ),
        compiler_params=pltpu.CompilerParams(vmem_limit_bytes=VMEM_BYTES),
        cost_estimate=pl.CostEstimate(
            flops=12 * heads * rows * span * HD, bytes_accessed=10 << 20,
            transcendentals=heads * rows * span,
        ),
    )(
        odd, me, *in_vmem(lo, near, prob, factor, att),
        hbm[0], vmem[0], hbm[1], vmem[1], hbm[2], vmem[2], *vmem[3:], *in_vmem(*stats),
    )


def layer(queries, key_rows, value_rows, out_weight, cotangent, offsets):
    rows, cols = queries.shape
    count = lax.axis_size("ctx")
    index = lax.axis_index("ctx")
    base = index * rows
    odd = (index % 2).astype(jnp.int32).reshape(1)
    me = lax.axis_index("head").astype(jnp.int32).reshape(1)

    def along(shard, by):
        return passed_along(shard, "ctx", by)

    def across(shard, bit):
        return swapped(shard, "head", bit)

    def exchanged(shard):
        return swapped(shard, "ctx", 1)

    def ringed(shard, by, bit):
        groups = lax.axis_size("head")
        pairs = []
        for i in range(count):
            for h in range(groups):
                to = i - by if (h & 1) == bit else i + by
                here = i * groups + h
                pairs.append((here, to * groups + h if 0 <= to < count else here ^ 1))
        return lax.ppermute(shard, ("ctx", "head"), pairs)

    cot_far = across(cotangent, 2)
    cot_near = across(cotangent, 1)
    up, down = payload_call(
        odd, me, ((0, 1, 0, 1), (1, 0, 1, 0)), *in_hbm(key_rows, queries)
    )
    (side,) = payload_call(odd, me, ((0, 1, 1, 0),), *in_vmem(up, down))
    up = ringed(up, 2, 1)
    down = ringed(down, 2, 0)
    r1 = exchanged(side)
    v2 = along(value_rows, 2)
    cot_both = across(cot_far, 1)
    values = in_hbm(value_rows)
    r2 = exchanged(*payload_call(odd, me, ((0, 0, 1, 2),), *values, *in_vmem(up, down)))

    g = grad_out_call(me, (cotangent, cot_near, cot_far, cot_both), out_weight)
    g2 = along(g, -2)
    bounds = jnp.stack([base, count * rows]).astype(jnp.int32)
    lo_col, lo_row = windows_call(bounds, offsets, rows)
    r3 = exchanged(*payload_call(odd, me, ((1, 0, 2, 2),), *in_vmem(up, down, v2)))
    g1 = exchanged(*payload_call(odd, me, ((0, 0, 1, 1),), *in_vmem(g2, g)))

    near, *near_rows = near_call(
        me, lo_col, queries, key_rows, up, down, value_rows, v2
    )
    attended, prob, factor, stat, sent, kept, kept_far = attend_call(
        odd, me, lo_col, queries, r1, r2, r3, g, near_rows, out_weight
    )
    stats = [stat] + [ringed(stat, n, bit) for n in (1, 2) for bit in (0, 1)]
    came = across(sent, 1)
    far = across((kept_far + came[:, cols:].astype(F32)).astype(BF16), 2)

    grad_queries, grad_keys, grad_values = grads_call(
        odd, me, lo_row, near, prob, factor, attended, (key_rows, up), (value_rows, v2), (queries, down),
        (r1, r2, r3), (g, g1, g2), stats,
    )
    mixed = (kept + came[:, :cols].astype(F32) + far.astype(F32)).astype(BF16)
    return (mixed, grad_queries, grad_keys, grad_values)


def solution(mesh):
    in_specs = (
        P("ctx", "head"),
        P("ctx", "head"),
        P("ctx", "head"),
        P("head", None),
        P("ctx", "head"),
        P(),
    )
    out_specs = (P("ctx", "head"), P("ctx", "head"), P("ctx", "head"), P("ctx", "head"))
    return jax.shard_map(layer, mesh=mesh, in_specs=in_specs, out_specs=out_specs, check_vma=False)
```

```python
import functools
import math

import jax
import jax.numpy as jnp
from jax import lax
from jax.experimental import pallas as pl
from jax.experimental.pallas import tpu as pltpu
from jax.sharding import PartitionSpec as P


HD = 128
REACH = 2
PREV = 3
ROWS = 128
NEG_FILL = -1e30
SCALE = 1.0 / math.sqrt(HD)
LOG2E = 1.4426950408889634
VMEM_BYTES = 32 << 20
F32 = jnp.float32
BF16 = jnp.bfloat16


NT = (((1,), (1,)), ((), ()))
NN = (((1,), (0,)), ((), ()))


def passed_along(shard, axis, by):
    length = lax.axis_size(axis)
    pairs = [(i, i + by) for i in range(length) if 0 <= i + by < length]
    return lax.ppermute(shard, axis, pairs)


def swapped(shard, axis, bit):
    length = lax.axis_size(axis)
    return lax.ppermute(shard, axis, [(i, i ^ bit) for i in range(length)])


RESIDENT = pl.BlockSpec(memory_space=pltpu.VMEM)


def windows_kernel(base_ref, offsets_ref, col_ref, row_ref):
    tiles, rows = row_ref.shape
    lines = tiles * rows // HD
    place = HD * lax.broadcasted_iota(jnp.int32, (lines, HD), 0) + lax.broadcasted_iota(
        jnp.int32, (lines, HD), 1
    )
    position = base_ref[0] + place

    def step(m, first):
        return jnp.where(offsets_ref[m + PREV] <= position, offsets_ref[m], first)

    first = lax.fori_loop(
        0, offsets_ref.shape[0] - PREV, step, jnp.zeros_like(position), unroll=4
    )
    first = jnp.where(position < base_ref[1], first - base_ref[0], tiles * rows)
    for line in range(lines):
        tile, start = divmod(line * HD, rows)
        row_ref[tile : tile + 1, start : start + HD] = first[line : line + 1, :]
        if tile == 0:
            spread = jnp.broadcast_to(first[line : line + 1, :], (HD, HD))
            col_ref[start : start + HD, :] = spread.T


def windows_call(base, offsets, rows):
    return pl.pallas_call(
        windows_kernel,
        name="windows",
        out_shape=(
            jax.ShapeDtypeStruct((rows, HD), jnp.int32),
            jax.ShapeDtypeStruct((REACH + 1, rows), jnp.int32),
        ),
        in_specs=[pl.BlockSpec(memory_space=pltpu.SMEM)] * 2,
        compiler_params=pltpu.CompilerParams(vmem_limit_bytes=VMEM_BYTES),
        cost_estimate=pl.CostEstimate(flops=1 << 20, bytes_accessed=1 << 18, transcendentals=0),
    )(base, offsets)


def in_hbm(*arrays):
    return [pltpu.with_memory_space_constraint(x, pltpu.HBM) for x in arrays]


def in_vmem(*arrays):
    return [pltpu.with_memory_space_constraint(x, pltpu.VMEM) for x in arrays]


def mm(a, b, dims):
    return lax.dot_general(a, b, dims, preferred_element_type=F32)


def payload_kernel(table, kinds, odd_ref, me_ref, *refs):
    sources, outs, sems = refs[:kinds], refs[kinds : kinds + len(table)], refs[-1]
    seat = 2 * odd_ref[0] + (me_ref[0] & 1)
    for n, into in enumerate(outs):
        for kind in range(kinds):
            hits = [seat == place for place in range(4) if table[n][place] == kind]
            if hits:

                @pl.when(functools.reduce(jnp.logical_or, hits))
                def _():
                    pltpu.make_async_copy(sources[kind], into, sems.at[n]).start()

    for n, into in enumerate(outs):
        pltpu.make_async_copy(sources[0], into, sems.at[n]).wait()


def payload_call(odd, me, table, *arrays):
    smem, anywhere = pl.BlockSpec(memory_space=pltpu.SMEM), pl.BlockSpec(memory_space=pl.ANY)
    shape = arrays[0].shape
    return pl.pallas_call(
        functools.partial(payload_kernel, table, len(arrays)),
        name="payload",
        out_shape=(jax.ShapeDtypeStruct(shape, BF16),) * len(table),
        in_specs=[smem, smem] + [anywhere] * len(arrays),
        out_specs=(anywhere,) * len(table),
        scratch_shapes=[pltpu.SemaphoreType.DMA((len(table),))],
        compiler_params=pltpu.CompilerParams(vmem_limit_bytes=1 << 20),
        cost_estimate=pl.CostEstimate(
            flops=0, bytes_accessed=4 * len(table) * shape[0] * shape[1], transcendentals=0
        ),
    )(odd, me, *arrays)


def grad_out_kernel(me_ref, c0, c1, c2, c3, w_ref, out_ref):
    cols = c0.shape[1]
    total = None
    for s, c in enumerate((c0, c1, c2, c3)):
        start = pl.multiple_of((me_ref[0] ^ s) * cols, cols)
        part = mm(c[...], w_ref[:, pl.ds(start, cols)], NT)
        total = part if total is None else total + part
    out_ref[...] = total.astype(BF16)


def grad_out_call(me, shards, weight):
    rows, cols = shards[0].shape
    whole = pl.BlockSpec((rows, cols), lambda h, me: (0, 0))
    return pl.pallas_call(
        grad_out_kernel,
        name="grad_out",
        out_shape=jax.ShapeDtypeStruct((rows, cols), BF16),
        grid_spec=pltpu.PrefetchScalarGridSpec(
            num_scalar_prefetch=1,
            grid=(cols // (2 * HD),),
            in_specs=[whole] + [RESIDENT] * 3
            + [pl.BlockSpec((2 * HD, weight.shape[1]), lambda h, me: (h, 0))],
            out_specs=pl.BlockSpec((rows, 2 * HD), lambda h, me: (0, h)),
        ),
        compiler_params=pltpu.CompilerParams(vmem_limit_bytes=VMEM_BYTES),
        cost_estimate=pl.CostEstimate(
            flops=2 * rows * cols * weight.shape[1], bytes_accessed=6 << 20, transcendentals=0
        ),
    )(me, *in_hbm(shards[0]), *in_vmem(*shards[1:]), *in_hbm(weight))


def pick(odd, even_ref, odd_ref, into):
    into[...] = jnp.where(odd == 0, even_ref[...], odd_ref[...])


def head_cols():
    return pl.ds(pl.multiple_of(pl.program_id(0) * HD, HD), HD)


def spread(column):
    return jnp.broadcast_to(column, (column.shape[0], HD))


def near_kernel(
    odd_ref, me_ref, lo_ref, q, k0, up, down, r1, r2, v0, v2,
    prob_ref, top_ref, total_ref, sum_ref, k1, k2,
):
    rows = q.shape[0]
    blocks = range(0, rows, ROWS)
    cols = head_cols()
    head = pl.program_id(0)
    up, down, r1, r2, v2 = (x.at[:, cols] for x in (up, down, r1, r2, v2))
    top_ref, total_ref, sum_ref = (x.at[:, cols] for x in (top_ref, total_ref, sum_ref))
    prob_ref = prob_ref.at[head]
    pick(me_ref[0] & 1, up, down, k2)
    pick(odd_ref[0], r2, r1, k1)
    own = [mm(q[c:rows, :], k0[c : c + ROWS, :], NT) for c in blocks]
    far = [mm(q[0 : c + ROWS, :], k2[c : c + ROWS, :], NT) for c in blocks]
    last = mm(q[...], k1[...], NT)
    for b in blocks:
        mine = slice(b, b + ROWS)
        lo = lo_ref[mine, :]
        scores = []
        for c in blocks:
            lane = lax.broadcasted_iota(jnp.int32, (ROWS, HD), 1)
            ok = lane + (c - rows) >= lo
            scores.append((2 * rows + c, jnp.where(ok, last[mine, c : c + HD], NEG_FILL)))
            if c <= b:
                ok = lane + c >= lo
                if c == b:
                    ok &= lane <= lax.broadcasted_iota(jnp.int32, (ROWS, HD), 0)
                part = own[c // ROWS][b - c : b - c + ROWS, :]
                scores.append((c, jnp.where(ok, part, NEG_FILL)))
            if c >= b:
                ok = lane + (c - REACH * rows) >= lo
                part = far[c // ROWS][mine, :]
                scores.append((rows + c, jnp.where(ok, part, NEG_FILL)))
        top = jnp.max(functools.reduce(jnp.maximum, [x for _, x in scores]), axis=1, keepdims=True)
        shift = spread(top * (SCALE * LOG2E))
        exps = [jnp.exp2(x * (SCALE * LOG2E) - shift) for _, x in scores]
        total = jnp.sum(functools.reduce(jnp.add, exps), axis=1, keepdims=True)
        for (place, _), e in zip(scores, exps):
            prob_ref[mine, place : place + HD] = e.astype(BF16)
        sum_ref[mine, :] = mm(prob_ref[mine, 0 : b + ROWS], v0[0 : b + ROWS, :], NN) + mm(
            prob_ref[mine, rows + b : 2 * rows], v2[b:rows, :], NN
        )
        top_ref[mine, :] = shift
        total_ref[mine, :] = spread(total)


def near_call(odd, me, lo, q, k0, up, down, r1, r2, v0, v2):
    rows, cols = q.shape
    heads = cols // HD
    tile = pl.BlockSpec((rows, HD), lambda h, odd, me: (0, h))
    return pl.pallas_call(
        near_kernel,
        name="near",
        out_shape=(jax.ShapeDtypeStruct((heads, rows, (REACH + 1) * rows), BF16),)
        + (jax.ShapeDtypeStruct((rows, cols), F32),) * 3,
        grid_spec=pltpu.PrefetchScalarGridSpec(
            num_scalar_prefetch=2,
            grid=(heads,),
            in_specs=[RESIDENT, tile, tile] + [RESIDENT] * 4 + [tile, RESIDENT],
            out_specs=(RESIDENT,) * 4,
            scratch_shapes=[pltpu.VMEM((rows, HD), BF16)] * 2,
        ),
        compiler_params=pltpu.CompilerParams(vmem_limit_bytes=VMEM_BYTES),
        cost_estimate=pl.CostEstimate(
            flops=24 * heads * rows * rows * HD, bytes_accessed=10 << 20,
            transcendentals=3 * heads * rows * rows,
        ),
    )(odd, me, *in_vmem(lo), *in_hbm(q, k0), *in_vmem(up, down, r1, r2), *in_hbm(v0), *in_vmem(v2))


def attend_kernel(
    odd_ref, me_ref, r2, r3, g, prob_ref, top_ref, total_ref, sum_ref, w_ref,
    att_ref, factor_ref, stat_ref, sent_ref, mine_ref, far_ref, v1,
):
    rows = g.shape[0]
    head = pl.program_id(0)
    cols = head_cols()
    r2, r3, g, top_ref, total_ref, sum_ref, factor_ref = (
        x.at[:, cols] for x in (r2, r3, g, top_ref, total_ref, sum_ref, factor_ref)
    )
    prob_ref, stat_ref = prob_ref.at[head], stat_ref.at[head]
    pick(odd_ref[0], r3, r2, v1)
    last = mm(prob_ref[:, 2 * rows :], v1[...], NN)
    for b in range(0, rows, ROWS):
        mine = slice(b, b + ROWS)
        total = total_ref[mine, :]
        factor = 1.0 / total
        attended = ((sum_ref[mine, :] + last[mine, :]) * factor).astype(BF16)
        att_ref[mine, cols] = attended
        factor_ref[mine, :] = factor
        delta = jnp.sum(attended.astype(F32) * g[mine, :].astype(F32), axis=1, keepdims=True)
        log_total = top_ref[mine, :] + jnp.log2(total)
        lane = lax.broadcasted_iota(jnp.int32, (ROWS, ROWS), 1)
        stats = jnp.where(lane == 0, log_total, delta).T
        stat_ref[:, mine] = stats[0:2, :]

    @pl.when(head == pl.num_programs(0) - 1)
    def _():
        cols = att_ref.shape[1]

        def project(group):
            start = pl.multiple_of((me_ref[0] ^ group) * cols, cols)
            return mm(att_ref[...], w_ref[:, pl.ds(start, cols)], NN)

        sent_ref[:, 0:cols] = project(1).astype(BF16)
        sent_ref[:, cols : 2 * cols] = project(3).astype(BF16)
        far_ref[...] = project(2)
        mine_ref[...] = project(0)


def attend_call(odd, me, r2, r3, g, scored, weight):
    rows, cols = g.shape
    heads = cols // HD
    return pl.pallas_call(
        attend_kernel,
        name="attend",
        out_shape=(
            jax.ShapeDtypeStruct((rows, cols), BF16),
            jax.ShapeDtypeStruct((rows, cols), F32),
            jax.ShapeDtypeStruct((heads, 2, rows), F32),
            jax.ShapeDtypeStruct((rows, 2 * cols), BF16),
            jax.ShapeDtypeStruct((rows, cols), F32),
            jax.ShapeDtypeStruct((rows, cols), F32),
        ),
        grid_spec=pltpu.PrefetchScalarGridSpec(
            num_scalar_prefetch=2,
            grid=(heads,),
            in_specs=[RESIDENT] * 8,
            out_specs=(RESIDENT,) * 6,
            scratch_shapes=[pltpu.VMEM((rows, HD), BF16)],
        ),
        compiler_params=pltpu.CompilerParams(vmem_limit_bytes=VMEM_BYTES),
        cost_estimate=pl.CostEstimate(
            flops=8 * heads * rows * rows * HD, bytes_accessed=12 << 20,
            transcendentals=heads * rows * rows,
        ),
    )(odd, me, *in_vmem(r2, r3, g, *scored, weight))


def grads_kernel(
    odd_ref, me_ref, lo_ref, prob_ref, factor_ref, att, k0, up, v0, v2, q0, down, r1, r2, r3, g0, g1, g2,
    s0, s10, s11, s20, s21, dq_ref, dk_ref, dv_ref,
    kc, qc, gc, v1, s1, s2, probs, grad_s, grad_q,
):
    rows = g0.shape[0]
    blocks = range(0, rows, ROWS)
    cols = head_cols()
    head = pl.program_id(0)
    factor_ref, att, up, v2, down, r1, r2, r3, g0, g1, g2 = (
        x.at[:, cols] for x in (factor_ref, att, up, v2, down, r1, r2, r3, g0, g1, g2)
    )
    prob_ref, s0, s10, s11, s20, s21 = (
        x.at[head] for x in (prob_ref, s0, s10, s11, s20, s21)
    )

    @pl.when(pl.program_id(0) == 0)
    def _():
        nothing = jnp.zeros((ROWS, ROWS), BF16)
        for early in blocks:
            for late in range(early + ROWS, rows, ROWS):
                far = 2 * rows
                for into in (probs, grad_s):
                    into[late : late + ROWS, early : early + ROWS] = nothing
                    into[early : early + ROWS, far + late : far + late + ROWS] = nothing
                grad_q[early : early + ROWS, late : late + ROWS] = nothing
                grad_q[late : late + ROWS, rows + early : rows + early + ROWS] = nothing

    odd, group = odd_ref[0], me_ref[0] & 1
    tiles = [slice(t * rows, (t + 1) * rows) for t in range(REACH + 1)]
    pick(odd, r2, r1, kc.at[tiles[2], :])
    pick(odd, r3, r2, v1)
    pick(odd, r1, r3, qc.at[tiles[1], :])
    pick(group, s10, s11, s1)
    pick(group, s20, s21, s2)
    pick(group, up, down, kc.at[tiles[1], :])
    pick(group, down, up, qc.at[tiles[2], :])
    for into, t, ref in (
        (kc, 0, k0), (qc, 0, q0), (gc, 0, g0), (gc, 1, g1), (gc, 2, g2)
    ):
        into[tiles[t], :] = ref[...]
    values, stats = (v0, v1, v2), (s0, s1, s2)

    for t in (0, 2, 1):
        for c in blocks:
            first, last = {0: (0, c + ROWS), 1: (0, rows), 2: (c, rows)}[t]
            at = t * rows + c
            asked = q0[c : c + ROWS, :] if t == 0 else qc[at : at + ROWS, :]
            grad = (g0, g1, g2)[t][c : c + ROWS, :]
            raw = mm(k0[first:last, :], asked, NT)
            grad_prob = mm(values[0][first:last, :], grad, NT)
            lo = lo_ref[t : t + 1, c : c + ROWS]
            log_total = stats[t][0:1, c : c + ROWS]
            delta = stats[t][1:2, c : c + ROWS]
            for r in range(first, last, ROWS):
                here = slice(r - first, r - first + ROWS)
                part = raw[here, :]
                pos = r + lax.broadcasted_iota(jnp.int32, part.shape, 0)
                ok = pos >= lo
                if t == 0 and r == c:
                    ok &= pos <= c + lax.broadcasted_iota(jnp.int32, part.shape, 1)
                prob = jnp.where(ok, jnp.exp2(part * (SCALE * LOG2E) - log_total), 0.0)
                probs[r : r + ROWS, at : at + ROWS] = prob.astype(BF16)
                grad_s[r : r + ROWS, at : at + ROWS] = (
                    prob * (grad_prob[here, :] - delta)
                ).astype(BF16)
    dk_ref[...] = (mm(grad_s[...], qc[...], NN) * SCALE).astype(BF16)
    dv_ref[...] = mm(probs[...], gc[...], NN).astype(BF16)

    product = att[...].astype(F32) * g0[...].astype(F32)
    delta = jnp.broadcast_to(jnp.sum(product, axis=1, keepdims=True), (rows, HD))
    for t in (0, 2, 1):
        for c in blocks:
            first, last = {0: (c, rows), 1: (0, rows), 2: (0, c + ROWS)}[t]
            grad_prob = mm(g0[first:last, :], values[t][c : c + ROWS, :], NT)
            into = {0: 0, 2: rows, 1: 2 * rows}[t] + c
            prob = prob_ref[first:last, into : into + ROWS].astype(F32)
            grad_q[first:last, into : into + ROWS] = (
                prob * (grad_prob - delta[first:last, :])
            ).astype(BF16)
    dq_ref[...] = (mm(grad_q[...], kc[...], NN) * (factor_ref[...] * SCALE)).astype(BF16)


def grads_call(odd, me, lo, prob, factor, att, k, v, q, received, grads, stats):
    rows, cols = q[0].shape
    heads = cols // HD
    tile = pl.BlockSpec((rows, HD), lambda h, odd, me: (0, h))
    span = (REACH + 1) * rows
    hbm = in_hbm(k[0], v[0], q[0])
    vmem = in_vmem(k[1], v[1], q[1], *received, *grads)
    return pl.pallas_call(
        grads_kernel,
        name="grads",
        out_shape=(jax.ShapeDtypeStruct((rows, cols), BF16),) * 3,
        grid_spec=pltpu.PrefetchScalarGridSpec(
            num_scalar_prefetch=2,
            grid=(heads,),
            in_specs=[RESIDENT] * 4
            + [tile, RESIDENT, tile, RESIDENT, tile, RESIDENT]
            + [RESIDENT] * 11,
            out_specs=(tile,) * 3,
            scratch_shapes=[pltpu.VMEM((span, HD), BF16)] * 3
            + [pltpu.VMEM((rows, HD), BF16)]
            + [pltpu.VMEM((2, rows), F32)] * 2
            + [pltpu.VMEM((rows, span), BF16)] * 3,
        ),
        compiler_params=pltpu.CompilerParams(vmem_limit_bytes=VMEM_BYTES),
        cost_estimate=pl.CostEstimate(
            flops=12 * heads * rows * span * HD, bytes_accessed=10 << 20,
            transcendentals=heads * rows * span,
        ),
    )(
        odd, me, *in_vmem(lo, prob, factor, att),
        hbm[0], vmem[0], hbm[1], vmem[1], hbm[2], vmem[2], *vmem[3:], *in_vmem(*stats),
    )


def layer(queries, key_rows, value_rows, out_weight, cotangent, offsets):
    rows, cols = queries.shape
    count = lax.axis_size("ctx")
    index = lax.axis_index("ctx")
    base = index * rows
    odd = (index % 2).astype(jnp.int32).reshape(1)
    me = lax.axis_index("head").astype(jnp.int32).reshape(1)

    def along(shard, by):
        return passed_along(shard, "ctx", by)

    def across(shard, bit):
        return swapped(shard, "head", bit)

    def exchanged(shard):
        return swapped(shard, "ctx", 1)

    def ringed(shard, by, bit):
        groups = lax.axis_size("head")
        pairs = []
        for i in range(count):
            for h in range(groups):
                to = i - by if (h & 1) == bit else i + by
                here = i * groups + h
                pairs.append((here, to * groups + h if 0 <= to < count else here ^ 1))
        return lax.ppermute(shard, ("ctx", "head"), pairs)

    cot_far = across(cotangent, 2)
    cot_near = across(cotangent, 1)
    up, down = payload_call(
        odd, me, ((0, 1, 0, 1), (1, 0, 1, 0)), *in_hbm(key_rows, queries)
    )
    (side,) = payload_call(odd, me, ((0, 1, 1, 0),), *in_vmem(up, down))
    up = ringed(up, 2, 1)
    down = ringed(down, 2, 0)
    r1 = exchanged(side)
    v2 = along(value_rows, 2)
    cot_both = across(cot_far, 1)
    values = in_hbm(value_rows)
    r2 = exchanged(*payload_call(odd, me, ((0, 0, 1, 2),), *values, *in_vmem(up, down)))

    g = grad_out_call(me, (cotangent, cot_near, cot_far, cot_both), out_weight)
    g2 = along(g, -2)
    bounds = jnp.stack([base, count * rows]).astype(jnp.int32)
    lo_col, lo_row = windows_call(bounds, offsets, rows)
    r3 = exchanged(*payload_call(odd, me, ((1, 0, 2, 2),), *in_vmem(up, down, v2)))
    g1 = exchanged(*payload_call(odd, me, ((0, 0, 1, 1),), *in_vmem(g2, g)))

    scored = near_call(
        odd, me, lo_col, queries, key_rows, up, down, r1, r2, value_rows, v2
    )
    attended, factor, stat, sent, kept, kept_far = attend_call(
        odd, me, r2, r3, g, scored, out_weight
    )
    stats = [stat] + [ringed(stat, n, bit) for n in (1, 2) for bit in (0, 1)]
    came = across(sent, 1)
    far = across((kept_far + came[:, cols:].astype(F32)).astype(BF16), 2)

    grad_queries, grad_keys, grad_values = grads_call(
        odd, me, lo_row, scored[0], factor, attended, (key_rows, up), (value_rows, v2), (queries, down),
        (r1, r2, r3), (g, g1, g2), stats,
    )
    mixed = (kept + came[:, :cols].astype(F32) + far.astype(F32)).astype(BF16)
    return (mixed, grad_queries, grad_keys, grad_values)


def solution(mesh):
    in_specs = (
        P("ctx", "head"),
        P("ctx", "head"),
        P("ctx", "head"),
        P("head", None),
        P("ctx", "head"),
        P(),
    )
    out_specs = (P("ctx", "head"), P("ctx", "head"), P("ctx", "head"), P("ctx", "head"))
    return jax.shard_map(layer, mesh=mesh, in_specs=in_specs, out_specs=out_specs, check_vma=False)
```

```python
import functools
import math

import jax
import jax.numpy as jnp
from jax import lax
from jax.experimental import pallas as pl
from jax.experimental.pallas import tpu as pltpu
from jax.sharding import PartitionSpec as P


HD = 128
REACH = 2
PREV = 3
ROWS = 128
NEG_FILL = -1e30
SCALE = 1.0 / math.sqrt(HD)
LOG2E = 1.4426950408889634
VMEM_BYTES = 32 << 20
F32 = jnp.float32
BF16 = jnp.bfloat16


NT = (((1,), (1,)), ((), ()))
NN = (((1,), (0,)), ((), ()))


def passed_along(shard, axis, by):
    length = lax.axis_size(axis)
    pairs = [(i, i + by) for i in range(length) if 0 <= i + by < length]
    return lax.ppermute(shard, axis, pairs)


def swapped(shard, axis, bit):
    length = lax.axis_size(axis)
    return lax.ppermute(shard, axis, [(i, i ^ bit) for i in range(length)])


RESIDENT = pl.BlockSpec(memory_space=pltpu.VMEM)


def windows_kernel(base_ref, offsets_ref, col_ref, row_ref):
    tiles, rows = row_ref.shape
    lines = tiles * rows // HD
    place = HD * lax.broadcasted_iota(jnp.int32, (lines, HD), 0) + lax.broadcasted_iota(
        jnp.int32, (lines, HD), 1
    )
    position = base_ref[0] + place

    def step(m, first):
        return jnp.where(offsets_ref[m + PREV] <= position, offsets_ref[m], first)

    first = lax.fori_loop(
        0, offsets_ref.shape[0] - PREV, step, jnp.zeros_like(position), unroll=4
    )
    first = jnp.where(position < base_ref[1], first - base_ref[0], tiles * rows)
    for line in range(lines):
        tile, start = divmod(line * HD, rows)
        row_ref[tile : tile + 1, start : start + HD] = first[line : line + 1, :]
        if tile == 0:
            spread = jnp.broadcast_to(first[line : line + 1, :], (HD, HD))
            col_ref[start : start + HD, :] = spread.T


def windows_call(base, offsets, rows):
    return pl.pallas_call(
        windows_kernel,
        name="windows",
        out_shape=(
            jax.ShapeDtypeStruct((rows, HD), jnp.int32),
            jax.ShapeDtypeStruct((REACH + 1, rows), jnp.int32),
        ),
        in_specs=[pl.BlockSpec(memory_space=pltpu.SMEM)] * 2,
        compiler_params=pltpu.CompilerParams(vmem_limit_bytes=VMEM_BYTES),
        cost_estimate=pl.CostEstimate(flops=1 << 20, bytes_accessed=1 << 18, transcendentals=0),
    )(base, offsets)


def in_hbm(*arrays):
    return [pltpu.with_memory_space_constraint(x, pltpu.HBM) for x in arrays]


def in_vmem(*arrays):
    return [pltpu.with_memory_space_constraint(x, pltpu.VMEM) for x in arrays]


def mm(a, b, dims):
    return lax.dot_general(a, b, dims, preferred_element_type=F32)


def payload_kernel(table, kinds, odd_ref, me_ref, *refs):
    sources, outs, sems = refs[:kinds], refs[kinds : kinds + len(table)], refs[-1]
    seat = 2 * odd_ref[0] + (me_ref[0] & 1)
    for n, into in enumerate(outs):
        for kind in range(kinds):
            hits = [seat == place for place in range(4) if table[n][place] == kind]
            if hits:

                @pl.when(functools.reduce(jnp.logical_or, hits))
                def _():
                    pltpu.make_async_copy(sources[kind], into, sems.at[n]).start()

    for n, into in enumerate(outs):
        pltpu.make_async_copy(sources[0], into, sems.at[n]).wait()


def payload_call(odd, me, table, *arrays):
    smem, anywhere = pl.BlockSpec(memory_space=pltpu.SMEM), pl.BlockSpec(memory_space=pl.ANY)
    shape = arrays[0].shape
    return pl.pallas_call(
        functools.partial(payload_kernel, table, len(arrays)),
        name="payload",
        out_shape=(jax.ShapeDtypeStruct(shape, BF16),) * len(table),
        in_specs=[smem, smem] + [anywhere] * len(arrays),
        out_specs=(anywhere,) * len(table),
        scratch_shapes=[pltpu.SemaphoreType.DMA((len(table),))],
        compiler_params=pltpu.CompilerParams(vmem_limit_bytes=1 << 20),
        cost_estimate=pl.CostEstimate(
            flops=0, bytes_accessed=4 * len(table) * shape[0] * shape[1], transcendentals=0
        ),
    )(odd, me, *arrays)


def grad_out_kernel(groups, me_ref, w_ref, *refs):
    shards, base, out_ref = refs[: len(groups)], refs[len(groups) : -1], refs[-1]
    cols = shards[0].shape[1]
    width = 2 * HD
    step = pl.ds(pl.multiple_of(pl.program_id(0) * width, width), width)
    total = base[0][:, step] if base else None
    for group, shard in zip(groups, shards):
        start = pl.multiple_of((me_ref[0] ^ group) * cols, cols)
        part = mm(shard[...], w_ref[step, pl.ds(start, cols)], NT)
        total = part if total is None else total + part
    out_ref[:, step] = total.astype(out_ref.dtype)


def grad_out_call(me, weight, groups, shards, base, dtype):
    rows, cols = shards[0].shape
    operands = in_vmem(weight, *shards, *base)
    return pl.pallas_call(
        functools.partial(grad_out_kernel, groups),
        out_shape=jax.ShapeDtypeStruct((rows, cols), dtype),
        grid_spec=pltpu.PrefetchScalarGridSpec(
            num_scalar_prefetch=1,
            grid=(cols // (2 * HD),),
            in_specs=[RESIDENT] * len(operands),
            out_specs=RESIDENT,
        ),
        compiler_params=pltpu.CompilerParams(vmem_limit_bytes=VMEM_BYTES),
        cost_estimate=pl.CostEstimate(
            flops=2 * len(groups) * rows * cols * cols, bytes_accessed=3 << 20, transcendentals=0
        ),
    )(me, *operands)


def pick(odd, even_ref, odd_ref, into):
    into[...] = jnp.where(odd == 0, even_ref[...], odd_ref[...])


def head_cols():
    return pl.ds(pl.multiple_of(pl.program_id(0) * HD, HD), HD)


def spread(column):
    return jnp.broadcast_to(column, (column.shape[0], HD))


def near_kernel(
    odd_ref, me_ref, lo_ref, q, k0, up, down, r1, r2, v0, v2,
    prob_ref, top_ref, total_ref, sum_ref, k1, k2,
):
    rows = q.shape[0]
    blocks = range(0, rows, ROWS)
    cols = head_cols()
    head = pl.program_id(0)
    up, down, r1, r2, v2 = (x.at[:, cols] for x in (up, down, r1, r2, v2))
    top_ref, total_ref, sum_ref = (x.at[:, cols] for x in (top_ref, total_ref, sum_ref))
    prob_ref = prob_ref.at[head]
    pick(me_ref[0] & 1, up, down, k2)
    pick(odd_ref[0], r2, r1, k1)
    own = [mm(q[c:rows, :], k0[c : c + ROWS, :], NT) for c in blocks]
    far = [mm(q[0 : c + ROWS, :], k2[c : c + ROWS, :], NT) for c in blocks]
    last = mm(q[...], k1[...], NT)
    for b in blocks:
        mine = slice(b, b + ROWS)
        lo = lo_ref[mine, :]
        scores = []
        for c in blocks:
            lane = lax.broadcasted_iota(jnp.int32, (ROWS, HD), 1)
            ok = lane + (c - rows) >= lo
            scores.append((2 * rows + c, jnp.where(ok, last[mine, c : c + HD], NEG_FILL)))
            if c <= b:
                ok = lane + c >= lo
                if c == b:
                    ok &= lane <= lax.broadcasted_iota(jnp.int32, (ROWS, HD), 0)
                part = own[c // ROWS][b - c : b - c + ROWS, :]
                scores.append((c, jnp.where(ok, part, NEG_FILL)))
            if c >= b:
                ok = lane + (c - REACH * rows) >= lo
                part = far[c // ROWS][mine, :]
                scores.append((rows + c, jnp.where(ok, part, NEG_FILL)))
        top = jnp.max(functools.reduce(jnp.maximum, [x for _, x in scores]), axis=1, keepdims=True)
        shift = spread(top * (SCALE * LOG2E))
        exps = [jnp.exp2(x * (SCALE * LOG2E) - shift) for _, x in scores]
        total = jnp.sum(functools.reduce(jnp.add, exps), axis=1, keepdims=True)
        for (place, _), e in zip(scores, exps):
            prob_ref[mine, place : place + HD] = e.astype(BF16)
        sum_ref[mine, :] = mm(prob_ref[mine, 0 : b + ROWS], v0[0 : b + ROWS, :], NN) + mm(
            prob_ref[mine, rows + b : 2 * rows], v2[b:rows, :], NN
        )
        top_ref[mine, :] = shift
        total_ref[mine, :] = spread(total)


def near_call(odd, me, lo, q, k0, up, down, r1, r2, v0, v2):
    rows, cols = q.shape
    heads = cols // HD
    tile = pl.BlockSpec((rows, HD), lambda h, odd, me: (0, h))
    return pl.pallas_call(
        near_kernel,
        name="near",
        out_shape=(jax.ShapeDtypeStruct((heads, rows, (REACH + 1) * rows), BF16),)
        + (jax.ShapeDtypeStruct((rows, cols), F32),) * 3,
        grid_spec=pltpu.PrefetchScalarGridSpec(
            num_scalar_prefetch=2,
            grid=(heads,),
            in_specs=[RESIDENT, tile, tile] + [RESIDENT] * 4 + [tile, RESIDENT],
            out_specs=(RESIDENT,) * 4,
            scratch_shapes=[pltpu.VMEM((rows, HD), BF16)] * 2,
        ),
        compiler_params=pltpu.CompilerParams(vmem_limit_bytes=VMEM_BYTES),
        cost_estimate=pl.CostEstimate(
            flops=24 * heads * rows * rows * HD, bytes_accessed=10 << 20,
            transcendentals=3 * heads * rows * rows,
        ),
    )(odd, me, *in_vmem(lo), *in_hbm(q, k0), *in_vmem(up, down, r1, r2), *in_hbm(v0), *in_vmem(v2))


def attend_kernel(
    odd_ref, me_ref, r2, r3, g, prob_ref, top_ref, total_ref, sum_ref, w_ref,
    att_ref, factor_ref, stat_ref, sent_ref, mine_ref, far_ref, v1,
):
    rows = g.shape[0]
    head = pl.program_id(0)
    cols = head_cols()
    r2, r3, g, top_ref, total_ref, sum_ref, factor_ref = (
        x.at[:, cols] for x in (r2, r3, g, top_ref, total_ref, sum_ref, factor_ref)
    )
    prob_ref, stat_ref = prob_ref.at[head], stat_ref.at[head]
    pick(odd_ref[0], r3, r2, v1)
    last = mm(prob_ref[:, 2 * rows :], v1[...], NN)
    for b in range(0, rows, ROWS):
        mine = slice(b, b + ROWS)
        total = total_ref[mine, :]
        factor = 1.0 / total
        attended = ((sum_ref[mine, :] + last[mine, :]) * factor).astype(BF16)
        att_ref[mine, cols] = attended
        factor_ref[mine, :] = factor
        delta = jnp.sum(attended.astype(F32) * g[mine, :].astype(F32), axis=1, keepdims=True)
        log_total = top_ref[mine, :] + jnp.log2(total)
        lane = lax.broadcasted_iota(jnp.int32, (ROWS, ROWS), 1)
        stats = jnp.where(lane == 0, log_total, delta).T
        stat_ref[:, mine] = stats[0:2, :]

    @pl.when(head == pl.num_programs(0) - 1)
    def _():
        cols = att_ref.shape[1]

        def project(group):
            start = pl.multiple_of((me_ref[0] ^ group) * cols, cols)
            return mm(att_ref[...], w_ref[:, pl.ds(start, cols)], NN)

        sent_ref[:, 0:cols] = project(1).astype(BF16)
        sent_ref[:, cols : 2 * cols] = project(3).astype(BF16)
        far_ref[...] = project(2)
        mine_ref[...] = project(0)


def attend_call(odd, me, r2, r3, g, scored, weight):
    rows, cols = g.shape
    heads = cols // HD
    return pl.pallas_call(
        attend_kernel,
        name="attend",
        out_shape=(
            jax.ShapeDtypeStruct((rows, cols), BF16),
            jax.ShapeDtypeStruct((rows, cols), F32),
            jax.ShapeDtypeStruct((heads, 2, rows), F32),
            jax.ShapeDtypeStruct((rows, 2 * cols), BF16),
            jax.ShapeDtypeStruct((rows, cols), F32),
            jax.ShapeDtypeStruct((rows, cols), F32),
        ),
        grid_spec=pltpu.PrefetchScalarGridSpec(
            num_scalar_prefetch=2,
            grid=(heads,),
            in_specs=[RESIDENT] * 8,
            out_specs=(RESIDENT,) * 6,
            scratch_shapes=[pltpu.VMEM((rows, HD), BF16)],
        ),
        compiler_params=pltpu.CompilerParams(vmem_limit_bytes=VMEM_BYTES),
        cost_estimate=pl.CostEstimate(
            flops=8 * heads * rows * rows * HD, bytes_accessed=12 << 20,
            transcendentals=heads * rows * rows,
        ),
    )(odd, me, *in_vmem(r2, r3, g, *scored, weight))


def weigh(raw, grad_prob, first, c, same, lo, stat, probs, grad_s, at):
    log_total, delta = stat[0:1, c : c + ROWS], stat[1:2, c : c + ROWS]
    for r in range(first, first + raw.shape[0], ROWS):
        here = slice(r - first, r - first + ROWS)
        part = raw[here, :]
        pos = r + lax.broadcasted_iota(jnp.int32, part.shape, 0)
        ok = pos >= lo
        if same and r == c:
            ok &= pos <= c + lax.broadcasted_iota(jnp.int32, part.shape, 1)
        prob = jnp.where(ok, jnp.exp2(part * (SCALE * LOG2E) - log_total), 0.0)
        probs[r : r + ROWS, at : at + ROWS] = prob.astype(BF16)
        grad_s[r : r + ROWS, at : at + ROWS] = (prob * (grad_prob[here, :] - delta)).astype(BF16)


def grads_own_kernel(
    odd_ref, me_ref, lo_ref, prob_ref, factor_ref, att, stat, up, down, v2, r1, r2, r3, g0,
    k0, v0, q0, dq_ref, dk_ref, dv_ref, kc, v1, probs, grad_s, grad_q,
):
    rows = g0.shape[0]
    blocks = range(0, rows, ROWS)
    cols = head_cols()
    head = pl.program_id(0)
    factor_ref, att, up, down, v2, r1, r2, r3, g0, dk_ref, dv_ref = (
        x.at[:, cols] for x in (factor_ref, att, up, down, v2, r1, r2, r3, g0, dk_ref, dv_ref)
    )
    prob_ref, stat = prob_ref.at[head], stat.at[head]

    @pl.when(head == 0)
    def _():
        nothing = jnp.zeros((ROWS, ROWS), BF16)
        for early in blocks:
            for late in range(early + ROWS, rows, ROWS):
                for into in (probs, grad_s):
                    into[late : late + ROWS, early : early + ROWS] = nothing
                grad_q[early : early + ROWS, late : late + ROWS] = nothing
                grad_q[late : late + ROWS, rows + early : rows + early + ROWS] = nothing

    kc[0:rows, :] = k0[...]
    pick(me_ref[0] & 1, up, down, kc.at[rows : 2 * rows, :])
    pick(odd_ref[0], r2, r1, kc.at[2 * rows : 3 * rows, :])
    pick(odd_ref[0], r3, r2, v1)

    product = att[...].astype(F32) * g0[...].astype(F32)
    delta = spread(jnp.sum(product, axis=1, keepdims=True))
    for t, values in ((0, v0), (2, v2), (1, v1)):
        for c in blocks:
            first, last = {0: (c, rows), 1: (0, rows), 2: (0, c + ROWS)}[t]
            grad_prob = mm(g0[first:last, :], values[c : c + ROWS, :], NT)
            into = {0: 0, 2: rows, 1: 2 * rows}[t] + c
            prob = prob_ref[first:last, into : into + ROWS].astype(F32)
            grad_q[first:last, into : into + ROWS] = (
                prob * (grad_prob - delta[first:last, :])
            ).astype(BF16)

    for c in blocks:
        raw = mm(k0[0 : c + ROWS, :], q0[c : c + ROWS, :], NT)
        grad_prob = mm(v0[0 : c + ROWS, :], g0[c : c + ROWS, :], NT)
        weigh(raw, grad_prob, 0, c, True, lo_ref[0:1, c : c + ROWS], stat, probs, grad_s, c)
    dq_ref[...] = (mm(grad_q[...], kc[...], NN) * (factor_ref[...] * SCALE)).astype(BF16)
    dk_ref[...] = mm(grad_s[...], q0[...], NN)
    dv_ref[...] = mm(probs[...], g0[...], NN)


def grads_own_call(odd, me, lo, prob, factor, att, stat, up, down, v2, received, g, k, v, q):
    rows, cols = q.shape
    heads = cols // HD
    tile = pl.BlockSpec((rows, HD), lambda h, odd, me: (0, h))
    span = (REACH + 1) * rows
    vmem = in_vmem(lo, prob, factor, att, stat, up, down, v2, *received, g)
    return pl.pallas_call(
        grads_own_kernel,
        name="grads_own",
        out_shape=(jax.ShapeDtypeStruct((rows, cols), BF16),)
        + (jax.ShapeDtypeStruct((rows, cols), F32),) * 2,
        grid_spec=pltpu.PrefetchScalarGridSpec(
            num_scalar_prefetch=2,
            grid=(heads,),
            in_specs=[RESIDENT] * len(vmem) + [tile] * 3,
            out_specs=(tile, RESIDENT, RESIDENT),
            scratch_shapes=[
                pltpu.VMEM((span, HD), BF16), pltpu.VMEM((rows, HD), BF16),
                pltpu.VMEM((rows, rows), BF16), pltpu.VMEM((rows, rows), BF16),
                pltpu.VMEM((rows, span), BF16),
            ],
        ),
        compiler_params=pltpu.CompilerParams(vmem_limit_bytes=VMEM_BYTES),
        cost_estimate=pl.CostEstimate(
            flops=8 * heads * rows * span * HD, bytes_accessed=10 << 20,
            transcendentals=heads * rows * rows,
        ),
    )(odd, me, *vmem, *in_hbm(k, v, q))


def grads_far_kernel(
    odd_ref, me_ref, lo_ref, up, down, r1, r3, g1, g2, s10, s11, s20, s21, dk0, dv0,
    k0, v0, dk_ref, dv_ref, qc, gc, s1, s2, probs, grad_s,
):
    rows = k0.shape[0]
    blocks = range(0, rows, ROWS)
    cols = head_cols()
    head = pl.program_id(0)
    up, down, r1, r3, g1, g2, dk0, dv0 = (
        x.at[:, cols] for x in (up, down, r1, r3, g1, g2, dk0, dv0)
    )
    s10, s11, s20, s21 = (x.at[head] for x in (s10, s11, s20, s21))

    @pl.when(head == 0)
    def _():
        nothing = jnp.zeros((ROWS, ROWS), BF16)
        for early in blocks:
            for late in range(early + ROWS, rows, ROWS):
                for into in (probs, grad_s):
                    into[early : early + ROWS, rows + late : rows + late + ROWS] = nothing

    group = me_ref[0] & 1
    pick(group, s20, s21, s2)
    pick(group, down, up, qc.at[rows : 2 * rows, :])
    gc[rows : 2 * rows, :] = g2[...]
    pick(group, s10, s11, s1)
    pick(odd_ref[0], r1, r3, qc.at[0:rows, :])
    gc[0:rows, :] = g1[...]
    for t, stat in ((2, s2), (1, s1)):
        for c in blocks:
            first = c if t == 2 else 0
            at = (t - 1) * rows + c
            raw = mm(k0[first:rows, :], qc[at : at + ROWS, :], NT)
            grad_prob = mm(v0[first:rows, :], gc[at : at + ROWS, :], NT)
            lo = lo_ref[t : t + 1, c : c + ROWS]
            weigh(raw, grad_prob, first, c, False, lo, stat, probs, grad_s, at)
    dk_ref[...] = ((dk0[...] + mm(grad_s[...], qc[...], NN)) * SCALE).astype(BF16)
    dv_ref[...] = (dv0[...] + mm(probs[...], gc[...], NN)).astype(BF16)


def grads_far_call(odd, me, lo, up, down, r1, r3, g1, g2, stats, dk0, dv0, k, v):
    rows, cols = k.shape
    heads = cols // HD
    tile = pl.BlockSpec((rows, HD), lambda h, odd, me: (0, h))
    span = REACH * rows
    vmem = in_vmem(lo, up, down, r1, r3, g1, g2, *stats, dk0, dv0)
    return pl.pallas_call(
        grads_far_kernel,
        name="grads_far",
        out_shape=(jax.ShapeDtypeStruct((rows, cols), BF16),) * 2,
        grid_spec=pltpu.PrefetchScalarGridSpec(
            num_scalar_prefetch=2,
            grid=(heads,),
            in_specs=[RESIDENT] * len(vmem) + [tile] * 2,
            out_specs=(tile, tile),
            scratch_shapes=[pltpu.VMEM((span, HD), BF16)] * 2
            + [pltpu.VMEM((2, rows), F32)] * 2
            + [pltpu.VMEM((rows, span), BF16)] * 2,
        ),
        compiler_params=pltpu.CompilerParams(vmem_limit_bytes=VMEM_BYTES),
        cost_estimate=pl.CostEstimate(
            flops=8 * heads * rows * span * HD, bytes_accessed=8 << 20,
            transcendentals=heads * rows * span,
        ),
    )(odd, me, *vmem, *in_hbm(k, v))


def layer(queries, key_rows, value_rows, out_weight, cotangent, offsets):
    rows, cols = queries.shape
    count = lax.axis_size("ctx")
    index = lax.axis_index("ctx")
    base = index * rows
    odd = (index % 2).astype(jnp.int32).reshape(1)
    me = lax.axis_index("head").astype(jnp.int32).reshape(1)

    def along(shard, by):
        return passed_along(shard, "ctx", by)

    def across(shard, bit):
        return swapped(shard, "head", bit)

    def exchanged(shard):
        return swapped(shard, "ctx", 1)

    def ringed(shard, by, bit):
        groups = lax.axis_size("head")
        pairs = []
        for i in range(count):
            for h in range(groups):
                to = i - by if (h & 1) == bit else i + by
                here = i * groups + h
                pairs.append((here, to * groups + h if 0 <= to < count else here ^ 1))
        return lax.ppermute(shard, ("ctx", "head"), pairs)

    cot_far = across(cotangent, 2)
    cot_near = across(cotangent, 1)
    up, down = payload_call(
        odd, me, ((0, 1, 0, 1), (1, 0, 1, 0)), *in_hbm(key_rows, queries)
    )
    (side,) = payload_call(odd, me, ((0, 1, 1, 0),), *in_vmem(up, down))
    up = ringed(up, 2, 1)
    down = ringed(down, 2, 0)
    r1 = exchanged(side)
    v2 = along(value_rows, 2)
    g_near = grad_out_call(me, out_weight, (0, 1), (cotangent, cot_near), (), F32)
    cot_both = across(cot_far, 1)
    values = in_hbm(value_rows)
    r2 = exchanged(*payload_call(odd, me, ((0, 0, 1, 2),), *values, *in_vmem(up, down)))

    g = grad_out_call(me, out_weight, (2, 3), (cot_far, cot_both), (g_near,), BF16)
    g2 = along(g, -2)
    bounds = jnp.stack([base, count * rows]).astype(jnp.int32)
    lo_col, lo_row = windows_call(bounds, offsets, rows)
    r3 = exchanged(*payload_call(odd, me, ((1, 0, 2, 2),), *in_vmem(up, down, v2)))
    g1 = exchanged(*payload_call(odd, me, ((0, 0, 1, 1),), *in_vmem(g2, g)))

    scored = near_call(
        odd, me, lo_col, queries, key_rows, up, down, r1, r2, value_rows, v2
    )
    attended, factor, stat, sent, kept, kept_far = attend_call(
        odd, me, r2, r3, g, scored, out_weight
    )
    stats = [ringed(stat, n, bit) for n in (1, 2) for bit in (0, 1)]
    came = across(sent, 1)
    far = across((kept_far + came[:, cols:].astype(F32)).astype(BF16), 2)

    grad_queries, own_keys, own_values = grads_own_call(
        odd, me, lo_row, scored[0], factor, attended, stat, up, down, v2, (r1, r2, r3), g,
        key_rows, value_rows, queries,
    )
    grad_keys, grad_values = grads_far_call(
        odd, me, lo_row, up, down, r1, r3, g1, g2, stats, own_keys, own_values,
        key_rows, value_rows,
    )
    mixed = (kept + came[:, :cols].astype(F32) + far.astype(F32)).astype(BF16)
    return (mixed, grad_queries, grad_keys, grad_values)


def solution(mesh):
    in_specs = (
        P("ctx", "head"),
        P("ctx", "head"),
        P("ctx", "head"),
        P("head", None),
        P("ctx", "head"),
        P(),
    )
    out_specs = (P("ctx", "head"), P("ctx", "head"), P("ctx", "head"), P("ctx", "head"))
    return jax.shard_map(layer, mesh=mesh, in_specs=in_specs, out_specs=out_specs, check_vma=False)
```

```python
import functools
import math

import jax
import jax.numpy as jnp
from jax import lax
from jax.experimental import pallas as pl
from jax.experimental.pallas import tpu as pltpu
from jax.sharding import PartitionSpec as P


HD = 128
REACH = 2
PREV = 3
ROWS = 128
NEG_FILL = -1e30
SCALE = 1.0 / math.sqrt(HD)
LOG2E = 1.4426950408889634
VMEM_BYTES = 32 << 20
F32 = jnp.float32
BF16 = jnp.bfloat16


NT = (((1,), (1,)), ((), ()))
NN = (((1,), (0,)), ((), ()))


def passed_along(shard, axis, by):
    length = lax.axis_size(axis)
    pairs = [(i, i + by) for i in range(length) if 0 <= i + by < length]
    return lax.ppermute(shard, axis, pairs)


def swapped(shard, axis, bit):
    length = lax.axis_size(axis)
    return lax.ppermute(shard, axis, [(i, i ^ bit) for i in range(length)])


RESIDENT = pl.BlockSpec(memory_space=pltpu.VMEM)


def windows_kernel(base_ref, offsets_ref, col_ref, row_ref):
    tiles, rows = row_ref.shape
    lines = tiles * rows // HD
    place = HD * lax.broadcasted_iota(jnp.int32, (lines, HD), 0) + lax.broadcasted_iota(
        jnp.int32, (lines, HD), 1
    )
    position = base_ref[0] + place

    def step(m, first):
        return jnp.where(offsets_ref[m + PREV] <= position, offsets_ref[m], first)

    first = lax.fori_loop(
        0, offsets_ref.shape[0] - PREV, step, jnp.zeros_like(position), unroll=4
    )
    first = jnp.where(position < base_ref[1], first - base_ref[0], tiles * rows)
    for line in range(lines):
        tile, start = divmod(line * HD, rows)
        row_ref[tile : tile + 1, start : start + HD] = first[line : line + 1, :]
        if tile == 0:
            spread = jnp.broadcast_to(first[line : line + 1, :], (HD, HD))
            col_ref[start : start + HD, :] = spread.T


def windows_call(base, offsets, rows):
    return pl.pallas_call(
        windows_kernel,
        name="windows",
        out_shape=(
            jax.ShapeDtypeStruct((rows, HD), jnp.int32),
            jax.ShapeDtypeStruct((REACH + 1, rows), jnp.int32),
        ),
        in_specs=[pl.BlockSpec(memory_space=pltpu.SMEM)] * 2,
        compiler_params=pltpu.CompilerParams(vmem_limit_bytes=VMEM_BYTES),
        cost_estimate=pl.CostEstimate(flops=1 << 20, bytes_accessed=1 << 18, transcendentals=0),
    )(base, offsets)


def in_hbm(*arrays):
    return [pltpu.with_memory_space_constraint(x, pltpu.HBM) for x in arrays]


def in_vmem(*arrays):
    return [pltpu.with_memory_space_constraint(x, pltpu.VMEM) for x in arrays]


def mm(a, b, dims):
    return lax.dot_general(a, b, dims, preferred_element_type=F32)


def payload_kernel(table, kinds, odd_ref, me_ref, *refs):
    sources, outs, sems = refs[:kinds], refs[kinds : kinds + len(table)], refs[-1]
    seat = 2 * odd_ref[0] + (me_ref[0] & 1)
    for n, into in enumerate(outs):
        for kind in range(kinds):
            hits = [seat == place for place in range(4) if table[n][place] == kind]
            if hits:

                @pl.when(functools.reduce(jnp.logical_or, hits))
                def _():
                    pltpu.make_async_copy(sources[kind], into, sems.at[n]).start()

    for n, into in enumerate(outs):
        pltpu.make_async_copy(sources[0], into, sems.at[n]).wait()


def payload_call(odd, me, table, *arrays):
    smem, anywhere = pl.BlockSpec(memory_space=pltpu.SMEM), pl.BlockSpec(memory_space=pl.ANY)
    shape = arrays[0].shape
    return pl.pallas_call(
        functools.partial(payload_kernel, table, len(arrays)),
        name="payload",
        out_shape=(jax.ShapeDtypeStruct(shape, BF16),) * len(table),
        in_specs=[smem, smem] + [anywhere] * len(arrays),
        out_specs=(anywhere,) * len(table),
        scratch_shapes=[pltpu.SemaphoreType.DMA((len(table),))],
        compiler_params=pltpu.CompilerParams(vmem_limit_bytes=1 << 20),
        cost_estimate=pl.CostEstimate(
            flops=0, bytes_accessed=4 * len(table) * shape[0] * shape[1], transcendentals=0
        ),
    )(odd, me, *arrays)


def grad_out_kernel(groups, me_ref, w_ref, *refs):
    shards, base, out_ref = refs[: len(groups)], refs[len(groups) : -1], refs[-1]
    cols = shards[0].shape[1]
    width = 2 * HD
    step = pl.ds(pl.multiple_of(pl.program_id(0) * width, width), width)
    total = base[0][:, step] if base else None
    for group, shard in zip(groups, shards):
        start = pl.multiple_of((me_ref[0] ^ group) * cols, cols)
        part = mm(shard[...], w_ref[step, pl.ds(start, cols)], NT)
        total = part if total is None else total + part
    out_ref[:, step] = total.astype(out_ref.dtype)


def grad_out_call(me, weight, groups, shards, base, dtype):
    rows, cols = shards[0].shape
    operands = in_vmem(weight, *shards, *base)
    return pl.pallas_call(
        functools.partial(grad_out_kernel, groups),
        out_shape=jax.ShapeDtypeStruct((rows, cols), dtype),
        grid_spec=pltpu.PrefetchScalarGridSpec(
            num_scalar_prefetch=1,
            grid=(cols // (2 * HD),),
            in_specs=[RESIDENT] * len(operands),
            out_specs=RESIDENT,
        ),
        compiler_params=pltpu.CompilerParams(vmem_limit_bytes=VMEM_BYTES),
        cost_estimate=pl.CostEstimate(
            flops=2 * len(groups) * rows * cols * cols, bytes_accessed=3 << 20, transcendentals=0
        ),
    )(me, *operands)


def pick(odd, even_ref, odd_ref, into):
    into[...] = jnp.where(odd == 0, even_ref[...], odd_ref[...])


def head_cols():
    return pl.ds(pl.multiple_of(pl.program_id(0) * HD, HD), HD)


def spread(column):
    return jnp.broadcast_to(column, (column.shape[0], HD))


def near_kernel(
    odd_ref, me_ref, lo_ref, q, k0, up, down, r1, r2, v0, v2,
    prob_ref, top_ref, total_ref, sum_ref, k1, k2,
):
    rows = q.shape[0]
    blocks = range(0, rows, ROWS)
    cols = head_cols()
    head = pl.program_id(0)
    up, down, r1, r2, v2 = (x.at[:, cols] for x in (up, down, r1, r2, v2))
    top_ref, total_ref, sum_ref = (x.at[:, cols] for x in (top_ref, total_ref, sum_ref))
    prob_ref = prob_ref.at[head]
    pick(me_ref[0] & 1, up, down, k2)
    pick(odd_ref[0], r2, r1, k1)
    own = [mm(q[c:rows, :], k0[c : c + ROWS, :], NT) for c in blocks]
    far = [mm(q[0 : c + ROWS, :], k2[c : c + ROWS, :], NT) for c in blocks]
    last = mm(q[...], k1[...], NT)
    for b in blocks:
        mine = slice(b, b + ROWS)
        lo = lo_ref[mine, :]
        scores = []
        for c in blocks:
            lane = lax.broadcasted_iota(jnp.int32, (ROWS, HD), 1)
            ok = lane + (c - rows) >= lo
            scores.append((2 * rows + c, jnp.where(ok, last[mine, c : c + HD], NEG_FILL)))
            if c <= b:
                ok = lane + c >= lo
                if c == b:
                    ok &= lane <= lax.broadcasted_iota(jnp.int32, (ROWS, HD), 0)
                part = own[c // ROWS][b - c : b - c + ROWS, :]
                scores.append((c, jnp.where(ok, part, NEG_FILL)))
            if c >= b:
                ok = lane + (c - REACH * rows) >= lo
                part = far[c // ROWS][mine, :]
                scores.append((rows + c, jnp.where(ok, part, NEG_FILL)))
        top = jnp.max(functools.reduce(jnp.maximum, [x for _, x in scores]), axis=1, keepdims=True)
        shift = spread(top * (SCALE * LOG2E))
        exps = [jnp.exp2(x * (SCALE * LOG2E) - shift) for _, x in scores]
        total = jnp.sum(functools.reduce(jnp.add, exps), axis=1, keepdims=True)
        for (place, _), e in zip(scores, exps):
            prob_ref[mine, place : place + HD] = e.astype(BF16)
        sum_ref[mine, :] = mm(prob_ref[mine, 0 : b + ROWS], v0[0 : b + ROWS, :], NN) + mm(
            prob_ref[mine, rows + b : 2 * rows], v2[b:rows, :], NN
        )
        top_ref[mine, :] = shift
        total_ref[mine, :] = spread(total)


def near_call(odd, me, lo, q, k0, up, down, r1, r2, v0, v2):
    rows, cols = q.shape
    heads = cols // HD
    tile = pl.BlockSpec((rows, HD), lambda h, odd, me: (0, h))
    return pl.pallas_call(
        near_kernel,
        name="near",
        out_shape=(jax.ShapeDtypeStruct((heads, rows, (REACH + 1) * rows), BF16),)
        + (jax.ShapeDtypeStruct((rows, cols), F32),) * 3,
        grid_spec=pltpu.PrefetchScalarGridSpec(
            num_scalar_prefetch=2,
            grid=(heads,),
            in_specs=[RESIDENT, tile, tile] + [RESIDENT] * 4 + [tile, RESIDENT],
            out_specs=(RESIDENT,) * 4,
            scratch_shapes=[pltpu.VMEM((rows, HD), BF16)] * 2,
        ),
        compiler_params=pltpu.CompilerParams(vmem_limit_bytes=VMEM_BYTES),
        cost_estimate=pl.CostEstimate(
            flops=24 * heads * rows * rows * HD, bytes_accessed=10 << 20,
            transcendentals=3 * heads * rows * rows,
        ),
    )(odd, me, *in_vmem(lo), *in_hbm(q, k0), *in_vmem(up, down, r1, r2), *in_hbm(v0), *in_vmem(v2))


def attend_kernel(
    odd_ref, me_ref, r2, r3, g, prob_ref, top_ref, total_ref, sum_ref, w_ref,
    att_ref, factor_ref, stat_ref, sent_ref, mine_ref, far_ref, v1,
):
    rows = g.shape[0]
    head = pl.program_id(0)
    cols = head_cols()
    r2, r3, g, top_ref, total_ref, sum_ref, factor_ref = (
        x.at[:, cols] for x in (r2, r3, g, top_ref, total_ref, sum_ref, factor_ref)
    )
    prob_ref, stat_ref = prob_ref.at[head], stat_ref.at[head]
    pick(odd_ref[0], r3, r2, v1)
    last = mm(prob_ref[:, 2 * rows :], v1[...], NN)
    for b in range(0, rows, ROWS):
        mine = slice(b, b + ROWS)
        total = total_ref[mine, :]
        factor = 1.0 / total
        attended = ((sum_ref[mine, :] + last[mine, :]) * factor).astype(BF16)
        att_ref[mine, cols] = attended
        factor_ref[mine, :] = factor
        delta = jnp.sum(attended.astype(F32) * g[mine, :].astype(F32), axis=1, keepdims=True)
        log_total = top_ref[mine, :] + jnp.log2(total)
        lane = lax.broadcasted_iota(jnp.int32, (ROWS, ROWS), 1)
        stats = jnp.where(lane == 0, log_total, delta).T
        stat_ref[:, mine] = stats[0:2, :]

    @pl.when(head == pl.num_programs(0) - 1)
    def _():
        cols = att_ref.shape[1]

        def project(group):
            start = pl.multiple_of((me_ref[0] ^ group) * cols, cols)
            return mm(att_ref[...], w_ref[:, pl.ds(start, cols)], NN)

        sent_ref[:, 0:cols] = project(1).astype(BF16)
        sent_ref[:, cols : 2 * cols] = project(3).astype(BF16)
        far_ref[...] = project(2)
        mine_ref[...] = project(0)


def attend_call(odd, me, r2, r3, g, scored, weight):
    rows, cols = g.shape
    heads = cols // HD
    return pl.pallas_call(
        attend_kernel,
        name="attend",
        out_shape=(
            jax.ShapeDtypeStruct((rows, cols), BF16),
            jax.ShapeDtypeStruct((rows, cols), F32),
            jax.ShapeDtypeStruct((heads, 2, rows), F32),
            jax.ShapeDtypeStruct((rows, 2 * cols), BF16),
            jax.ShapeDtypeStruct((rows, cols), F32),
            jax.ShapeDtypeStruct((rows, cols), F32),
        ),
        grid_spec=pltpu.PrefetchScalarGridSpec(
            num_scalar_prefetch=2,
            grid=(heads,),
            in_specs=[RESIDENT] * 8,
            out_specs=(RESIDENT,) * 6,
            scratch_shapes=[pltpu.VMEM((rows, HD), BF16)],
        ),
        compiler_params=pltpu.CompilerParams(vmem_limit_bytes=VMEM_BYTES),
        cost_estimate=pl.CostEstimate(
            flops=8 * heads * rows * rows * HD, bytes_accessed=12 << 20,
            transcendentals=heads * rows * rows,
        ),
    )(odd, me, *in_vmem(r2, r3, g, *scored, weight))


def grads_kernel(
    odd_ref, me_ref, lo_ref, prob_ref, factor_ref, att, k0, up, v0, v2, q0, down, r1, r2, r3, g0, g1, g2,
    s0, s10, s11, s20, s21, dq_ref, dk_ref, dv_ref,
    kc, qc, gc, v1, s1, s2, probs, grad_s, grad_q,
):
    rows = g0.shape[0]
    blocks = range(0, rows, ROWS)
    cols = head_cols()
    head = pl.program_id(0)
    factor_ref, att, up, v2, down, r1, r2, r3, g0, g1, g2 = (
        x.at[:, cols] for x in (factor_ref, att, up, v2, down, r1, r2, r3, g0, g1, g2)
    )
    prob_ref, s0, s10, s11, s20, s21 = (
        x.at[head] for x in (prob_ref, s0, s10, s11, s20, s21)
    )

    @pl.when(pl.program_id(0) == 0)
    def _():
        nothing = jnp.zeros((ROWS, ROWS), BF16)
        for early in blocks:
            for late in range(early + ROWS, rows, ROWS):
                far = 2 * rows
                for into in (probs, grad_s):
                    into[late : late + ROWS, early : early + ROWS] = nothing
                    into[early : early + ROWS, far + late : far + late + ROWS] = nothing
                grad_q[early : early + ROWS, late : late + ROWS] = nothing
                grad_q[late : late + ROWS, rows + early : rows + early + ROWS] = nothing

    odd, group = odd_ref[0], me_ref[0] & 1
    tiles = [slice(t * rows, (t + 1) * rows) for t in range(REACH + 1)]
    pick(odd, r2, r1, kc.at[tiles[2], :])
    pick(odd, r3, r2, v1)
    pick(odd, r1, r3, qc.at[tiles[1], :])
    pick(group, s10, s11, s1)
    pick(group, s20, s21, s2)
    pick(group, up, down, kc.at[tiles[1], :])
    pick(group, down, up, qc.at[tiles[2], :])
    for into, t, ref in (
        (kc, 0, k0), (qc, 0, q0), (gc, 0, g0), (gc, 1, g1), (gc, 2, g2)
    ):
        into[tiles[t], :] = ref[...]
    values, stats = (v0, v1, v2), (s0, s1, s2)

    product = att[...].astype(F32) * g0[...].astype(F32)
    delta = jnp.broadcast_to(jnp.sum(product, axis=1, keepdims=True), (rows, HD))
    for t in (0, 2, 1):
        for c in blocks:
            first, last = {0: (c, rows), 1: (0, rows), 2: (0, c + ROWS)}[t]
            grad_prob = mm(g0[first:last, :], values[t][c : c + ROWS, :], NT)
            into = {0: 0, 2: rows, 1: 2 * rows}[t] + c
            prob = prob_ref[first:last, into : into + ROWS].astype(F32)
            grad_q[first:last, into : into + ROWS] = (
                prob * (grad_prob - delta[first:last, :])
            ).astype(BF16)
    for t in (0,):
        for c in blocks:
            first, last = {0: (0, c + ROWS), 1: (0, rows), 2: (c, rows)}[t]
            at = t * rows + c
            asked = q0[c : c + ROWS, :] if t == 0 else qc[at : at + ROWS, :]
            grad = (g0, g1, g2)[t][c : c + ROWS, :]
            raw = mm(k0[first:last, :], asked, NT)
            grad_prob = mm(values[0][first:last, :], grad, NT)
            lo = lo_ref[t : t + 1, c : c + ROWS]
            log_total = stats[t][0:1, c : c + ROWS]
            delta = stats[t][1:2, c : c + ROWS]
            for r in range(first, last, ROWS):
                here = slice(r - first, r - first + ROWS)
                part = raw[here, :]
                pos = r + lax.broadcasted_iota(jnp.int32, part.shape, 0)
                ok = pos >= lo
                if t == 0 and r == c:
                    ok &= pos <= c + lax.broadcasted_iota(jnp.int32, part.shape, 1)
                prob = jnp.where(ok, jnp.exp2(part * (SCALE * LOG2E) - log_total), 0.0)
                probs[r : r + ROWS, at : at + ROWS] = prob.astype(BF16)
                grad_s[r : r + ROWS, at : at + ROWS] = (
                    prob * (grad_prob[here, :] - delta)
                ).astype(BF16)
    dq_ref[...] = (mm(grad_q[...], kc[...], NN) * (factor_ref[...] * SCALE)).astype(BF16)
    for t in (2,):
        for c in blocks:
            first, last = {0: (0, c + ROWS), 1: (0, rows), 2: (c, rows)}[t]
            at = t * rows + c
            asked = q0[c : c + ROWS, :] if t == 0 else qc[at : at + ROWS, :]
            grad = (g0, g1, g2)[t][c : c + ROWS, :]
            raw = mm(k0[first:last, :], asked, NT)
            grad_prob = mm(values[0][first:last, :], grad, NT)
            lo = lo_ref[t : t + 1, c : c + ROWS]
            log_total = stats[t][0:1, c : c + ROWS]
            delta = stats[t][1:2, c : c + ROWS]
            for r in range(first, last, ROWS):
                here = slice(r - first, r - first + ROWS)
                part = raw[here, :]
                pos = r + lax.broadcasted_iota(jnp.int32, part.shape, 0)
                ok = pos >= lo
                if t == 0 and r == c:
                    ok &= pos <= c + lax.broadcasted_iota(jnp.int32, part.shape, 1)
                prob = jnp.where(ok, jnp.exp2(part * (SCALE * LOG2E) - log_total), 0.0)
                probs[r : r + ROWS, at : at + ROWS] = prob.astype(BF16)
                grad_s[r : r + ROWS, at : at + ROWS] = (
                    prob * (grad_prob[here, :] - delta)
                ).astype(BF16)
    for t in (1,):
        for c in blocks:
            first, last = {0: (0, c + ROWS), 1: (0, rows), 2: (c, rows)}[t]
            at = t * rows + c
            asked = q0[c : c + ROWS, :] if t == 0 else qc[at : at + ROWS, :]
            grad = (g0, g1, g2)[t][c : c + ROWS, :]
            raw = mm(k0[first:last, :], asked, NT)
            grad_prob = mm(values[0][first:last, :], grad, NT)
            lo = lo_ref[t : t + 1, c : c + ROWS]
            log_total = stats[t][0:1, c : c + ROWS]
            delta = stats[t][1:2, c : c + ROWS]
            for r in range(first, last, ROWS):
                here = slice(r - first, r - first + ROWS)
                part = raw[here, :]
                pos = r + lax.broadcasted_iota(jnp.int32, part.shape, 0)
                ok = pos >= lo
                if t == 0 and r == c:
                    ok &= pos <= c + lax.broadcasted_iota(jnp.int32, part.shape, 1)
                prob = jnp.where(ok, jnp.exp2(part * (SCALE * LOG2E) - log_total), 0.0)
                probs[r : r + ROWS, at : at + ROWS] = prob.astype(BF16)
                grad_s[r : r + ROWS, at : at + ROWS] = (
                    prob * (grad_prob[here, :] - delta)
                ).astype(BF16)
    dk_ref[...] = (mm(grad_s[...], qc[...], NN) * SCALE).astype(BF16)
    dv_ref[...] = mm(probs[...], gc[...], NN).astype(BF16)


def grads_call(odd, me, lo, prob, factor, att, k, v, q, received, grads, stats):
    rows, cols = q[0].shape
    heads = cols // HD
    tile = pl.BlockSpec((rows, HD), lambda h, odd, me: (0, h))
    span = (REACH + 1) * rows
    hbm = in_hbm(k[0], v[0], q[0])
    vmem = in_vmem(k[1], v[1], q[1], *received, *grads)
    return pl.pallas_call(
        grads_kernel,
        name="grads",
        out_shape=(jax.ShapeDtypeStruct((rows, cols), BF16),) * 3,
        grid_spec=pltpu.PrefetchScalarGridSpec(
            num_scalar_prefetch=2,
            grid=(heads,),
            in_specs=[RESIDENT] * 4
            + [tile, RESIDENT, tile, RESIDENT, tile, RESIDENT]
            + [RESIDENT] * 11,
            out_specs=(tile,) * 3,
            scratch_shapes=[pltpu.VMEM((span, HD), BF16)] * 3
            + [pltpu.VMEM((rows, HD), BF16)]
            + [pltpu.VMEM((2, rows), F32)] * 2
            + [pltpu.VMEM((rows, span), BF16)] * 3,
        ),
        compiler_params=pltpu.CompilerParams(vmem_limit_bytes=VMEM_BYTES),
        cost_estimate=pl.CostEstimate(
            flops=12 * heads * rows * span * HD, bytes_accessed=10 << 20,
            transcendentals=heads * rows * span,
        ),
    )(
        odd, me, *in_vmem(lo, prob, factor, att),
        hbm[0], vmem[0], hbm[1], vmem[1], hbm[2], vmem[2], *vmem[3:], *in_vmem(*stats),
    )


def layer(queries, key_rows, value_rows, out_weight, cotangent, offsets):
    rows, cols = queries.shape
    count = lax.axis_size("ctx")
    index = lax.axis_index("ctx")
    base = index * rows
    odd = (index % 2).astype(jnp.int32).reshape(1)
    me = lax.axis_index("head").astype(jnp.int32).reshape(1)

    def along(shard, by):
        return passed_along(shard, "ctx", by)

    def across(shard, bit):
        return swapped(shard, "head", bit)

    def exchanged(shard):
        return swapped(shard, "ctx", 1)

    def ringed(shard, by, bit):
        groups = lax.axis_size("head")
        pairs = []
        for i in range(count):
            for h in range(groups):
                to = i - by if (h & 1) == bit else i + by
                here = i * groups + h
                pairs.append((here, to * groups + h if 0 <= to < count else here ^ 1))
        return lax.ppermute(shard, ("ctx", "head"), pairs)

    cot_far = across(cotangent, 2)
    cot_near = across(cotangent, 1)
    up, down = payload_call(
        odd, me, ((0, 1, 0, 1), (1, 0, 1, 0)), *in_hbm(key_rows, queries)
    )
    (side,) = payload_call(odd, me, ((0, 1, 1, 0),), *in_vmem(up, down))
    up = ringed(up, 2, 1)
    down = ringed(down, 2, 0)
    r1 = exchanged(side)
    v2 = along(value_rows, 2)
    g_near = grad_out_call(me, out_weight, (0, 1), (cotangent, cot_near), (), F32)
    cot_both = across(cot_far, 1)
    r2 = exchanged(*payload_call(odd, me, ((0, 0, 1, 2),), *in_vmem(value_rows, up, down)))

    g = grad_out_call(me, out_weight, (2, 3), (cot_far, cot_both), (g_near,), BF16)
    g2 = along(g, -2)
    bounds = jnp.stack([base, count * rows]).astype(jnp.int32)
    lo_col, lo_row = windows_call(bounds, offsets, rows)
    r3 = exchanged(*payload_call(odd, me, ((1, 0, 2, 2),), *in_vmem(up, down, v2)))
    g1 = exchanged(*payload_call(odd, me, ((0, 0, 1, 1),), *in_vmem(g2, g)))

    scored = near_call(
        odd, me, lo_col, queries, key_rows, up, down, r1, r2, value_rows, v2
    )
    attended, factor, stat, sent, kept, kept_far = attend_call(
        odd, me, r2, r3, g, scored, out_weight
    )
    stats = [stat] + [ringed(stat, n, bit) for n in (1, 2) for bit in (0, 1)]
    came = across(sent, 1)
    far = across((kept_far + came[:, cols:].astype(F32)).astype(BF16), 2)

    grad_queries, grad_keys, grad_values = grads_call(
        odd, me, lo_row, scored[0], factor, attended, (key_rows, up), (value_rows, v2), (queries, down),
        (r1, r2, r3), (g, g1, g2), stats,
    )
    mixed = (kept + came[:, :cols].astype(F32) + far.astype(F32)).astype(BF16)
    return (mixed, grad_queries, grad_keys, grad_values)


def solution(mesh):
    in_specs = (
        P("ctx", "head"),
        P("ctx", "head"),
        P("ctx", "head"),
        P("head", None),
        P("ctx", "head"),
        P(),
    )
    out_specs = (P("ctx", "head"), P("ctx", "head"), P("ctx", "head"), P("ctx", "head"))
    return jax.shard_map(layer, mesh=mesh, in_specs=in_specs, out_specs=out_specs, check_vma=False)
```
